32 devices in a mesh: lvl: 4 (over z), sp: 8 (over y, x, core).
Axes of the slice: x: 2, y: 2, z: 4, core: 2. Of those that a mesh axis runs over, the one named last changes fastest.
Arguments:
- input_field: bfloat16 [3, 800, 128, 128], P(None, 'lvl', 'sp'), may hold values from -6 to 6
- cotangent: bfloat16 [3, 800, 128, 128], P(None, 'lvl', 'sp'), may hold values from -6 to 6
- ocean_mask: int32 [3, 128, 128], P(None, 'sp'), may hold values 0 or 1
- crop_rows: int32 [3, 8], P(None, 'sp'), may hold values from 8 to 16, as said below
- step_count: int32 [], replicated, may hold values from 1 to 20
- kernel: float32 [800, 49], P('lvl'), may hold values from -0.875 to 0.875
- kernel_first: float32 [800, 49], P('lvl'), may hold values from -56 to 56
- kernel_second: float32 [800, 49], P('lvl'), may hold values from 7.86432 to 31.45728
- scales: float32 [2, 800], P(None, 'lvl'), may hold values from 0.5 to 1.5
- scales_first: float32 [2, 800], P(None, 'lvl'), may hold values from -56 to 56
- scales_second: float32 [2, 800], P(None, 'lvl'), may hold values from 7.86432 to 31.45728
- expand: float32 [800, 3200], P(None, 'sp'), may hold values from -0.21875 to 0.21875
- expand_first: float32 [800, 3200], P(None, 'sp'), may hold values from -28 to 28
- expand_second: float32 [800, 3200], P(None, 'sp'), may hold values from 1.96608 to 7.86432
- uplift: float32 [3200], P('sp'), may hold values from -1.75 to 1.75
- uplift_first: float32 [3200], P('sp'), may hold values from -28 to 28
- uplift_second: float32 [3200], P('sp'), may hold values from 1.96608 to 7.86432
- shrink: float32 [3200, 800], P('sp'), may hold values from -0.109375 to 0.109375
- shrink_first: float32 [3200, 800], P('sp'), may hold values from -64 to 64
- shrink_second: float32 [3200, 800], P('sp'), may hold values from 9.8304 to 39.3216
- offset: float32 [800], P('sp'), may hold values from -1.75 to 1.75
- offset_first: float32 [800], P('sp'), may hold values from -112 to 112
- offset_second: float32 [800], P('sp'), may hold values from 27.52512 to 108.1344
Outputs:
- block_output: float32 [3, 800, 128, 128], P(None, 'lvl', 'sp')
- input_grad: float32 [3, 800, 128, 128], P(None, 'lvl', 'sp')
- kernel_grad: float32 [800, 49], P('lvl')
- kernel_moment: float32 [800, 49], P('lvl')
- kernel_next: float32 [800, 49], P('lvl')
- scales_grad: float32 [2, 800], P(None, 'lvl')
- scales_moment: float32 [2, 800], P(None, 'lvl')
- scales_next: float32 [2, 800], P(None, 'lvl')
- expand_grad: float32 [800, 3200], P(None, 'sp')
- expand_moment: float32 [800, 3200], P(None, 'sp')
- expand_next: float32 [800, 3200], P(None, 'sp')
- uplift_grad: float32 [3200], P('sp')
- uplift_moment: float32 [3200], P('sp')
- uplift_next: float32 [3200], P('sp')
- shrink_grad: float32 [3200, 800], P('sp')
- shrink_moment: float32 [3200, 800], P('sp')
- shrink_next: float32 [3200, 800], P('sp')
- offset_grad: float32 [800], P('sp')
- offset_moment: float32 [800], P('sp')
- offset_next: float32 [800], P('sp')
- step_next: int32 [], replicated
The draws below stay inside these ranges and needn't reach their ends.
Inputs may be any that keep to these rules, and one draw needn't show every extreme that they name: `crop_rows`: at least half of a tile's rows; in each micro-batch some tile keeps all 16.
All inputs are finite; a program needn't handle non-finite values. No bound on the sum of `ocean_mask` on one device may be relied on, other than what follows from the above.
Results may differ from the reference program's by a relative error of at most 0.007.
Values may be sent and summed in bfloat16 or wider, within the bound.
A program may use at most 256 MiB of HBM per device.

```python
import math
import jax
import jax.numpy as jnp
from jax import lax

C = 800
H = 3200
KW = 7
MB = 3
WD = 128
TILE_ROWS = 16
TILES = 8
NY = 128
PIXELS = 49152


def draw_crop_rows(key, part):
    base = jax.random.fold_in(key, 7)
    first_key, second_key = jax.random.split(base)
    values = jax.random.randint(first_key, (MB, TILES), TILE_ROWS // 2, TILE_ROWS + 1)
    spot = jax.random.randint(second_key, (MB, 1), 0, TILES)
    places = jnp.arange(TILES, dtype=jnp.int32)[None, :]
    return jnp.where(places == spot, TILE_ROWS, values).astype(jnp.int32)


def plant(drawn, rng, low, top_value):
    spot = [jax.random.randint(jax.random.fold_in(rng, axis), (), 0, length) for axis, length in enumerate(drawn.shape)]
    main_axis = drawn.shape.index(max(drawn.shape))
    neighbour = spot[:main_axis] + [(spot[main_axis] + 1) % drawn.shape[main_axis]] + spot[main_axis + 1:]
    return drawn.at[tuple(spot)].set(low).at[tuple(neighbour)].set(top_value)


def block_scale(rng, shape, cuts, low, top_value):
    loudness, own = 1.0, jax.random.fold_in(rng, 6)
    for dim, blocks in cuts:
        draws = jnp.exp(jax.random.uniform(jax.random.fold_in(own, dim), (blocks,), jnp.float32, low / len(cuts), top_value / len(cuts)))
        loudness = loudness * jnp.repeat(draws, shape[dim] // blocks).reshape([-1 if axis == dim else 1 for axis in range(len(shape))])
    return loudness


def scatter_about(own_key, shape, deviation, limit, cuts=(), held_as=jnp.bfloat16):
    gain = block_scale(own_key, shape, cuts, -0.22, 0.18) if cuts else 1.0
    array = jax.random.normal(own_key, shape, jnp.float32) * deviation * gain
    return jnp.minimum(jnp.maximum(array, -limit), limit).astype(held_as)


def setup_inputs(seed: int = 0) -> dict:
    key_of = jax.random.split(jax.random.key(seed), 24)
    input_field = scatter_about(key_of[0], (MB, C, NY, WD), 1.0, 6.0, ((1, 4), (2, 8)))
    cotangent = scatter_about(key_of[1], (MB, C, NY, WD), 1.0, 6.0, ((1, 4), (2, 8)))
    ocean_mask = plant((jax.random.randint(key_of[2], (MB, NY, WD), 0, 4) < 3).astype(jnp.int32), jax.random.fold_in(key_of[2], 1), 0, 1)
    crop_rows = draw_crop_rows(jax.random.fold_in(key_of[23], 71), 0)
    step_count = jax.random.randint(key_of[4], (), 1, 21).astype(jnp.int32)
    kernel = scatter_about(key_of[5], (C, KW * KW), (KW * KW) ** -0.5, 0.875, ((0, 4),), jnp.float32)
    kernel_first = scatter_about(key_of[6], (C, KW * KW), (0.044 * PIXELS ** 0.5), 56.0, ((0, 4),), jnp.float32)
    kernel_second = jnp.clip(jnp.exp(math.log(31.45728) - 1.3862944 * jax.random.uniform(key_of[7], (C, KW * KW), jnp.float32) ** block_scale(key_of[7], (C, KW * KW), ((0, 4),), -0.2, 0.2)), 7.86432, 31.45728)
    scales = jnp.clip(0.5 + 1.0 * jax.random.uniform(key_of[8], (2, C), jnp.float32) ** block_scale(key_of[8], (2, C), ((1, 4),), -0.2, 0.2), 0.5, 1.5)
    scales_first = scatter_about(key_of[9], (2, C), (0.044 * PIXELS ** 0.5), 56.0, ((1, 4),), jnp.float32)
    scales_second = jnp.clip(jnp.exp(math.log(31.45728) - 1.3862944 * jax.random.uniform(key_of[10], (2, C), jnp.float32) ** block_scale(key_of[10], (2, C), ((1, 4),), -0.2, 0.2)), 7.86432, 31.45728)
    expand = scatter_about(key_of[11], (C, H), C ** -0.5, 0.21875, ((1, 8),), jnp.float32)
    expand_first = scatter_about(key_of[12], (C, H), (0.022 * PIXELS ** 0.5), 28.0, ((1, 8),), jnp.float32)
    expand_second = jnp.clip(jnp.exp(math.log(7.86432) - 1.3862944 * jax.random.uniform(key_of[13], (C, H), jnp.float32) ** block_scale(key_of[13], (C, H), ((1, 8),), -0.2, 0.2)), 1.96608, 7.86432)
    uplift = scatter_about(key_of[14], (H,), 0.3, 1.75, ((0, 8),), jnp.float32)
    uplift_first = scatter_about(key_of[15], (H,), (0.022 * PIXELS ** 0.5), 28.0, ((0, 8),), jnp.float32)
    uplift_second = jnp.clip(jnp.exp(math.log(7.86432) - 1.3862944 * jax.random.uniform(key_of[16], (H,), jnp.float32) ** block_scale(key_of[16], (H,), ((0, 8),), -0.2, 0.2)), 1.96608, 7.86432)
    shrink = scatter_about(key_of[17], (H, C), H ** -0.5, 0.109375, ((0, 8),), jnp.float32)
    shrink_first = scatter_about(key_of[18], (H, C), (0.05 * PIXELS ** 0.5), 64.0, ((0, 8),), jnp.float32)
    shrink_second = jnp.clip(jnp.exp(math.log(39.3216) - 1.3862944 * jax.random.uniform(key_of[19], (H, C), jnp.float32) ** block_scale(key_of[19], (H, C), ((0, 8),), -0.2, 0.2)), 9.8304, 39.3216)
    offset = scatter_about(key_of[20], (C,), 0.3, 1.75, ((0, 8),), jnp.float32)
    offset_first = scatter_about(key_of[21], (C,), (0.083 * PIXELS ** 0.5), 112.0, ((0, 8),), jnp.float32)
    offset_second = jnp.clip(jnp.exp(math.log(108.1344) - 1.3682759 * jax.random.uniform(key_of[22], (C,), jnp.float32) ** block_scale(key_of[22], (C,), ((0, 8),), -0.2, 0.2)), 27.52512, 108.1344)
    return dict(input_field=input_field, cotangent=cotangent, ocean_mask=ocean_mask, crop_rows=crop_rows, step_count=step_count, kernel=kernel, kernel_first=kernel_first, kernel_second=kernel_second, scales=scales, scales_first=scales_first, scales_second=scales_second, expand=expand, expand_first=expand_first, expand_second=expand_second, uplift=uplift, uplift_first=uplift_first, uplift_second=uplift_second, shrink=shrink, shrink_first=shrink_first, shrink_second=shrink_second, offset=offset, offset_first=offset_first, offset_second=offset_second)


@jax.custom_vjp
def low(v):
    return lax.optimization_barrier(v.astype(jnp.bfloat16)).astype(jnp.float32)

@jax.custom_vjp
def low_back(v):
    return v

def low_keep(v):
    return (low(v), None)

def low_pass(kept, grad):
    return (grad,)

def back_keep(v):
    return (v, None)

def back_low(kept, grad):
    return (low(grad),)
low.defvjp(low_keep, low_pass)
low_back.defvjp(back_keep, back_low)
beta_one = 0.9
beta_two = 0.999
epsilon = 1e-08
weight_decay = 0.01
highest = lax.Precision.HIGHEST

def depthwise(field_now, kernel):
    margin = KW // 2
    height = field_now.shape[1]
    breadth = field_now.shape[2]
    padded = jnp.pad(field_now, ((0, 0), (margin, margin), (margin, margin)))
    running = jnp.zeros_like(field_now)
    for vertical in range(KW):
        for lateral in range(KW):
            weights_now = kernel[:, vertical * KW + lateral][:, None, None]
            running = running + weights_now * padded[:, vertical:vertical + height, lateral:lateral + breadth]
    return running

def one_batch(field_raw, mask_now, crop_now, kernel, scales, expand_low, uplift_low, shrink_low, offset_low):
    row_ids = jnp.arange(NY, dtype=jnp.int32)
    limits = crop_now[row_ids // TILE_ROWS]
    valid_rows = (row_ids % TILE_ROWS < limits).astype(jnp.float32)[None, :, None]
    field_now = field_raw * valid_rows
    ocean_cells = mask_now.astype(jnp.float32)[None] * valid_rows
    convolved = depthwise(field_now, kernel)
    ocean_count = jnp.maximum(jnp.sum(ocean_cells), 1.0)
    mean_value = lax.optimization_barrier(jnp.sum(ocean_cells * convolved, axis=(1, 2))) / ocean_count
    centred = convolved - mean_value[:, None, None]
    variance = lax.optimization_barrier(jnp.sum(ocean_cells * centred * centred, axis=(1, 2))) / ocean_count
    whitened = centred * lax.rsqrt(variance + 1e-05)[:, None, None]
    normed = whitened * scales[0][:, None, None] + scales[1][:, None, None]
    sent_field = low_back(low(normed))
    pixels = NY * WD
    block_size = math.gcd(pixels, 4096)
    pieces = sent_field.reshape(C, pixels // block_size, block_size).transpose(1, 0, 2)

    def feed_forward(piece_now):
        hidden = jnp.dot(expand_low.T, piece_now, precision=highest, preferred_element_type=jnp.float32) + uplift_low[:, None]
        active = low(jax.nn.gelu(low_back(hidden)))
        result = jnp.dot(shrink_low.T, active, precision=highest, preferred_element_type=jnp.float32) + offset_low[:, None]
        return low_back(low(result))
    mixed_back = lax.map(jax.checkpoint(feed_forward), pieces).transpose(1, 0, 2).reshape(C, NY, WD)
    return ocean_cells * (field_now + mixed_back)

def adamw(weight, first, second, grad, rate, step_float):
    first_new = beta_one * first + (1.0 - beta_one) * grad
    second_new = beta_two * second + (1.0 - beta_two) * grad * grad
    fix_first = 1.0 - jnp.power(beta_one, step_float)
    fix_second = 1.0 - jnp.power(beta_two, step_float)
    update = first_new / fix_first / (jnp.sqrt(second_new / fix_second) + epsilon) + weight_decay * weight
    return (second_new, weight - rate * update)

def reference(input_field, cotangent, ocean_mask, crop_rows, step_count, kernel, kernel_first, kernel_second, scales, scales_first, scales_second, expand, expand_first, expand_second, uplift, uplift_first, uplift_second, shrink, shrink_first, shrink_second, offset, offset_first, offset_second):

    def forward(field_all, kernel_in, scales_in, expand_in, uplift_in, shrink_in, offset_in):
        expand_low = low(expand_in)
        uplift_low = low(uplift_in)
        shrink_low = low(shrink_in)
        offset_low = low(offset_in)

        def batch_run(batch_items):
            return jax.checkpoint(one_batch)(batch_items[0], batch_items[1], batch_items[2], kernel_in, scales_in, expand_low, uplift_low, shrink_low, offset_low)
        return lax.map(batch_run, (field_all, ocean_mask, crop_rows))
    block_output, pull_back = jax.vjp(forward, input_field.astype(jnp.float32), kernel, scales, expand, uplift, shrink, offset)
    gradients = pull_back(cotangent.astype(jnp.float32))
    step_float = (step_count + 1).astype(jnp.float32)
    kernel_moment, kernel_next = adamw(kernel, kernel_first, kernel_second, gradients[1], 0.15, step_float)
    scales_moment, scales_next = adamw(scales, scales_first, scales_second, gradients[2], 0.2, step_float)
    expand_moment, expand_next = adamw(expand, expand_first, expand_second, gradients[3], 0.035, step_float)
    uplift_moment, uplift_next = adamw(uplift, uplift_first, uplift_second, gradients[4], 0.1, step_float)
    shrink_moment, shrink_next = adamw(shrink, shrink_first, shrink_second, gradients[5], 0.018, step_float)
    offset_moment, offset_next = adamw(offset, offset_first, offset_second, gradients[6], 0.1, step_float)
    return (block_output, gradients[0], gradients[1], kernel_moment, kernel_next, gradients[2], scales_moment, scales_next, gradients[3], expand_moment, expand_next, gradients[4], uplift_moment, uplift_next, gradients[5], shrink_moment, shrink_next, gradients[6], offset_moment, offset_next, step_count + 1)
```

```python
import functools
import math

import jax
import jax.numpy as jnp
from jax import lax
from jax.experimental import pallas as pl
from jax.experimental.pallas import tpu as pltpu
from jax.sharding import PartitionSpec as P

KW = 7
MARGIN = KW // 2
GROUP = 8
ROWS = 16

beta_one = 0.9
beta_two = 0.999
epsilon = 1e-08
weight_decay = 0.01
GELU_A = math.sqrt(2.0 / math.pi)
GELU_B = 0.044715


def adamw(weight, first, second, grad, rate, step_float):
    first_new = beta_one * first + (1.0 - beta_one) * grad
    second_new = beta_two * second + (1.0 - beta_two) * grad * grad
    fix_first = 1.0 - jnp.power(beta_one, step_float)
    fix_second = 1.0 - jnp.power(beta_two, step_float)
    update = (
        first_new / fix_first / (jnp.sqrt(second_new / fix_second) + epsilon)
        + weight_decay * weight
    )
    return (second_new, weight - rate * update)


def lane_tap_masks(width):
    lane = lax.broadcasted_iota(jnp.int32, (GROUP, width), 1)
    return [
        jnp.logical_and(lane + (b - MARGIN) >= 0, lane + (b - MARGIN) < width)
        for b in range(KW)
    ]


def shifted(value, amount):
    width = value.shape[-1]
    turn = (-amount) % width
    return value if turn == 0 else pltpu.roll(value, turn, 1)


def put_columns(columns):
    lane = lax.broadcasted_iota(jnp.int32, (GROUP, 128), 1)
    out = jnp.zeros((GROUP, 128), jnp.float32)
    for at, column in columns:
        out = jnp.where(lane == at, column, out)
    return out


def conv_body(
    crop, x_ref, cot_ref, up_ref, dn_ref, k_ref, mask_ref,
    conv_ref, xt_ref, dres_ref, stat_ref, scr, scc, wscr,
):
    batches, _, height, width = x_ref.shape
    masks = lane_tap_masks(width)
    for a in range(KW):
        for b in range(KW):
            t = a * KW + b
            spread = jnp.broadcast_to(k_ref[:, t : t + 1], (GROUP, width))
            wscr[t] = jnp.where(masks[b], spread, 0.0)

    def one(m, stats):
        for c in range(GROUP):
            scr[c * height : (c + 1) * height, :] = x_ref[m, c].astype(jnp.float32)
            scc[c * height : (c + 1) * height, :] = cot_ref[m, c].astype(jnp.float32)
        limit = crop[m, 0]
        for i in range(height):
            row = scr[pl.ds(i, GROUP, stride=height), :]
            xt_ref[m, MARGIN + i] = jnp.where(i < limit, row, 0.0)
            back = scc[pl.ds(i, GROUP, stride=height), :]
            dres_ref[m, i] = (back * mask_ref[m, i : i + 1, :]).astype(jnp.bfloat16)
        for r in range(MARGIN):
            xt_ref[m, r] = up_ref[m, r].astype(jnp.float32)
            xt_ref[m, MARGIN + height + r] = dn_ref[m, r].astype(jnp.float32)
        total = jnp.zeros((GROUP, width), jnp.float32)
        for base in range(0, height, ROWS):
            acc = [None] * ROWS
            for b in range(KW):
                rolled = [
                    shifted(xt_ref[m, base + r], b - MARGIN) for r in range(ROWS + KW - 1)
                ]
                for a in range(KW):
                    tap = wscr[a * KW + b]
                    for i in range(ROWS):
                        term = tap * rolled[i + a]
                        acc[i] = term if acc[i] is None else acc[i] + term
            for i in range(ROWS):
                conv_ref[m, base + i] = acc[i]
                total = total + acc[i] * mask_ref[m, base + i : base + i + 1, :]
        cells = jnp.sum(mask_ref[m])
        summed = jnp.sum(total, axis=1, keepdims=True)
        mean = summed / jnp.maximum(cells, 1.0)
        spread = jnp.zeros((GROUP, width), jnp.float32)
        for i in range(height):
            off = conv_ref[m, i] - mean
            spread = spread + off * off * mask_ref[m, i : i + 1, :]
        squares = jnp.sum(spread, axis=1, keepdims=True)
        lane = lax.broadcasted_iota(jnp.int32, (GROUP, 128), 1)
        stats = jnp.where(lane == m, summed, stats)
        stats = jnp.where(lane == batches + m, squares, stats)
        return jnp.where(lane == 2 * batches + m, cells, stats)

    stat_ref[...] = lax.fori_loop(0, batches, one, jnp.zeros((GROUP, 128), jnp.float32))


def conv_forward(crop, x, cot, up, down, kernel, mask_cells):
    batches, channels, height, width = x.shape
    groups = pl.cdiv(channels, GROUP)
    natural = pl.BlockSpec((batches, GROUP, height, width), lambda g, c: (0, g, 0, 0))
    turned = lambda rows: pl.BlockSpec((batches, rows, GROUP, width), lambda g, c: (0, 0, g, 0))
    return pl.pallas_call(
        conv_body,
        grid_spec=pltpu.PrefetchScalarGridSpec(
            num_scalar_prefetch=1,
            grid=(groups,),
            in_specs=[
                natural,
                natural,
                turned(MARGIN),
                turned(MARGIN),
                pl.BlockSpec((GROUP, KW * KW), lambda g, c: (g, 0)),
                pl.BlockSpec((batches, height, width), lambda g, c: (0, 0, 0)),
            ],
            out_specs=[
                turned(height),
                turned(height + 2 * MARGIN),
                turned(height),
                pl.BlockSpec((GROUP, 128), lambda g, c: (g, 0)),
            ],
            scratch_shapes=[
                pltpu.VMEM((GROUP * height, width), jnp.float32),
                pltpu.VMEM((GROUP * height, width), jnp.float32),
                pltpu.VMEM((KW * KW, GROUP, width), jnp.float32),
            ],
        ),
        out_shape=[
            jax.ShapeDtypeStruct((batches, height, channels, width), jnp.float32),
            jax.ShapeDtypeStruct((batches, height + 2 * MARGIN, channels, width), jnp.float32),
            jax.ShapeDtypeStruct((batches, height, channels, width), jnp.bfloat16),
            jax.ShapeDtypeStruct((channels, 128), jnp.float32),
        ],
        cost_estimate=pl.CostEstimate(
            flops=2 * KW * KW * batches * channels * height * width,
            bytes_accessed=30 * batches * channels * height * width,
            transcendentals=0,
        ),
    )(crop, x, cot, up, down, kernel, mask_cells)


def chunks_of(total, size):
    return [(start, min(size, total - start)) for start in range(0, total, size)]


def nt(a, b):
    return lax.dot_general(a, b, (((1,), (1,)), ((), ())), preferred_element_type=jnp.float32)


def nn(a, b):
    return jnp.dot(a, b, preferred_element_type=jnp.float32)


def mlp_body(
    pin_ref, back_ref, et_ref, w_ref, up_ref, off_ref,
    res_ref, dn_ref, ge_out, gw_out, gu_out, go_out,
    pin, pint, back, backt, res_acc, dn_acc, ge, gw, gu, go,
):
    m = pl.program_id(0)
    last = pl.num_programs(0) - 1
    rows, channels, width = pin_ref.shape[1:]
    hidden = et_ref.shape[0]
    for r in range(rows):
        cols = slice(r * width, (r + 1) * width)
        value = pin_ref[0, r]
        pin[:, cols] = value
        pint[cols, :] = value.T
        value = back_ref[0, r]
        back[:, cols] = value
        backt[cols, :] = value.T

    @pl.when(m == 0)
    def _():
        ge[...] = jnp.zeros_like(ge)
        gw[...] = jnp.zeros_like(gw)
        gu[...] = jnp.zeros_like(gu)
        go[...] = jnp.zeros_like(go)

    go[...] += jnp.sum(backt[...].astype(jnp.float32), axis=0, keepdims=True)
    for index, (start, size) in enumerate(chunks_of(hidden, 512)):
        span = slice(start, start + size)
        et = et_ref[span, :]
        wt = w_ref[span, :]
        hid = nt(pint[...], et) + up_ref[:, span]
        dact = nt(backt[...], wt)
        square = hid * hid
        inner = GELU_A * hid * (1.0 + GELU_B * square)
        t = jnp.tanh(inner)
        half = 0.5 * (1.0 + t)
        act = (hid * half).astype(jnp.bfloat16)
        slope = half + 0.5 * hid * (1.0 - t * t) * (GELU_A * (1.0 + 3.0 * GELU_B * square))
        dhid = (slope * dact).astype(jnp.bfloat16)
        res_part = nn(act, wt)
        dn_part = nn(dhid, et)
        if index == 0:
            res_acc[...] = res_part
            dn_acc[...] = dn_part
        else:
            res_acc[...] += res_part
            dn_acc[...] += dn_part
        ge[:, span] += nn(pin[...], dhid)
        gw[:, span] += nn(back[...], act)
        gu[:, span] += jnp.sum(dhid.astype(jnp.float32), axis=0, keepdims=True)

        @pl.when(m == last)
        def _():
            ge_out[span, :] = ge[:, span].astype(jnp.bfloat16).T
            gw_out[span, :] = gw[:, span].astype(jnp.bfloat16).T

    for r in range(rows):
        cols = slice(r * width, (r + 1) * width)
        res_ref[0, r] = (res_acc[cols, :] + off_ref[...]).astype(jnp.bfloat16).T
        dn_ref[0, r] = dn_acc[cols, :].astype(jnp.bfloat16).T

    @pl.when(m == last)
    def _():
        gu_out[...] = gu[...]
        go_out[...] = go[...]


def mlp(pin, back, expand_t, shrink, uplift, offset):
    batches, rows, channels, width = pin.shape
    hidden = expand_t.shape[0]
    pixels = rows * width
    block = pl.BlockSpec((1, rows, channels, width), lambda m: (m, 0, 0, 0))
    whole = lambda shape: pl.BlockSpec(shape, lambda m: (0, 0), pipeline_mode=pl.Buffered(1))
    bf, f32 = jnp.bfloat16, jnp.float32
    return pl.pallas_call(
        mlp_body,
        grid=(batches,),
        in_specs=[
            block, block,
            whole((hidden, channels)), whole((hidden, channels)),
            whole((1, hidden)), whole((1, channels)),
        ],
        out_specs=[
            block, block,
            whole((hidden, channels)), whole((hidden, channels)),
            whole((1, hidden)), whole((1, channels)),
        ],
        out_shape=[
            jax.ShapeDtypeStruct(pin.shape, bf),
            jax.ShapeDtypeStruct(pin.shape, bf),
            jax.ShapeDtypeStruct((hidden, channels), bf),
            jax.ShapeDtypeStruct((hidden, channels), bf),
            jax.ShapeDtypeStruct((1, hidden), f32),
            jax.ShapeDtypeStruct((1, channels), f32),
        ],
        scratch_shapes=[
            pltpu.VMEM((channels, pixels), bf),
            pltpu.VMEM((pixels, channels), bf),
            pltpu.VMEM((channels, pixels), bf),
            pltpu.VMEM((pixels, channels), bf),
            pltpu.VMEM((pixels, channels), f32),
            pltpu.VMEM((pixels, channels), f32),
            pltpu.VMEM((channels, hidden), f32),
            pltpu.VMEM((channels, hidden), f32),
            pltpu.VMEM((1, hidden), f32),
            pltpu.VMEM((1, channels), f32),
        ],
        compiler_params=pltpu.CompilerParams(vmem_limit_bytes=62 * 1024 * 1024),
        cost_estimate=pl.CostEstimate(
            flops=12 * batches * pixels * channels * hidden,
            bytes_accessed=2 * 4 * channels * hidden,
            transcendentals=batches * pixels * hidden,
        ),
    )(pin, back, expand_t, shrink, uplift, offset)


def sums_body(xt_ref, res_ref, dn_ref, conv_ref, mask_ref, par_ref, out_ref, stat_ref, scr):
    batches, height = res_ref.shape[:2]
    width = res_ref.shape[3]

    def one(m, stats):
        lane = lax.broadcasted_iota(jnp.int32, (GROUP, 128), 1)
        mean = jnp.sum(jnp.where(lane == m, par_ref[...], 0.0), axis=1, keepdims=True)
        rho = jnp.sum(jnp.where(lane == batches + m, par_ref[...], 0.0), axis=1, keepdims=True)
        mean = jnp.broadcast_to(mean, (GROUP, width))
        rho = jnp.broadcast_to(rho, (GROUP, width))
        plain = jnp.zeros((GROUP, width), jnp.float32)
        cross = jnp.zeros((GROUP, width), jnp.float32)
        for i in range(height):
            grad = dn_ref[m, i].astype(jnp.float32)
            plain = plain + grad
            cross = cross + grad * ((conv_ref[m, i] - mean) * rho)
            value = xt_ref[m, MARGIN + i] + res_ref[m, i].astype(jnp.float32)
            scr[pl.ds(i, GROUP, stride=height), :] = value * mask_ref[m, i : i + 1, :]
        for c in range(GROUP):
            out_ref[m, c] = scr[c * height : (c + 1) * height, :]
        stats = jnp.where(lane == m, jnp.sum(plain, axis=1, keepdims=True), stats)
        return jnp.where(lane == batches + m, jnp.sum(cross, axis=1, keepdims=True), stats)

    stat_ref[...] = lax.fori_loop(0, batches, one, jnp.zeros((GROUP, 128), jnp.float32))


def output_and_sums(xt, res, dn, conv, mask_cells, params):
    batches, height, channels, width = res.shape
    turned = lambda rows: pl.BlockSpec((batches, rows, GROUP, width), lambda g: (0, 0, g, 0))
    return pl.pallas_call(
        sums_body,
        grid=(pl.cdiv(channels, GROUP),),
        in_specs=[
            turned(height + 2 * MARGIN),
            turned(height), turned(height), turned(height),
            pl.BlockSpec((batches, height, width), lambda g: (0, 0, 0)),
            pl.BlockSpec((GROUP, 128), lambda g: (g, 0)),
        ],
        out_specs=[
            pl.BlockSpec((batches, GROUP, height, width), lambda g: (0, g, 0, 0)),
            pl.BlockSpec((GROUP, 128), lambda g: (g, 0)),
        ],
        out_shape=[
            jax.ShapeDtypeStruct((batches, channels, height, width), jnp.float32),
            jax.ShapeDtypeStruct((channels, 128), jnp.float32),
        ],
        scratch_shapes=[pltpu.VMEM((GROUP * height, width), jnp.float32)],
        cost_estimate=pl.CostEstimate(
            flops=10 * batches * channels * height * width,
            bytes_accessed=20 * batches * channels * height * width,
            transcendentals=0,
        ),
    )(xt, res, dn, conv, mask_cells, params)


def conv_back_body(
    crop, xt_ref, grad_ref, up_ref, dn_ref, cot_ref, k_ref, mask_ref,
    out_ref, kg_ref, scr, wscr, frame, sums,
):
    batches, height = grad_ref.shape[:2]
    width = grad_ref.shape[3]
    masks = lane_tap_masks(width)
    for a in range(KW):
        for b in range(KW):
            t = a * KW + b
            spread = jnp.broadcast_to(k_ref[:, t : t + 1], (GROUP, width))
            wscr[t] = jnp.where(masks[KW - 1 - b], spread, 0.0)
            sums[t] = jnp.zeros((GROUP, width), jnp.float32)

    def one(m, carry):
        for r in range(MARGIN):
            frame[r] = up_ref[m, r]
            frame[MARGIN + height + r] = dn_ref[m, r]
        for i in range(height):
            frame[MARGIN + i] = grad_ref[m, i]
        for base in range(0, height, ROWS):
            for b in range(KW):
                rolled = [
                    shifted(xt_ref[m, base + r], b - MARGIN) for r in range(ROWS + KW - 1)
                ]
                for a in range(KW):
                    part = None
                    for i in range(ROWS):
                        term = frame[MARGIN + base + i] * rolled[i + a]
                        part = term if part is None else part + term
                    sums[a * KW + b] += part
            acc = [None] * ROWS
            for b in range(KW):
                rolled = [
                    shifted(frame[base + r], MARGIN - b) for r in range(ROWS + KW - 1)
                ]
                for a in range(KW):
                    tap = wscr[a * KW + b]
                    for i in range(ROWS):
                        term = tap * rolled[i + KW - 1 - a]
                        acc[i] = term if acc[i] is None else acc[i] + term
            for i in range(ROWS):
                scr[pl.ds(base + i, GROUP, stride=height), :] = acc[i]
        row = lax.broadcasted_iota(jnp.int32, (height, width), 0)
        for c in range(GROUP):
            dres = cot_ref[m, c].astype(jnp.float32) * mask_ref[m]
            total = dres + scr[c * height : (c + 1) * height, :]
            out_ref[m, c] = jnp.where(row < crop[m, 0], total, 0.0)
        return carry

    lax.fori_loop(0, batches, one, 0)
    columns = []
    for t in range(KW * KW):
        kept = jnp.where(masks[t % KW], sums[t], 0.0)
        columns.append((t, jnp.sum(kept, axis=1, keepdims=True)))
    kg_ref[...] = put_columns(columns)


def conv_backward(crop, xt, grad_conv, up, down, cot, kernel, mask_cells):
    batches, height, channels, width = grad_conv.shape
    natural = pl.BlockSpec((batches, GROUP, height, width), lambda g, c: (0, g, 0, 0))
    turned = lambda rows: pl.BlockSpec((batches, rows, GROUP, width), lambda g, c: (0, 0, g, 0))
    return pl.pallas_call(
        conv_back_body,
        grid_spec=pltpu.PrefetchScalarGridSpec(
            num_scalar_prefetch=1,
            grid=(pl.cdiv(channels, GROUP),),
            in_specs=[
                turned(height + 2 * MARGIN),
                turned(height),
                turned(MARGIN), turned(MARGIN),
                natural,
                pl.BlockSpec((GROUP, KW * KW), lambda g, c: (g, 0)),
                pl.BlockSpec((batches, height, width), lambda g, c: (0, 0, 0)),
            ],
            out_specs=[natural, pl.BlockSpec((GROUP, 128), lambda g, c: (g, 0))],
            scratch_shapes=[
                pltpu.VMEM((GROUP * height, width), jnp.float32),
                pltpu.VMEM((KW * KW, GROUP, width), jnp.float32),
                pltpu.VMEM((height + 2 * MARGIN, GROUP, width), jnp.float32),
                pltpu.VMEM((KW * KW, GROUP, width), jnp.float32),
            ],
        ),
        out_shape=[
            jax.ShapeDtypeStruct((batches, channels, height, width), jnp.float32),
            jax.ShapeDtypeStruct((channels, 128), jnp.float32),
        ],
        cost_estimate=pl.CostEstimate(
            flops=4 * KW * KW * batches * channels * height * width,
            bytes_accessed=14 * batches * channels * height * width,
            transcendentals=0,
        ),
    )(crop, xt, grad_conv, up, down, cot, kernel, mask_cells)


def neighbours(head, tail, axis):
    count = lax.axis_size(axis)
    up = lax.ppermute(tail, axis, [(i, i + 1) for i in range(count - 1)])
    down = lax.ppermute(head, axis, [(i + 1, i) for i in range(count - 1)])
    return up, down


def on_device(
    input_field, cotangent, ocean_mask, crop_rows, step_count,
    kernel, kernel_first, kernel_second,
    scales, scales_first, scales_second,
    expand, expand_first, expand_second,
    uplift, uplift_first, uplift_second,
    shrink, shrink_first, shrink_second,
    offset, offset_first, offset_second,
):
    f32, bf = jnp.float32, jnp.bfloat16
    batches, channels, height, width = input_field.shape
    sp = lax.axis_size("sp")
    lvl = lax.axis_size("lvl")
    expand_all = lax.all_gather(expand.T.astype(bf), "sp", axis=0, tiled=True)
    shrink_all = lax.all_gather(shrink.astype(bf), "sp", axis=0, tiled=True)
    uplift_all = lax.all_gather(uplift.astype(bf), "sp", axis=0, tiled=True)
    offset_all = lax.all_gather(offset.astype(bf), "sp", axis=0, tiled=True)

    valid = (jnp.arange(height, dtype=jnp.int32)[None, :] < crop_rows).astype(f32)
    mask_cells = ocean_mask.astype(f32) * valid[:, :, None]
    valid_low = valid.astype(bf)[:, None, :, None]
    head = input_field[:, :, :MARGIN] * valid_low[:, :, :MARGIN]
    tail = input_field[:, :, height - MARGIN :] * valid_low[:, :, height - MARGIN :]
    up, down = neighbours(head.transpose(0, 2, 1, 3), tail.transpose(0, 2, 1, 3), "sp")
    conv, xt, dres, stats = conv_forward(
        crop_rows, input_field, cotangent, up, down, kernel, mask_cells
    )
    every = lax.all_gather(stats[:, : 4 * batches], "sp", axis=0)
    sums = every[:, :, :batches]
    squares = every[:, :, batches : 2 * batches]
    cells = every[:, :, 2 * batches : 3 * batches]
    count = jnp.maximum(jnp.sum(cells, axis=0), 1.0)
    mean = jnp.sum(sums, axis=0) / count
    gap = sums / jnp.maximum(cells, 1.0) - mean[None]
    variance = jnp.sum(squares + cells * gap * gap, axis=0) / count
    rho = lax.rsqrt(variance + 1e-05)

    def spread(stat):
        return stat.T[:, None, :, None]

    gain = scales[0][None, None, :, None]
    shift = scales[1][None, None, :, None]
    normed = ((conv - spread(mean)) * spread(rho) * gain + shift).astype(bf)

    def to_pixels(v):
        return lax.all_to_all(v, "lvl", split_axis=1, concat_axis=2, tiled=True)

    def to_channels(v):
        return lax.all_to_all(v, "lvl", split_axis=2, concat_axis=1, tiled=True)

    pixel_back = to_pixels(dres)
    pixel_in = to_pixels(normed)
    result, grad_normed, grad_expand, grad_shrink, grad_uplift, grad_offset = mlp(
        pixel_in, pixel_back, expand_all, shrink_all,
        uplift_all.astype(f32)[None], offset_all.astype(f32)[None],
    )
    result = to_channels(result)
    grad_normed = to_channels(grad_normed)
    params = jnp.concatenate([mean, rho], axis=1)
    params = jnp.pad(params, ((0, 0), (0, 128 - params.shape[1])))
    block_output, local = output_and_sums(xt, result, grad_normed, conv, mask_cells, params)
    both = lax.psum(local[:, : 2 * batches], "sp")
    plain, cross = both[:, :batches], both[:, batches:]
    scales_grad = jnp.stack([jnp.sum(cross, axis=1), jnp.sum(plain, axis=1)], axis=0)
    whitened = (conv - spread(mean)) * spread(rho)
    grad_conv = spread(rho) * (
        gain * grad_normed.astype(f32)
        - mask_cells[:, :, None, :] * gain * (spread(plain) + whitened * spread(cross)) / spread(count)
    )
    back_up, back_down = neighbours(
        grad_conv[:, :MARGIN], grad_conv[:, height - MARGIN :], "sp"
    )
    input_grad, kernel_cols = conv_backward(
        crop_rows, xt, grad_conv, back_up, back_down, cotangent, kernel, mask_cells
    )
    kernel_grad = lax.psum(kernel_cols[:, : KW * KW], "sp")

    def own_share(partial):
        rows = partial.shape[0] // sp
        parts = lax.all_to_all(
            partial.reshape(sp, rows, partial.shape[1]), "sp", split_axis=0, concat_axis=0
        )
        share = jnp.sum(parts.astype(f32), axis=0).astype(bf)
        return jnp.sum(lax.all_gather(share, "lvl", axis=0).astype(f32), axis=0)

    share_expand = own_share(grad_expand)
    share_shrink = own_share(grad_shrink)
    small = lax.psum(
        jnp.concatenate([grad_uplift[0], grad_offset[0]]), ("sp", "lvl")
    )
    place = lax.axis_index("sp")
    share_uplift = lax.dynamic_slice_in_dim(small, place * uplift.shape[0], uplift.shape[0])
    share_offset = lax.dynamic_slice_in_dim(
        small, uplift_all.shape[0] + place * offset.shape[0], offset.shape[0]
    )
    step_float = (step_count + 1).astype(f32)
    kernel_moment, kernel_next = adamw(
        kernel, kernel_first, kernel_second, kernel_grad, 0.15, step_float
    )
    scales_moment, scales_next = adamw(
        scales, scales_first, scales_second, scales_grad, 0.2, step_float
    )
    expand_grad = share_expand.T
    expand_moment, expand_next = adamw(
        expand, expand_first, expand_second, expand_grad, 0.035, step_float
    )
    uplift_moment, uplift_next = adamw(
        uplift, uplift_first, uplift_second, share_uplift, 0.1, step_float
    )
    shrink_moment, shrink_next = adamw(
        shrink, shrink_first, shrink_second, share_shrink, 0.018, step_float
    )
    offset_moment, offset_next = adamw(
        offset, offset_first, offset_second, share_offset, 0.1, step_float
    )
    return (
        block_output, input_grad,
        kernel_grad, kernel_moment, kernel_next,
        scales_grad, scales_moment, scales_next,
        expand_grad, expand_moment, expand_next,
        share_uplift, uplift_moment, uplift_next,
        share_shrink, shrink_moment, shrink_next,
        share_offset, offset_moment, offset_next,
        step_count + 1,
    )


def solution(mesh):
    tile = P(None, "lvl", "sp", None)
    by_channel = P("lvl", None)
    by_scale = P(None, "lvl")
    by_hidden = P(None, "sp")
    by_row = P("sp", None)
    line = P("sp")
    in_specs = (
        tile, tile, P(None, "sp", None), P(None, "sp"), P(),
        by_channel, by_channel, by_channel,
        by_scale, by_scale, by_scale,
        by_hidden, by_hidden, by_hidden,
        line, line, line,
        by_row, by_row, by_row,
        line, line, line,
    )
    out_specs = (
        tile, tile,
        by_channel, by_channel, by_channel,
        by_scale, by_scale, by_scale,
        by_hidden, by_hidden, by_hidden,
        line, line, line,
        by_row, by_row, by_row,
        line, line, line,
        P(),
    )
    return jax.shard_map(
        on_device, mesh=mesh, in_specs=in_specs, out_specs=out_specs, check_vma=False
    )
```

```python
import functools
import math

import jax
import jax.numpy as jnp
from jax import lax
from jax.experimental import pallas as pl
from jax.experimental.pallas import tpu as pltpu
from jax.sharding import PartitionSpec as P

KW = 7
MARGIN = KW // 2
GROUP = 8
ROWS = 16

beta_one = 0.9
beta_two = 0.999
epsilon = 1e-08
weight_decay = 0.01
GELU_A = math.sqrt(2.0 / math.pi)
GELU_B = 0.044715


def adamw(weight, first, second, grad, rate, step_float):
    first_new = beta_one * first + (1.0 - beta_one) * grad
    second_new = beta_two * second + (1.0 - beta_two) * grad * grad
    fix_first = 1.0 - jnp.power(beta_one, step_float)
    fix_second = 1.0 - jnp.power(beta_two, step_float)
    update = (
        first_new / fix_first / (jnp.sqrt(second_new / fix_second) + epsilon)
        + weight_decay * weight
    )
    return (second_new, weight - rate * update)


def lane_tap_masks(width):
    lane = lax.broadcasted_iota(jnp.int32, (GROUP, width), 1)
    return [
        jnp.logical_and(lane + (b - MARGIN) >= 0, lane + (b - MARGIN) < width)
        for b in range(KW)
    ]


def shifted(value, amount):
    width = value.shape[-1]
    turn = (-amount) % width
    return value if turn == 0 else pltpu.roll(value, turn, 1)


def put_columns(columns):
    lane = lax.broadcasted_iota(jnp.int32, (GROUP, 128), 1)
    out = jnp.zeros((GROUP, 128), jnp.float32)
    for at, column in columns:
        out = jnp.where(lane == at, column, out)
    return out


def conv_body(
    crop, x_ref, cot_ref, up_ref, dn_ref, k_ref, mask_ref,
    conv_ref, xt_ref, dres_ref, stat_ref, scr, scc, wscr,
):
    batches, _, height, width = x_ref.shape
    masks = lane_tap_masks(width)
    for a in range(KW):
        for b in range(KW):
            t = a * KW + b
            spread = jnp.broadcast_to(k_ref[:, t : t + 1], (GROUP, width))
            wscr[t] = jnp.where(masks[b], spread, 0.0)

    def one(m, stats):
        for c in range(GROUP):
            scr[c * height : (c + 1) * height, :] = x_ref[m, c].astype(jnp.float32)
            scc[c * height : (c + 1) * height, :] = cot_ref[m, c].astype(jnp.float32)
        limit = crop[m, 0]
        for i in range(height):
            row = scr[pl.ds(i, GROUP, stride=height), :]
            xt_ref[m, MARGIN + i] = jnp.where(i < limit, row, 0.0)
            back = scc[pl.ds(i, GROUP, stride=height), :]
            dres_ref[m, i] = (back * mask_ref[m, i : i + 1, :]).astype(jnp.bfloat16)
        for r in range(MARGIN):
            xt_ref[m, r] = up_ref[m, r].astype(jnp.float32)
            xt_ref[m, MARGIN + height + r] = dn_ref[m, r].astype(jnp.float32)
        total = jnp.zeros((GROUP, width), jnp.float32)
        for base in range(0, height, ROWS):
            acc = [None] * ROWS
            for b in range(KW):
                rolled = [
                    shifted(xt_ref[m, base + r], b - MARGIN) for r in range(ROWS + KW - 1)
                ]
                for a in range(KW):
                    tap = wscr[a * KW + b]
                    for i in range(ROWS):
                        term = tap * rolled[i + a]
                        acc[i] = term if acc[i] is None else acc[i] + term
            for i in range(ROWS):
                conv_ref[m, base + i] = acc[i]
                total = total + acc[i] * mask_ref[m, base + i : base + i + 1, :]
        cells = jnp.sum(mask_ref[m])
        summed = jnp.sum(total, axis=1, keepdims=True)
        mean = summed / jnp.maximum(cells, 1.0)
        spread = jnp.zeros((GROUP, width), jnp.float32)
        for i in range(height):
            off = conv_ref[m, i] - mean
            spread = spread + off * off * mask_ref[m, i : i + 1, :]
        squares = jnp.sum(spread, axis=1, keepdims=True)
        lane = lax.broadcasted_iota(jnp.int32, (GROUP, 128), 1)
        stats = jnp.where(lane == m, summed, stats)
        stats = jnp.where(lane == batches + m, squares, stats)
        return jnp.where(lane == 2 * batches + m, cells, stats)

    stat_ref[...] = lax.fori_loop(0, batches, one, jnp.zeros((GROUP, 128), jnp.float32))


def conv_forward(crop, x, cot, up, down, kernel, mask_cells):
    batches, channels, height, width = x.shape
    groups = pl.cdiv(channels, GROUP)
    natural = pl.BlockSpec((batches, GROUP, height, width), lambda g, c: (0, g, 0, 0))
    turned = lambda rows: pl.BlockSpec((batches, rows, GROUP, width), lambda g, c: (0, 0, g, 0))
    return pl.pallas_call(
        conv_body,
        grid_spec=pltpu.PrefetchScalarGridSpec(
            num_scalar_prefetch=1,
            grid=(groups,),
            in_specs=[
                natural,
                natural,
                turned(MARGIN),
                turned(MARGIN),
                pl.BlockSpec((GROUP, KW * KW), lambda g, c: (g, 0)),
                pl.BlockSpec((batches, height, width), lambda g, c: (0, 0, 0)),
            ],
            out_specs=[
                turned(height),
                turned(height + 2 * MARGIN),
                turned(height),
                pl.BlockSpec((GROUP, 128), lambda g, c: (g, 0)),
            ],
            scratch_shapes=[
                pltpu.VMEM((GROUP * height, width), jnp.float32),
                pltpu.VMEM((GROUP * height, width), jnp.float32),
                pltpu.VMEM((KW * KW, GROUP, width), jnp.float32),
            ],
        ),
        out_shape=[
            jax.ShapeDtypeStruct((batches, height, channels, width), jnp.float32),
            jax.ShapeDtypeStruct((batches, height + 2 * MARGIN, channels, width), jnp.float32),
            jax.ShapeDtypeStruct((batches, height, channels, width), jnp.bfloat16),
            jax.ShapeDtypeStruct((channels, 128), jnp.float32),
        ],
        cost_estimate=pl.CostEstimate(
            flops=2 * KW * KW * batches * channels * height * width,
            bytes_accessed=30 * batches * channels * height * width,
            transcendentals=0,
        ),
    )(crop, x, cot, up, down, kernel, mask_cells)


def chunks_of(total, size):
    return [(start, min(size, total - start)) for start in range(0, total, size)]


def nt(a, b):
    return lax.dot_general(a, b, (((1,), (1,)), ((), ())), preferred_element_type=jnp.float32)


def nn(a, b):
    return jnp.dot(a, b, preferred_element_type=jnp.float32)


def mlp_body(
    pin_ref, back_ref, et_ref, w_ref, up_ref, off_ref,
    res_ref, dn_ref, ge_out, gw_out, gu_out, go_out,
    pin, pint, back, backt, res_acc, dn_acc, ge, gw, gu, go,
):
    m = pl.program_id(0)
    last = pl.num_programs(0) - 1
    rows, channels, width = pin_ref.shape[1:]
    hidden = et_ref.shape[0]
    for r in range(rows):
        cols = slice(r * width, (r + 1) * width)
        value = pin_ref[0, r]
        pin[:, cols] = value
        pint[cols, :] = value.T
        value = back_ref[0, r]
        back[:, cols] = value
        backt[cols, :] = value.T

    @pl.when(m == 0)
    def _():
        ge[...] = jnp.zeros_like(ge)
        gw[...] = jnp.zeros_like(gw)
        gu[...] = jnp.zeros_like(gu)
        go[...] = jnp.zeros_like(go)

    go[...] += jnp.sum(backt[...].astype(jnp.float32), axis=0, keepdims=True)
    for index, (start, size) in enumerate(chunks_of(hidden, 512)):
        span = slice(start, start + size)
        et = et_ref[span, :]
        wt = w_ref[span, :]
        hid = nt(pint[...], et) + up_ref[:, span]
        dact = nt(backt[...], wt)
        square = hid * hid
        inner = GELU_A * hid * (1.0 + GELU_B * square)
        t = jnp.tanh(inner)
        half = 0.5 * (1.0 + t)
        act = (hid * half).astype(jnp.bfloat16)
        slope = half + 0.5 * hid * (1.0 - t * t) * (GELU_A * (1.0 + 3.0 * GELU_B * square))
        dhid = (slope * dact).astype(jnp.bfloat16)
        res_part = nn(act, wt)
        dn_part = nn(dhid, et)
        if index == 0:
            res_acc[...] = res_part
            dn_acc[...] = dn_part
        else:
            res_acc[...] += res_part
            dn_acc[...] += dn_part
        ge[:, span] += nn(pin[...], dhid)
        gw[:, span] += nn(back[...], act)
        gu[:, span] += jnp.sum(dhid.astype(jnp.float32), axis=0, keepdims=True)

        @pl.when(m == last)
        def _():
            ge_out[span, :] = ge[:, span].astype(jnp.bfloat16).T
            gw_out[span, :] = gw[:, span].astype(jnp.bfloat16).T

    for r in range(rows):
        cols = slice(r * width, (r + 1) * width)
        res_ref[0, r] = (res_acc[cols, :] + off_ref[...]).astype(jnp.bfloat16).T
        dn_ref[0, r] = dn_acc[cols, :].astype(jnp.bfloat16).T

    @pl.when(m == last)
    def _():
        gu_out[...] = gu[...]
        go_out[...] = go[...]


def mlp(pin, back, expand_t, shrink, uplift, offset):
    batches, rows, channels, width = pin.shape
    hidden = expand_t.shape[0]
    pixels = rows * width
    block = pl.BlockSpec((1, rows, channels, width), lambda m: (m, 0, 0, 0))
    whole = lambda shape: pl.BlockSpec(shape, lambda m: (0, 0), pipeline_mode=pl.Buffered(1))
    bf, f32 = jnp.bfloat16, jnp.float32
    return pl.pallas_call(
        mlp_body,
        grid=(batches,),
        in_specs=[
            block, block,
            whole((hidden, channels)), whole((hidden, channels)),
            whole((1, hidden)), whole((1, channels)),
        ],
        out_specs=[
            block, block,
            whole((hidden, channels)), whole((hidden, channels)),
            whole((1, hidden)), whole((1, channels)),
        ],
        out_shape=[
            jax.ShapeDtypeStruct(pin.shape, bf),
            jax.ShapeDtypeStruct(pin.shape, bf),
            jax.ShapeDtypeStruct((hidden, channels), bf),
            jax.ShapeDtypeStruct((hidden, channels), bf),
            jax.ShapeDtypeStruct((1, hidden), f32),
            jax.ShapeDtypeStruct((1, channels), f32),
        ],
        scratch_shapes=[
            pltpu.VMEM((channels, pixels), bf),
            pltpu.VMEM((pixels, channels), bf),
            pltpu.VMEM((channels, pixels), bf),
            pltpu.VMEM((pixels, channels), bf),
            pltpu.VMEM((pixels, channels), f32),
            pltpu.VMEM((pixels, channels), f32),
            pltpu.VMEM((channels, hidden), f32),
            pltpu.VMEM((channels, hidden), f32),
            pltpu.VMEM((1, hidden), f32),
            pltpu.VMEM((1, channels), f32),
        ],
        compiler_params=pltpu.CompilerParams(vmem_limit_bytes=62 * 1024 * 1024),
        cost_estimate=pl.CostEstimate(
            flops=12 * batches * pixels * channels * hidden,
            bytes_accessed=2 * 4 * channels * hidden,
            transcendentals=batches * pixels * hidden,
        ),
    )(pin, back, expand_t, shrink, uplift, offset)


def mlp_fused_body(
    normed, back_ref, et_hbm, w_hbm, up_ref, off_ref,
    res_out, dn_out, ge_out, gw_out, gu_ref, go_ref,
    land, stage, et_ref, w_ref, pin, pint, back, backt, res_acc, dn_acc, ge, gw, gstage,
    in_send, in_recv, out_send, out_recv, load_sem, own_sem, keep_sem, grad_sem,
):
    batches, height, channels, width = normed.shape
    peers = lax.axis_size("lvl")
    me = lax.axis_index("lvl")
    rows = height // peers
    hidden = et_ref.shape[0]
    last = batches - 1

    loads = [
        pltpu.make_async_copy(et_hbm, et_ref, load_sem.at[0]),
        pltpu.make_async_copy(w_hbm, w_ref, load_sem.at[1]),
    ]
    for load in loads:
        load.start()

    barrier = pltpu.get_barrier_semaphore()
    for k in range(1, peers):
        pl.semaphore_signal(
            barrier, inc=1, device_id={"lvl": lax.rem(me + k, peers)},
            device_id_type=pl.DeviceIdType.MESH,
        )
    pl.semaphore_wait(barrier, peers - 1)

    def span_of(at):
        return pl.ds(pl.multiple_of(at * channels, 8), channels)

    def in_copy(m, k):
        to = lax.rem(me + k, peers)
        return pltpu.make_async_remote_copy(
            src_ref=normed.at[m, pl.ds(to * rows, rows)],
            dst_ref=land.at[m, :, span_of(me), :],
            send_sem=in_send.at[m, k], recv_sem=in_recv.at[m, k],
            device_id={"lvl": to}, device_id_type=pl.DeviceIdType.MESH,
        )

    def own_in(m):
        return pltpu.make_async_copy(
            normed.at[m, pl.ds(me * rows, rows)], land.at[m, :, span_of(me), :], own_sem.at[m]
        )

    outs = (res_out, dn_out)

    def out_copy(m, k, which):
        to = lax.rem(me + k, peers)
        return pltpu.make_async_remote_copy(
            src_ref=stage.at[which, m, :, span_of(to), :],
            dst_ref=outs[which].at[m, pl.ds(me * rows, rows)],
            send_sem=out_send.at[which, m, k], recv_sem=out_recv.at[which, m, k],
            device_id={"lvl": to}, device_id_type=pl.DeviceIdType.MESH,
        )

    def own_out(m, which):
        return pltpu.make_async_copy(
            stage.at[which, m, :, span_of(me), :],
            outs[which].at[m, pl.ds(me * rows, rows)],
            keep_sem.at[which, m],
        )

    for m in range(batches):
        own_in(m).start()
    for k in range(1, peers):
        in_copy(0, k).start()
    ge[...] = jnp.zeros_like(ge)
    gw[...] = jnp.zeros_like(gw)
    gu_ref[...] = jnp.zeros_like(gu_ref)
    go_ref[...] = jnp.zeros_like(go_ref)
    for load in loads:
        load.wait()

    spans = chunks_of(hidden, 512)

    def grad_copies(index):
        start, size = spans[index]
        slot = index % 2
        return [
            pltpu.make_async_copy(
                gstage.at[which, slot, pl.ds(0, size), :],
                (ge_out, gw_out)[which].at[pl.ds(start, size), :],
                grad_sem.at[which, slot],
            )
            for which in range(2)
        ]

    def one(m, carry):
        own_in(m).wait()
        for k in range(1, peers):
            in_copy(m, k).wait()

        @pl.when(m == 0)
        def _():
            for other in range(1, batches):
                for k in range(1, peers):
                    in_copy(other, k).start()

        for r in range(rows):
            cols = slice(r * width, (r + 1) * width)
            value = land[m, r]
            pin[:, cols] = value
            pint[cols, :] = value.T
            value = back_ref[m, r]
            back[:, cols] = value
            backt[cols, :] = value.T
        go_ref[...] += jnp.sum(backt[...].astype(jnp.float32), axis=0, keepdims=True)
        for index, (start, size) in enumerate(spans):
            span = slice(start, start + size)
            et = et_ref[span, :]
            wt = w_ref[span, :]
            hid = nt(pint[...], et) + up_ref[:, span]
            dact = nt(backt[...], wt)
            square = hid * hid
            t = jnp.tanh(GELU_A * hid * (1.0 + GELU_B * square))
            half = 0.5 * (1.0 + t)
            act = (hid * half).astype(jnp.bfloat16)
            slope = half + 0.5 * hid * (1.0 - t * t) * (
                GELU_A * (1.0 + 3.0 * GELU_B * square)
            )
            dhid = (slope * dact).astype(jnp.bfloat16)
            res_part = nn(act, wt)
            dn_part = nn(dhid, et)
            if index == 0:
                res_acc[...] = res_part
                dn_acc[...] = dn_part
            else:
                res_acc[...] += res_part
                dn_acc[...] += dn_part
            ge[:, span] += nn(pin[...], dhid)
            gw[:, span] += nn(back[...], act)
            gu_ref[:, span] += jnp.sum(dhid.astype(jnp.float32), axis=0, keepdims=True)

            @pl.when(m == last)
            def _():
                if index >= 2:
                    for copy in grad_copies(index - 2):
                        copy.wait()
                gstage[0, index % 2, :size, :] = ge[:, span].astype(jnp.bfloat16).T
                gstage[1, index % 2, :size, :] = gw[:, span].astype(jnp.bfloat16).T
                for copy in grad_copies(index):
                    copy.start()

        for r in range(rows):
            cols = slice(r * width, (r + 1) * width)
            stage[0, m, r] = (res_acc[cols, :] + off_ref[...]).astype(jnp.bfloat16).T
            stage[1, m, r] = dn_acc[cols, :].astype(jnp.bfloat16).T
        for which in range(2):
            for k in range(1, peers):
                out_copy(m, k, which).start()
            own_out(m, which).start()
        return carry

    lax.fori_loop(0, batches, one, 0)
    for index in range(max(len(spans) - 2, 0), len(spans)):
        for copy in grad_copies(index):
            copy.wait()
    for m in range(batches):
        for which in range(2):
            own_out(m, which).wait()
            for k in range(1, peers):
                out_copy(m, k, which).wait()


def mlp_fused(normed, back, expand_t, shrink, uplift, offset, ident):
    batches, height, channels, width = normed.shape
    peers = lax.axis_size("lvl")
    rows = height // peers
    hidden, every = expand_t.shape
    pixels = rows * width
    bf, f32 = jnp.bfloat16, jnp.float32
    hbm = pl.BlockSpec(memory_space=pl.ANY)
    vmem = pl.BlockSpec(memory_space=pltpu.VMEM)
    dma = pltpu.SemaphoreType.DMA
    chunk = min(512, hidden)
    return pl.pallas_call(
        mlp_fused_body,
        in_specs=[hbm, vmem, hbm, hbm, vmem, vmem],
        out_specs=[hbm, hbm, hbm, hbm, vmem, vmem],
        out_shape=[
            jax.ShapeDtypeStruct(normed.shape, bf),
            jax.ShapeDtypeStruct(normed.shape, bf),
            jax.ShapeDtypeStruct((hidden, every), bf),
            jax.ShapeDtypeStruct((hidden, every), bf),
            jax.ShapeDtypeStruct((1, hidden), f32),
            jax.ShapeDtypeStruct((1, every), f32),
        ],
        scratch_shapes=[
            pltpu.VMEM((batches, rows, every, width), bf),
            pltpu.VMEM((2, batches, rows, every, width), bf),
            pltpu.VMEM((hidden, every), bf),
            pltpu.VMEM((hidden, every), bf),
            pltpu.VMEM((every, pixels), bf),
            pltpu.VMEM((pixels, every), bf),
            pltpu.VMEM((every, pixels), bf),
            pltpu.VMEM((pixels, every), bf),
            pltpu.VMEM((pixels, every), f32),
            pltpu.VMEM((pixels, every), f32),
            pltpu.VMEM((every, hidden), f32),
            pltpu.VMEM((every, hidden), f32),
            pltpu.VMEM((2, 2, chunk, every), bf),
            dma((batches, peers)), dma((batches, peers)),
            dma((2, batches, peers)), dma((2, batches, peers)),
            dma((2,)), dma((batches,)), dma((2, batches)), dma((2, 2)),
        ],
        compiler_params=pltpu.CompilerParams(
            vmem_limit_bytes=63 * 1024 * 1024, collective_id=ident, has_side_effects=True
        ),
        cost_estimate=pl.CostEstimate(
            flops=12 * batches * pixels * every * hidden,
            bytes_accessed=8 * every * hidden,
            transcendentals=batches * pixels * hidden,
        ),
    )(normed, back, expand_t, shrink, uplift, offset)


def sums_body(xt_ref, res_ref, dn_ref, conv_ref, mask_ref, par_ref, out_ref, stat_ref, scr):
    batches, height = res_ref.shape[:2]
    width = res_ref.shape[3]

    def one(m, stats):
        lane = lax.broadcasted_iota(jnp.int32, (GROUP, 128), 1)
        mean = jnp.sum(jnp.where(lane == m, par_ref[...], 0.0), axis=1, keepdims=True)
        rho = jnp.sum(jnp.where(lane == batches + m, par_ref[...], 0.0), axis=1, keepdims=True)
        mean = jnp.broadcast_to(mean, (GROUP, width))
        rho = jnp.broadcast_to(rho, (GROUP, width))
        plain = jnp.zeros((GROUP, width), jnp.float32)
        cross = jnp.zeros((GROUP, width), jnp.float32)
        for i in range(height):
            grad = dn_ref[m, i].astype(jnp.float32)
            plain = plain + grad
            cross = cross + grad * ((conv_ref[m, i] - mean) * rho)
            value = xt_ref[m, MARGIN + i] + res_ref[m, i].astype(jnp.float32)
            scr[pl.ds(i, GROUP, stride=height), :] = value * mask_ref[m, i : i + 1, :]
        for c in range(GROUP):
            out_ref[m, c] = scr[c * height : (c + 1) * height, :]
        stats = jnp.where(lane == m, jnp.sum(plain, axis=1, keepdims=True), stats)
        return jnp.where(lane == batches + m, jnp.sum(cross, axis=1, keepdims=True), stats)

    stat_ref[...] = lax.fori_loop(0, batches, one, jnp.zeros((GROUP, 128), jnp.float32))


def output_and_sums(xt, res, dn, conv, mask_cells, params):
    batches, height, channels, width = res.shape
    turned = lambda rows: pl.BlockSpec((batches, rows, GROUP, width), lambda g: (0, 0, g, 0))
    return pl.pallas_call(
        sums_body,
        grid=(pl.cdiv(channels, GROUP),),
        in_specs=[
            turned(height + 2 * MARGIN),
            turned(height), turned(height), turned(height),
            pl.BlockSpec((batches, height, width), lambda g: (0, 0, 0)),
            pl.BlockSpec((GROUP, 128), lambda g: (g, 0)),
        ],
        out_specs=[
            pl.BlockSpec((batches, GROUP, height, width), lambda g: (0, g, 0, 0)),
            pl.BlockSpec((GROUP, 128), lambda g: (g, 0)),
        ],
        out_shape=[
            jax.ShapeDtypeStruct((batches, channels, height, width), jnp.float32),
            jax.ShapeDtypeStruct((channels, 128), jnp.float32),
        ],
        scratch_shapes=[pltpu.VMEM((GROUP * height, width), jnp.float32)],
        cost_estimate=pl.CostEstimate(
            flops=10 * batches * channels * height * width,
            bytes_accessed=20 * batches * channels * height * width,
            transcendentals=0,
        ),
    )(xt, res, dn, conv, mask_cells, params)


def conv_back_body(
    crop, xt_ref, grad_ref, up_ref, dn_ref, cot_ref, k_ref, mask_ref,
    out_ref, kg_ref, scr, wscr, frame, sums,
):
    batches, height = grad_ref.shape[:2]
    width = grad_ref.shape[3]
    masks = lane_tap_masks(width)
    for a in range(KW):
        for b in range(KW):
            t = a * KW + b
            spread = jnp.broadcast_to(k_ref[:, t : t + 1], (GROUP, width))
            wscr[t] = jnp.where(masks[KW - 1 - b], spread, 0.0)
            sums[t] = jnp.zeros((GROUP, width), jnp.float32)

    def one(m, carry):
        for r in range(MARGIN):
            frame[r] = up_ref[m, r]
            frame[MARGIN + height + r] = dn_ref[m, r]
        for i in range(height):
            frame[MARGIN + i] = grad_ref[m, i]
        for base in range(0, height, ROWS):
            for b in range(KW):
                rolled = [
                    shifted(xt_ref[m, base + r], b - MARGIN) for r in range(ROWS + KW - 1)
                ]
                for a in range(KW):
                    part = None
                    for i in range(ROWS):
                        term = frame[MARGIN + base + i] * rolled[i + a]
                        part = term if part is None else part + term
                    sums[a * KW + b] += part
            acc = [None] * ROWS
            for b in range(KW):
                rolled = [
                    shifted(frame[base + r], MARGIN - b) for r in range(ROWS + KW - 1)
                ]
                for a in range(KW):
                    tap = wscr[a * KW + b]
                    for i in range(ROWS):
                        term = tap * rolled[i + KW - 1 - a]
                        acc[i] = term if acc[i] is None else acc[i] + term
            for i in range(ROWS):
                scr[pl.ds(base + i, GROUP, stride=height), :] = acc[i]
        row = lax.broadcasted_iota(jnp.int32, (height, width), 0)
        for c in range(GROUP):
            dres = cot_ref[m, c].astype(jnp.float32) * mask_ref[m]
            total = dres + scr[c * height : (c + 1) * height, :]
            out_ref[m, c] = jnp.where(row < crop[m, 0], total, 0.0)
        return carry

    lax.fori_loop(0, batches, one, 0)
    columns = []
    for t in range(KW * KW):
        kept = jnp.where(masks[t % KW], sums[t], 0.0)
        columns.append((t, jnp.sum(kept, axis=1, keepdims=True)))
    kg_ref[...] = put_columns(columns)


def conv_backward(crop, xt, grad_conv, up, down, cot, kernel, mask_cells):
    batches, height, channels, width = grad_conv.shape
    natural = pl.BlockSpec((batches, GROUP, height, width), lambda g, c: (0, g, 0, 0))
    turned = lambda rows: pl.BlockSpec((batches, rows, GROUP, width), lambda g, c: (0, 0, g, 0))
    return pl.pallas_call(
        conv_back_body,
        grid_spec=pltpu.PrefetchScalarGridSpec(
            num_scalar_prefetch=1,
            grid=(pl.cdiv(channels, GROUP),),
            in_specs=[
                turned(height + 2 * MARGIN),
                turned(height),
                turned(MARGIN), turned(MARGIN),
                natural,
                pl.BlockSpec((GROUP, KW * KW), lambda g, c: (g, 0)),
                pl.BlockSpec((batches, height, width), lambda g, c: (0, 0, 0)),
            ],
            out_specs=[natural, pl.BlockSpec((GROUP, 128), lambda g, c: (g, 0))],
            scratch_shapes=[
                pltpu.VMEM((GROUP * height, width), jnp.float32),
                pltpu.VMEM((KW * KW, GROUP, width), jnp.float32),
                pltpu.VMEM((height + 2 * MARGIN, GROUP, width), jnp.float32),
                pltpu.VMEM((KW * KW, GROUP, width), jnp.float32),
            ],
        ),
        out_shape=[
            jax.ShapeDtypeStruct((batches, channels, height, width), jnp.float32),
            jax.ShapeDtypeStruct((channels, 128), jnp.float32),
        ],
        cost_estimate=pl.CostEstimate(
            flops=4 * KW * KW * batches * channels * height * width,
            bytes_accessed=14 * batches * channels * height * width,
            transcendentals=0,
        ),
    )(crop, xt, grad_conv, up, down, cot, kernel, mask_cells)


def neighbours(head, tail, axis):
    count = lax.axis_size(axis)
    up = lax.ppermute(tail, axis, [(i, i + 1) for i in range(count - 1)])
    down = lax.ppermute(head, axis, [(i + 1, i) for i in range(count - 1)])
    return up, down


def on_device(
    input_field, cotangent, ocean_mask, crop_rows, step_count,
    kernel, kernel_first, kernel_second,
    scales, scales_first, scales_second,
    expand, expand_first, expand_second,
    uplift, uplift_first, uplift_second,
    shrink, shrink_first, shrink_second,
    offset, offset_first, offset_second,
):
    f32, bf = jnp.float32, jnp.bfloat16
    batches, channels, height, width = input_field.shape
    sp = lax.axis_size("sp")
    lvl = lax.axis_size("lvl")
    expand_all = lax.all_gather(expand.T.astype(bf), "sp", axis=0, tiled=True)
    shrink_all = lax.all_gather(shrink.astype(bf), "sp", axis=0, tiled=True)
    uplift_all = lax.all_gather(uplift.astype(bf), "sp", axis=0, tiled=True)
    offset_all = lax.all_gather(offset.astype(bf), "sp", axis=0, tiled=True)

    valid = (jnp.arange(height, dtype=jnp.int32)[None, :] < crop_rows).astype(f32)
    mask_cells = ocean_mask.astype(f32) * valid[:, :, None]
    valid_low = valid.astype(bf)[:, None, :, None]
    head = input_field[:, :, :MARGIN] * valid_low[:, :, :MARGIN]
    tail = input_field[:, :, height - MARGIN :] * valid_low[:, :, height - MARGIN :]
    up, down = neighbours(head.transpose(0, 2, 1, 3), tail.transpose(0, 2, 1, 3), "sp")
    conv, xt, dres, stats = conv_forward(
        crop_rows, input_field, cotangent, up, down, kernel, mask_cells
    )
    every = lax.all_gather(stats[:, : 4 * batches], "sp", axis=0)
    sums = every[:, :, :batches]
    squares = every[:, :, batches : 2 * batches]
    cells = every[:, :, 2 * batches : 3 * batches]
    count = jnp.maximum(jnp.sum(cells, axis=0), 1.0)
    mean = jnp.sum(sums, axis=0) / count
    gap = sums / jnp.maximum(cells, 1.0) - mean[None]
    variance = jnp.sum(squares + cells * gap * gap, axis=0) / count
    rho = lax.rsqrt(variance + 1e-05)

    def spread(stat):
        return stat.T[:, None, :, None]

    gain = scales[0][None, None, :, None]
    shift = scales[1][None, None, :, None]
    normed = ((conv - spread(mean)) * spread(rho) * gain + shift).astype(bf)

    def to_pixels(v):
        return lax.all_to_all(v, "lvl", split_axis=1, concat_axis=2, tiled=True)

    def to_channels(v):
        return lax.all_to_all(v, "lvl", split_axis=2, concat_axis=1, tiled=True)

    pixel_back = to_pixels(dres)
    biases = (uplift_all.astype(f32)[None], offset_all.astype(f32)[None])
    if channels % 8 == 0:
        result, grad_normed, grad_expand, grad_shrink, grad_uplift, grad_offset = mlp_fused(
            normed, pixel_back, expand_all, shrink_all, *biases, 1
        )
    else:
        result, grad_normed, grad_expand, grad_shrink, grad_uplift, grad_offset = mlp(
            to_pixels(normed), pixel_back, expand_all, shrink_all, *biases
        )
        result = to_channels(result)
        grad_normed = to_channels(grad_normed)
    params = jnp.concatenate([mean, rho], axis=1)
    params = jnp.pad(params, ((0, 0), (0, 128 - params.shape[1])))
    block_output, local = output_and_sums(xt, result, grad_normed, conv, mask_cells, params)
    both = lax.psum(local[:, : 2 * batches], "sp")
    plain, cross = both[:, :batches], both[:, batches:]
    scales_grad = jnp.stack([jnp.sum(cross, axis=1), jnp.sum(plain, axis=1)], axis=0)
    whitened = (conv - spread(mean)) * spread(rho)
    grad_conv = spread(rho) * (
        gain * grad_normed.astype(f32)
        - mask_cells[:, :, None, :] * gain * (spread(plain) + whitened * spread(cross)) / spread(count)
    )
    back_up, back_down = neighbours(
        grad_conv[:, :MARGIN], grad_conv[:, height - MARGIN :], "sp"
    )
    input_grad, kernel_cols = conv_backward(
        crop_rows, xt, grad_conv, back_up, back_down, cotangent, kernel, mask_cells
    )
    kernel_grad = lax.psum(kernel_cols[:, : KW * KW], "sp")

    def own_share(partial):
        rows = partial.shape[0] // sp
        parts = lax.all_to_all(
            partial.reshape(sp, rows, partial.shape[1]), "sp", split_axis=0, concat_axis=0
        )
        share = jnp.sum(parts.astype(f32), axis=0).astype(bf)
        return jnp.sum(lax.all_gather(share, "lvl", axis=0).astype(f32), axis=0)

    share_expand = own_share(grad_expand)
    share_shrink = own_share(grad_shrink)
    small = lax.psum(
        jnp.concatenate([grad_uplift[0], grad_offset[0]]), ("sp", "lvl")
    )
    place = lax.axis_index("sp")
    share_uplift = lax.dynamic_slice_in_dim(small, place * uplift.shape[0], uplift.shape[0])
    share_offset = lax.dynamic_slice_in_dim(
        small, uplift_all.shape[0] + place * offset.shape[0], offset.shape[0]
    )
    step_float = (step_count + 1).astype(f32)
    kernel_moment, kernel_next = adamw(
        kernel, kernel_first, kernel_second, kernel_grad, 0.15, step_float
    )
    scales_moment, scales_next = adamw(
        scales, scales_first, scales_second, scales_grad, 0.2, step_float
    )
    expand_grad = share_expand.T
    expand_moment, expand_next = adamw(
        expand, expand_first, expand_second, expand_grad, 0.035, step_float
    )
    uplift_moment, uplift_next = adamw(
        uplift, uplift_first, uplift_second, share_uplift, 0.1, step_float
    )
    shrink_moment, shrink_next = adamw(
        shrink, shrink_first, shrink_second, share_shrink, 0.018, step_float
    )
    offset_moment, offset_next = adamw(
        offset, offset_first, offset_second, share_offset, 0.1, step_float
    )
    return (
        block_output, input_grad,
        kernel_grad, kernel_moment, kernel_next,
        scales_grad, scales_moment, scales_next,
        expand_grad, expand_moment, expand_next,
        share_uplift, uplift_moment, uplift_next,
        share_shrink, shrink_moment, shrink_next,
        share_offset, offset_moment, offset_next,
        step_count + 1,
    )


def solution(mesh):
    tile = P(None, "lvl", "sp", None)
    by_channel = P("lvl", None)
    by_scale = P(None, "lvl")
    by_hidden = P(None, "sp")
    by_row = P("sp", None)
    line = P("sp")
    in_specs = (
        tile, tile, P(None, "sp", None), P(None, "sp"), P(),
        by_channel, by_channel, by_channel,
        by_scale, by_scale, by_scale,
        by_hidden, by_hidden, by_hidden,
        line, line, line,
        by_row, by_row, by_row,
        line, line, line,
    )
    out_specs = (
        tile, tile,
        by_channel, by_channel, by_channel,
        by_scale, by_scale, by_scale,
        by_hidden, by_hidden, by_hidden,
        line, line, line,
        by_row, by_row, by_row,
        line, line, line,
        P(),
    )
    return jax.shard_map(
        on_device, mesh=mesh, in_specs=in_specs, out_specs=out_specs, check_vma=False
    )
```

```python
import functools
import math

import jax
import jax.numpy as jnp
from jax import lax
from jax.experimental import pallas as pl
from jax.experimental.pallas import tpu as pltpu
from jax.sharding import PartitionSpec as P

KW = 7
MARGIN = KW // 2
GROUP = 8
CLOSE_BLOCK = 40
ROWS = 16

beta_one = 0.9
beta_two = 0.999
epsilon = 1e-08
weight_decay = 0.01
GELU_A = math.sqrt(2.0 / math.pi)
GELU_B = 0.044715


def adamw(weight, first, second, grad, rate, step_float):
    first_new = beta_one * first + (1.0 - beta_one) * grad
    second_new = beta_two * second + (1.0 - beta_two) * grad * grad
    fix_first = 1.0 - jnp.power(beta_one, step_float)
    fix_second = 1.0 - jnp.power(beta_two, step_float)
    update = (
        first_new / fix_first / (jnp.sqrt(second_new / fix_second) + epsilon)
        + weight_decay * weight
    )
    return (second_new, weight - rate * update)


def lane_tap_masks(width):
    lane = lax.broadcasted_iota(jnp.int32, (GROUP, width), 1)
    return [
        jnp.logical_and(lane + (b - MARGIN) >= 0, lane + (b - MARGIN) < width)
        for b in range(KW)
    ]


def shifted(value, amount):
    width = value.shape[-1]
    turn = (-amount) % width
    return value if turn == 0 else pltpu.roll(value, turn, 1)


def chip_neighbours(chip):
    across = chip + 1 - 2 * lax.rem(chip, 2)
    along = lax.rem(chip + 2, 4)
    return across, along, lax.rem(across + 2, 4)


def fill_taps(k_ref, taps, masks, groups):
    width = taps.shape[2]

    def fill(g, carry):
        now = pl.ds(pl.multiple_of(g * GROUP, GROUP), GROUP)
        for a in range(KW):
            for b in range(KW):
                t = a * KW + b
                tap = jnp.broadcast_to(k_ref[now, t : t + 1], (GROUP, width))
                taps[t, now, :] = jnp.where(masks[b], tap, 0.0)
        return carry

    lax.fori_loop(0, groups, fill, 0)


def depthwise_rows(source, taps, now, rows, sign):
    width = taps.shape[2]
    outs = [None] * rows
    for first in range(0, rows, 8):
        values = [source(first + r) for r in range(8 + KW - 1)]
        for b in range(KW):
            part = [None] * 8
            for a in range(KW):
                tap = taps[a * KW + b, now, :]
                at = a if sign > 0 else KW - 1 - a
                for i in range(8):
                    term = tap * values[i + at]
                    part[i] = term if part[i] is None else part[i] + term
            for i in range(8):
                moved = shifted(part[i], sign * (b - MARGIN))
                at = first + i
                outs[at] = moved if outs[at] is None else outs[at] + moved
    return outs


def put_columns(columns):
    lane = lax.broadcasted_iota(jnp.int32, (GROUP, 128), 1)
    out = jnp.zeros((GROUP, 128), jnp.float32)
    for at, column in columns:
        out = jnp.where(lane == at, column, out)
    return out


def conv_body(
    crop, x_ref, cot_ref, up_ref, dn_ref, k_ref, mask_ref,
    conv_ref, xt_ref, dres_ref, stat_ref, scr, scc, wscr,
):
    batches, _, height, width = x_ref.shape
    masks = lane_tap_masks(width)
    for a in range(KW):
        for b in range(KW):
            t = a * KW + b
            spread = jnp.broadcast_to(k_ref[:, t : t + 1], (GROUP, width))
            wscr[t] = jnp.where(masks[b], spread, 0.0)

    def one(m, stats):
        for c in range(GROUP):
            scr[c * height : (c + 1) * height, :] = x_ref[m, c].astype(jnp.float32)
            scc[c * height : (c + 1) * height, :] = cot_ref[m, c].astype(jnp.float32)
        limit = crop[m, 0]
        for i in range(height):
            row = scr[pl.ds(i, GROUP, stride=height), :]
            xt_ref[m, MARGIN + i] = jnp.where(i < limit, row, 0.0)
            back = scc[pl.ds(i, GROUP, stride=height), :]
            dres_ref[m, i] = (back * mask_ref[m, i : i + 1, :]).astype(jnp.bfloat16)
        for r in range(MARGIN):
            xt_ref[m, r] = up_ref[m, r].astype(jnp.float32)
            xt_ref[m, MARGIN + height + r] = dn_ref[m, r].astype(jnp.float32)
        total = jnp.zeros((GROUP, width), jnp.float32)
        for base in range(0, height, ROWS):
            acc = [None] * ROWS
            for b in range(KW):
                rolled = [
                    shifted(xt_ref[m, base + r], b - MARGIN) for r in range(ROWS + KW - 1)
                ]
                for a in range(KW):
                    tap = wscr[a * KW + b]
                    for i in range(ROWS):
                        term = tap * rolled[i + a]
                        acc[i] = term if acc[i] is None else acc[i] + term
            for i in range(ROWS):
                conv_ref[m, base + i] = acc[i]
                total = total + acc[i] * mask_ref[m, base + i : base + i + 1, :]
        cells = jnp.sum(mask_ref[m])
        summed = jnp.sum(total, axis=1, keepdims=True)
        mean = summed / jnp.maximum(cells, 1.0)
        spread = jnp.zeros((GROUP, width), jnp.float32)
        for i in range(height):
            off = conv_ref[m, i] - mean
            spread = spread + off * off * mask_ref[m, i : i + 1, :]
        squares = jnp.sum(spread, axis=1, keepdims=True)
        lane = lax.broadcasted_iota(jnp.int32, (GROUP, 128), 1)
        stats = jnp.where(lane == m, summed, stats)
        stats = jnp.where(lane == batches + m, squares, stats)
        return jnp.where(lane == 2 * batches + m, cells, stats)

    stat_ref[...] = lax.fori_loop(0, batches, one, jnp.zeros((GROUP, 128), jnp.float32))


def conv_forward(crop, x, cot, up, down, kernel, mask_cells):
    batches, channels, height, width = x.shape
    groups = pl.cdiv(channels, GROUP)
    natural = pl.BlockSpec((batches, GROUP, height, width), lambda g, c: (0, g, 0, 0))
    turned = lambda rows: pl.BlockSpec((batches, rows, GROUP, width), lambda g, c: (0, 0, g, 0))
    return pl.pallas_call(
        conv_body,
        grid_spec=pltpu.PrefetchScalarGridSpec(
            num_scalar_prefetch=1,
            grid=(groups,),
            in_specs=[
                natural,
                natural,
                turned(MARGIN),
                turned(MARGIN),
                pl.BlockSpec((GROUP, KW * KW), lambda g, c: (g, 0)),
                pl.BlockSpec((batches, height, width), lambda g, c: (0, 0, 0)),
            ],
            out_specs=[
                turned(height),
                turned(height + 2 * MARGIN),
                turned(height),
                pl.BlockSpec((GROUP, 128), lambda g, c: (g, 0)),
            ],
            scratch_shapes=[
                pltpu.VMEM((GROUP * height, width), jnp.float32),
                pltpu.VMEM((GROUP * height, width), jnp.float32),
                pltpu.VMEM((KW * KW, GROUP, width), jnp.float32),
            ],
        ),
        out_shape=[
            jax.ShapeDtypeStruct((batches, height, channels, width), jnp.float32),
            jax.ShapeDtypeStruct((batches, height + 2 * MARGIN, channels, width), jnp.float32),
            jax.ShapeDtypeStruct((batches, height, channels, width), jnp.bfloat16),
            jax.ShapeDtypeStruct((channels, 128), jnp.float32),
        ],
        cost_estimate=pl.CostEstimate(
            flops=2 * KW * KW * batches * channels * height * width,
            bytes_accessed=30 * batches * channels * height * width,
            transcendentals=0,
        ),
    )(crop, x, cot, up, down, kernel, mask_cells)


def forward_body(
    crop, x_hbm, cot_hbm, ocean_ref, kt_ref, scale_ref, et_hbm, w_hbm, up_own, off_own,
    conv_hbm, xt_hbm, norm_hbm, back_hbm, et_all, w_all, par_ref, mask_ref, bias_ref, turned_k,
    xv, cotv, xt, conv, dres, norm, edge, rim, cast, scr, scc, taps, part, stat, msg, srecv, scal, bias, kpad, et_own, w_own,
    load_sem, save_sem, own_sem, pair_send, pair_recv, chip_send, chip_recv,
    b_send, b_recv, s_send, s_recv, h_send, h_recv, d_send, d_recv, d_own,
):
    f32, bf = jnp.float32, jnp.bfloat16
    batches, height, channels, width = conv.shape
    groups = channels // GROUP
    peers, place = lax.axis_size("lvl"), lax.axis_index("lvl")
    spots, spot = lax.axis_size("sp"), lax.axis_index("sp")
    chips = spots // 2
    chip, core = spot // 2, lax.rem(spot, 2)
    sibling = spot + 1 - 2 * core
    rows = height // peers
    mesh_id = pl.DeviceIdType.MESH
    near = chip_neighbours(chip)[:2]

    loads = [
        pltpu.make_async_copy(cot_hbm, cotv, load_sem.at[0]),
        pltpu.make_async_copy(x_hbm, xv, load_sem.at[1]),
    ]
    loads[0].start()
    loads[1].start()

    def own_load(which):
        return pltpu.make_async_copy(
            (et_hbm, w_hbm)[which], (et_own, w_own)[which], load_sem.at[2 + which]
        )

    for which in range(2):
        own_load(which).start()
    barrier = pltpu.get_barrier_semaphore()
    for k in range(1, peers):
        pl.semaphore_signal(
            barrier, inc=1, device_id={"lvl": lax.rem(place + k, peers)}, device_id_type=mesh_id
        )
    for k in range(1, spots):
        pl.semaphore_signal(
            barrier, inc=1, device_id={"sp": lax.rem(spot + k, spots)}, device_id_type=mesh_id
        )

    gathered = (et_all, w_all)

    def own_copy(which):
        return pltpu.make_async_copy(cast.at[which], gathered[which].at[spot], own_sem.at[which])

    def pair_copy(which):
        return pltpu.make_async_remote_copy(
            src_ref=cast.at[which], dst_ref=gathered[which].at[spot],
            send_sem=pair_send.at[which], recv_sem=pair_recv.at[which],
            device_id={"sp": sibling}, device_id_type=mesh_id,
        )

    def chip_copy(which, k):
        to = 2 * near[k] + core
        return pltpu.make_async_remote_copy(
            src_ref=cast.at[which], dst_ref=gathered[which].at[spot],
            send_sem=chip_send.at[which, k], recv_sem=chip_recv.at[which, k],
            device_id={"sp": to}, device_id_type=mesh_id,
        )

    def bias_copy(k):
        return pltpu.make_async_remote_copy(
            src_ref=bias, dst_ref=bias_ref.at[spot],
            send_sem=b_send.at[k], recv_sem=b_recv.at[k],
            device_id={"sp": lax.rem(spot + k, spots)}, device_id_type=mesh_id,
        )

    def stat_copy(k):
        return pltpu.make_async_remote_copy(
            src_ref=msg, dst_ref=srecv.at[k], send_sem=s_send.at[k], recv_sem=s_recv.at[k],
            device_id={"sp": lax.rem(spot + k, spots)}, device_id_type=mesh_id,
        )

    def to_next():
        return pltpu.make_async_remote_copy(
            src_ref=edge.at[1], dst_ref=rim.at[0], send_sem=h_send.at[0], recv_sem=h_recv.at[0],
            device_id={"sp": lax.rem(spot + 1, spots)}, device_id_type=mesh_id,
        )

    def to_prev():
        return pltpu.make_async_remote_copy(
            src_ref=edge.at[0], dst_ref=rim.at[1], send_sem=h_send.at[1], recv_sem=h_recv.at[1],
            device_id={"sp": lax.rem(spot + spots - 1, spots)}, device_id_type=mesh_id,
        )

    span = pl.ds(pl.multiple_of(place * channels, 8), channels)

    def dres_copy(k):
        to = lax.rem(place + k, peers)
        return pltpu.make_async_remote_copy(
            src_ref=dres.at[:, pl.ds(to * rows, rows)], dst_ref=back_hbm.at[:, :, span, :],
            send_sem=d_send.at[k], recv_sem=d_recv.at[k],
            device_id={"lvl": to}, device_id_type=mesh_id,
        )

    def dres_own():
        return pltpu.make_async_copy(
            dres.at[:, pl.ds(place * rows, rows)], back_hbm.at[:, :, span, :], d_own.at[0]
        )

    row = lax.broadcasted_iota(jnp.int32, (height, width), 0)
    for m in range(batches):
        keep = (row < crop[m]).astype(f32)
        mask_ref[m] = ocean_ref[m].astype(f32) * keep

    def turn_cot(g, carry):
        c0 = pl.multiple_of(g * GROUP, GROUP)
        now = pl.ds(c0, GROUP)
        for m in range(batches):
            for c in range(GROUP):
                scc[m, c * height : (c + 1) * height, :] = cotv[m, c0 + c].astype(f32) * mask_ref[m]
            for i in range(height):
                dres[m, i, now, :] = scc[m, pl.ds(i, GROUP, stride=height), :].astype(bf)
        return carry

    def turn_x(g, carry):
        c0 = pl.multiple_of(g * GROUP, GROUP)
        now = pl.ds(c0, GROUP)
        for m in range(batches):
            keep = (row < crop[m]).astype(f32)
            for c in range(GROUP):
                scr[m, c * height : (c + 1) * height, :] = xv[m, c0 + c].astype(f32) * keep
            for i in range(height):
                value = scr[m, pl.ds(i, GROUP, stride=height), :]
                xt[m, MARGIN + i, now, :] = value
                if i < MARGIN:
                    edge[0, m, i, now, :] = value.astype(bf)
                if i >= height - MARGIN:
                    edge[1, m, i - (height - MARGIN), now, :] = value.astype(bf)
        return carry

    loads[0].wait()
    lax.fori_loop(0, groups, turn_cot, 0)
    pl.semaphore_wait(barrier, peers - 1 + spots - 1)
    for k in range(1, peers):
        dres_copy(k).start()
    dres_own().start()
    loads[1].wait()
    lax.fori_loop(0, groups, turn_x, 0)

    @pl.when(spot < spots - 1)
    def _():
        to_next().start()

    @pl.when(spot > 0)
    def _():
        to_prev().start()

    for which in range(2):
        own_load(which).wait()
    cast[0] = et_own[...].astype(bf)
    cast[1] = w_own[...].astype(bf)
    bias[...] = jnp.zeros_like(bias)
    bias[0:1, : up_own.shape[1]] = up_own[...].astype(bf).astype(f32)
    bias[1:2, : off_own.shape[1]] = off_own[...].astype(bf).astype(f32)
    stat[...] = jnp.zeros_like(stat)
    kpad[...] = jnp.zeros_like(kpad)
    kpad[: KW * KW, :channels] = kt_ref[...]
    turned_k[...] = kpad[...].T
    scal[...] = jnp.zeros_like(scal)
    scal[0:2, :channels] = scale_ref[...]
    bias_ref[spot] = bias[...]
    for k in range(2):
        chip_copy(k, k).start()
    for k in range(2):
        chip_copy(1 - k, k).start()
    for which in range(2):
        pair_copy(which).start()
        own_copy(which).start()
    for k in range(1, spots):
        bias_copy(k).start()
    masks = lane_tap_masks(width)
    fill_taps(turned_k, taps, masks[::-1], groups)

    @pl.when(spot < spots - 1)
    def _():
        to_next().wait_send()
        to_prev().wait_recv()
        xt[:, MARGIN + height :] = rim[1].astype(f32)

    @pl.when(spot > 0)
    def _():
        to_prev().wait_send()
        to_next().wait_recv()
        xt[:, :MARGIN] = rim[0].astype(f32)

    @pl.when(spot == 0)
    def _():
        xt[:, :MARGIN] = jnp.zeros((batches, MARGIN, channels, width), f32)

    @pl.when(spot == spots - 1)
    def _():
        xt[:, MARGIN + height :] = jnp.zeros((batches, MARGIN, channels, width), f32)

    save_x = pltpu.make_async_copy(xt, xt_hbm, save_sem.at[0])
    save_x.start()

    def convolve(g, carry):
        now = pl.ds(pl.multiple_of(g * GROUP, GROUP), GROUP)

        def one(m, inner):
            for base in range(0, height, ROWS):
                outs = depthwise_rows(
                    lambda r: xt[m, base + r, now, :], taps, now, ROWS, 1
                )
                total = None
                for i in range(ROWS):
                    conv[m, base + i, now, :] = outs[i]
                    value = outs[i] * mask_ref[m, base + i : base + i + 1, :]
                    total = value if total is None else total + value
                if base == 0:
                    part[m, now, :] = total
                else:
                    part[m, now, :] += total
            return inner

        lax.fori_loop(0, batches, one, 0)
        return carry

    lax.fori_loop(0, groups, convolve, 0)
    cells = [jnp.sum(mask_ref[m]) for m in range(batches)]
    lane = lax.broadcasted_iota(jnp.int32, (channels, 128), 1)
    tile = jnp.zeros((channels, 128), f32)
    for m in range(batches):
        summed = jnp.sum(part[m], axis=1, keepdims=True)
        tile = jnp.where(lane == m, summed, tile)
        tile = jnp.where(lane == 16 + m, cells[m], tile)
        part[m] = jnp.broadcast_to(summed / jnp.maximum(cells[m], 1.0), (channels, width))

    def scatter(g, carry):
        now = pl.ds(pl.multiple_of(g * GROUP, GROUP), GROUP)
        for m in range(batches):
            mean = part[m, now, :]
            around = None
            for i in range(height):
                off = conv[m, i, now, :] - mean
                value = off * off * mask_ref[m, i : i + 1, :]
                around = value if around is None else around + value
            part[m, now, :] = around
        return carry

    lax.fori_loop(0, groups, scatter, 0)
    for m in range(batches):
        tile = jnp.where(lane == 8 + m, jnp.sum(part[m], axis=1, keepdims=True), tile)
    stat[:channels, :] = tile
    save_conv = pltpu.make_async_copy(conv, conv_hbm, save_sem.at[1])
    save_conv.start()
    msg[...] = stat[...].T[:24, :]
    srecv[0] = msg[...]
    for k in range(1, spots):
        stat_copy(k).start()
    for k in range(1, spots):
        stat_copy(k).wait()
    order = [lax.rem(spot - source + spots, spots) for source in range(spots)]
    summed, count = None, None
    for k in order:
        value, cell = srecv[k, 0:8, :], srecv[k, 16:24, :]
        summed = value if summed is None else summed + value
        count = cell if count is None else count + cell
    count = jnp.maximum(count, 1.0)
    mean = summed / count
    squares = None
    for k in order:
        cell = srecv[k, 16:24, :]
        gap = srecv[k, 0:8, :] / jnp.maximum(cell, 1.0) - mean
        value = srecv[k, 8:16, :] + cell * gap * gap
        squares = value if squares is None else squares + value
    rho = lax.rsqrt(squares / count + 1e-05)
    filler = jnp.zeros((128 - 32, mean.shape[1]), f32)
    par_ref[...] = jnp.concatenate([mean, rho, 1.0 / count, scal[...], filler], axis=0).T

    def normalize(g, carry):
        now = pl.ds(pl.multiple_of(g * GROUP, GROUP), GROUP)
        par = par_ref[now, :]
        gain = jnp.broadcast_to(par[:, 24:25], (GROUP, width))
        shift = jnp.broadcast_to(par[:, 25:26], (GROUP, width))
        for m in range(batches):
            mean = jnp.broadcast_to(par[:, m : m + 1], (GROUP, width))
            rho = jnp.broadcast_to(par[:, 8 + m : 9 + m], (GROUP, width))
            scale = rho * gain
            for i in range(height):
                value = (conv[m, i, now, :] - mean) * scale + shift
                norm[m, i, now, :] = value.astype(bf)
        return carry

    lax.fori_loop(0, groups, normalize, 0)
    save_norm = pltpu.make_async_copy(norm, norm_hbm, save_sem.at[2])
    save_norm.start()
    for k in range(1, spots):
        pltpu.make_async_remote_copy(
            src_ref=bias, dst_ref=bias_ref.at[lax.rem(spot + spots - k, spots)],
            send_sem=b_send.at[k], recv_sem=b_recv.at[k],
            device_id={"sp": lax.rem(spot + k, spots)}, device_id_type=mesh_id,
        ).wait()
    for which in range(2):
        own_copy(which).wait()
        pltpu.make_async_remote_copy(
            src_ref=cast.at[which], dst_ref=gathered[which].at[sibling],
            send_sem=pair_send.at[which], recv_sem=pair_recv.at[which],
            device_id={"sp": sibling}, device_id_type=mesh_id,
        ).wait()
        for k in range(2):
            other = 2 * near[k] + core
            pltpu.make_async_remote_copy(
                src_ref=cast.at[which], dst_ref=gathered[which].at[other],
                send_sem=chip_send.at[which, k], recv_sem=chip_recv.at[which, k],
                device_id={"sp": other}, device_id_type=mesh_id,
            ).wait()
    dres_own().wait()
    for k in range(1, peers):
        source = pl.ds(pl.multiple_of(lax.rem(place + peers - k, peers) * channels, 8), channels)
        pltpu.make_async_remote_copy(
            src_ref=dres.at[:, pl.ds(lax.rem(place + k, peers) * rows, rows)],
            dst_ref=back_hbm.at[:, :, source, :],
            send_sem=d_send.at[k], recv_sem=d_recv.at[k],
            device_id={"lvl": lax.rem(place + k, peers)}, device_id_type=mesh_id,
        ).wait()
    save_x.wait()
    save_conv.wait()
    save_norm.wait()


def forward(crop, x, cot, ocean, kernel, scales, expand_t, shrink, uplift, offset, ident):
    batches, channels, height, width = x.shape
    f32, bf = jnp.float32, jnp.bfloat16
    peers, spots = lax.axis_size("lvl"), lax.axis_size("sp")
    chips = spots // 2
    rows = height // peers
    owned, every = expand_t.shape
    padded = -(-channels // 128) * 128
    lanes = -(-max(owned, offset.shape[1]) // 128) * 128
    hbm = pl.BlockSpec(memory_space=pl.ANY)
    vmem = pl.BlockSpec(memory_space=pltpu.VMEM)
    dma = pltpu.SemaphoreType.DMA
    turned = (batches, height, channels, width)
    framed = (batches, height + 2 * MARGIN, channels, width)
    rim = (2, batches, MARGIN, channels, width)
    V, S = pltpu.VMEM, jax.ShapeDtypeStruct
    return pl.pallas_call(
        forward_body,
        in_specs=[pl.BlockSpec(memory_space=pltpu.SMEM), hbm, hbm, vmem, vmem, vmem, hbm, hbm, vmem, vmem],
        out_specs=[hbm] * 6 + [vmem] * 4,
        out_shape=[
            S(turned, f32), S(framed, f32), S(turned, bf),
            S((batches, rows, every, width), bf),
            S((spots, owned, every), bf), S((spots, owned, every), bf),
            S((padded, 128), f32), S((batches, height, width), f32), S((spots, 8, lanes), f32),
            S((padded, 128), f32),
        ],
        scratch_shapes=[
            V(x.shape, bf), V(x.shape, bf), V(framed, f32), V(turned, f32), V(turned, bf),
            V(turned, bf), V(rim, bf), V(rim, bf), V((2, owned, every), bf),
            V((batches, GROUP * height, width), f32), V((batches, GROUP * height, width), f32),
            V((KW * KW, channels, width), f32), V((batches, channels, width), f32),
            V((padded, 128), f32), V((24, padded), f32), V((spots, 24, padded), f32),
            V((8, padded), f32), V((8, lanes), f32), V((128, padded), f32),
            V((owned, every), f32), V((owned, every), f32),
            dma((4,)), dma((3,)), dma((2,)), dma((2,)), dma((2,)),
            dma((2, 2)), dma((2, 2)),
            dma((spots,)), dma((spots,)), dma((spots,)), dma((spots,)),
            dma((2,)), dma((2,)), dma((peers,)), dma((peers,)), dma((1,)),
        ],
        compiler_params=pltpu.CompilerParams(
            vmem_limit_bytes=60 * 1024 * 1024, collective_id=ident, has_side_effects=True
        ),
        cost_estimate=pl.CostEstimate(
            flops=2 * KW * KW * batches * channels * height * width,
            bytes_accessed=30 * batches * channels * height * width,
            transcendentals=0,
        ),
    )(crop, x, cot, ocean, kernel, scales, expand_t, shrink, uplift, offset)


def chunks_of(total, size):
    return [(start, min(size, total - start)) for start in range(0, total, size)]


def nt(a, b):
    return lax.dot_general(a, b, (((1,), (1,)), ((), ())), preferred_element_type=jnp.float32)


def nn(a, b):
    return jnp.dot(a, b, preferred_element_type=jnp.float32)


def mlp_body(
    pin_ref, back_ref, et_ref, w_ref, up_ref, off_ref,
    res_ref, dn_ref, ge_out, gw_out, gu_out, go_out,
    pin, pint, back, backt, res_acc, dn_acc, ge, gw, gu, go,
):
    m = pl.program_id(0)
    last = pl.num_programs(0) - 1
    rows, channels, width = pin_ref.shape[1:]
    hidden = et_ref.shape[0]
    for r in range(rows):
        cols = slice(r * width, (r + 1) * width)
        value = pin_ref[0, r]
        pin[:, cols] = value
        pint[cols, :] = value.T
        value = back_ref[0, r]
        back[:, cols] = value
        backt[cols, :] = value.T

    @pl.when(m == 0)
    def _():
        ge[...] = jnp.zeros_like(ge)
        gw[...] = jnp.zeros_like(gw)
        gu[...] = jnp.zeros_like(gu)
        go[...] = jnp.zeros_like(go)

    go[...] += jnp.sum(backt[...].astype(jnp.float32), axis=0, keepdims=True)
    for index, (start, size) in enumerate(chunks_of(hidden, 512)):
        span = slice(start, start + size)
        et = et_ref[span, :]
        wt = w_ref[span, :]
        hid = nt(pint[...], et) + up_ref[:, span]
        dact = nt(backt[...], wt)
        square = hid * hid
        inner = GELU_A * hid * (1.0 + GELU_B * square)
        t = jnp.tanh(inner)
        half = 0.5 * (1.0 + t)
        act = (hid * half).astype(jnp.bfloat16)
        slope = half + 0.5 * hid * (1.0 - t * t) * (GELU_A * (1.0 + 3.0 * GELU_B * square))
        dhid = (slope * dact).astype(jnp.bfloat16)
        res_part = nn(act, wt)
        dn_part = nn(dhid, et)
        if index == 0:
            res_acc[...] = res_part
            dn_acc[...] = dn_part
        else:
            res_acc[...] += res_part
            dn_acc[...] += dn_part
        ge[:, span] += nn(pin[...], dhid)
        gw[:, span] += nn(back[...], act)
        gu[:, span] += jnp.sum(dhid.astype(jnp.float32), axis=0, keepdims=True)

        @pl.when(m == last)
        def _():
            ge_out[span, :] = ge[:, span].astype(jnp.bfloat16).T
            gw_out[span, :] = gw[:, span].astype(jnp.bfloat16).T

    for r in range(rows):
        cols = slice(r * width, (r + 1) * width)
        res_ref[0, r] = (res_acc[cols, :] + off_ref[...]).astype(jnp.bfloat16).T
        dn_ref[0, r] = dn_acc[cols, :].astype(jnp.bfloat16).T

    @pl.when(m == last)
    def _():
        gu_out[...] = gu[...]
        go_out[...] = go[...]


def mlp(pin, back, expand_t, shrink, uplift, offset):
    batches, rows, channels, width = pin.shape
    hidden = expand_t.shape[0]
    pixels = rows * width
    block = pl.BlockSpec((1, rows, channels, width), lambda m: (m, 0, 0, 0))
    whole = lambda shape: pl.BlockSpec(shape, lambda m: (0, 0), pipeline_mode=pl.Buffered(1))
    bf, f32 = jnp.bfloat16, jnp.float32
    return pl.pallas_call(
        mlp_body,
        grid=(batches,),
        in_specs=[
            block, block,
            whole((hidden, channels)), whole((hidden, channels)),
            whole((1, hidden)), whole((1, channels)),
        ],
        out_specs=[
            block, block,
            whole((hidden, channels)), whole((hidden, channels)),
            whole((1, hidden)), whole((1, channels)),
        ],
        out_shape=[
            jax.ShapeDtypeStruct(pin.shape, bf),
            jax.ShapeDtypeStruct(pin.shape, bf),
            jax.ShapeDtypeStruct((hidden, channels), bf),
            jax.ShapeDtypeStruct((hidden, channels), bf),
            jax.ShapeDtypeStruct((1, hidden), f32),
            jax.ShapeDtypeStruct((1, channels), f32),
        ],
        scratch_shapes=[
            pltpu.VMEM((channels, pixels), bf),
            pltpu.VMEM((pixels, channels), bf),
            pltpu.VMEM((channels, pixels), bf),
            pltpu.VMEM((pixels, channels), bf),
            pltpu.VMEM((pixels, channels), f32),
            pltpu.VMEM((pixels, channels), f32),
            pltpu.VMEM((channels, hidden), f32),
            pltpu.VMEM((channels, hidden), f32),
            pltpu.VMEM((1, hidden), f32),
            pltpu.VMEM((1, channels), f32),
        ],
        compiler_params=pltpu.CompilerParams(vmem_limit_bytes=62 * 1024 * 1024),
        cost_estimate=pl.CostEstimate(
            flops=12 * batches * pixels * channels * hidden,
            bytes_accessed=2 * 4 * channels * hidden,
            transcendentals=batches * pixels * hidden,
        ),
    )(pin, back, expand_t, shrink, uplift, offset)


def mlp_fused_body(
    normed, back_hbm, et_hbm, w_hbm, bias_ref,
    res_out, dn_out, share_ref, low_ref, small_ref, pair_in, first_in, second_in,
    up_ref, off_ref, gu_ref, go_ref, line, land, land_back, stage, et_ref, w_ref,
    pin, pint, back, backt, res_acc, dn_acc, act_all, dhid_all,
    in_send, in_recv, out_send, out_recv, load_sem, own_sem, keep_sem,
    pair_send, pair_recv, first_send, first_recv, second_send, second_recv, fetch_sem,
    pass_send, pass_recv, relay_send, relay_recv,
):
    f32, bf = jnp.float32, jnp.bfloat16
    batches, height, channels, width = normed.shape
    peers = lax.axis_size("lvl")
    me = lax.axis_index("lvl")
    rows = height // peers
    pixels = rows * width
    hidden = et_ref.shape[0]
    spots = lax.axis_size("sp")
    spot = lax.axis_index("sp")
    chips = spots // 2
    chip, core = spot // 2, lax.rem(spot, 2)
    owned = hidden // spots
    across, along, diagonal = chip_neighbours(chip)
    near = (across, along)
    sibling = spot + 1 - 2 * core
    mine = (2 * across + core, 2 * along + core, 2 * diagonal + core)
    others = (2 * across + 1 - core, 2 * along + 1 - core, 2 * diagonal + 1 - core)
    mesh_id = pl.DeviceIdType.MESH
    weights = ((et_hbm, et_ref), (w_hbm, w_ref))

    def owner_rows(owner):
        return pl.ds(pl.multiple_of(owner * owned, 16), owned)

    def weight_load(which, k):
        owner = (mine[0], mine[1], spot, sibling)[k]
        return pltpu.make_async_copy(
            weights[which][0].at[owner], weights[which][1].at[owner_rows(owner), :],
            load_sem.at[which, k],
        )

    def weight_pass(which, k, owner):
        rows_now = owner_rows(owner)
        source = weights[which][1].at[rows_now, :] if k == 2 else weights[which][0].at[owner]
        return pltpu.make_async_remote_copy(
            src_ref=source, dst_ref=weights[which][1].at[rows_now, :],
            send_sem=pass_send.at[which, k], recv_sem=pass_recv.at[which, k],
            device_id={"sp": sibling}, device_id_type=mesh_id,
        )

    def relay(which, owner):
        return pltpu.make_async_remote_copy(
            src_ref=weights[which][0].at[owner], dst_ref=weights[which][1].at[owner_rows(owner), :],
            send_sem=relay_send.at[which], recv_sem=relay_recv.at[which],
            device_id={"sp": mine[which]}, device_id_type=mesh_id,
        )

    load_back = pltpu.make_async_copy(back_hbm, land_back, own_sem.at[batches])
    load_back.start()
    for which in range(2):
        for k in range(4):
            weight_load(which, k).start()

    barrier = pltpu.get_barrier_semaphore()
    for k in range(1, peers):
        pl.semaphore_signal(
            barrier, inc=1, device_id={"lvl": lax.rem(me + k, peers)}, device_id_type=mesh_id
        )
    pl.semaphore_signal(barrier, inc=1, device_id={"sp": sibling}, device_id_type=mesh_id)
    for k in range(3):
        pl.semaphore_signal(barrier, inc=1, device_id={"sp": mine[k]}, device_id_type=mesh_id)
    pl.semaphore_wait(barrier, peers - 1 + 4)

    def span_of(at):
        return pl.ds(pl.multiple_of(at * channels, 8), channels)

    def in_copy(m, k):
        to = lax.rem(me + k, peers)
        return pltpu.make_async_remote_copy(
            src_ref=normed.at[m, pl.ds(to * rows, rows)],
            dst_ref=land.at[m, :, span_of(me), :],
            send_sem=in_send.at[m, k], recv_sem=in_recv.at[m, k],
            device_id={"lvl": to}, device_id_type=mesh_id,
        )

    def own_in(m):
        return pltpu.make_async_copy(
            normed.at[m, pl.ds(me * rows, rows)], land.at[m, :, span_of(me), :], own_sem.at[m]
        )

    outs = (res_out, dn_out)

    def out_copy(m, k, which):
        to = lax.rem(me + k, peers)
        return pltpu.make_async_remote_copy(
            src_ref=stage.at[which, m, :, span_of(to), :],
            dst_ref=outs[which].at[m, pl.ds(me * rows, rows)],
            send_sem=out_send.at[which, m, k], recv_sem=out_recv.at[which, m, k],
            device_id={"lvl": to}, device_id_type=mesh_id,
        )

    def own_out(m, which):
        return pltpu.make_async_copy(
            stage.at[which, m, :, span_of(me), :],
            outs[which].at[m, pl.ds(me * rows, rows)],
            keep_sem.at[which, m],
        )

    for m in range(batches):
        own_in(m).start()
    for k in range(1, peers):
        in_copy(0, k).start()
    for which in range(2):
        relay(which, mine[1 - which]).start()
        for k in range(2):
            weight_pass(which, k, mine[k]).start()
    for s in range(spots):
        row = bias_ref[s]
        up_ref[:, s * owned : (s + 1) * owned] = row[0:1, :owned]
        each = off_ref.shape[1] // spots
        off_ref[:, s * each : (s + 1) * each] = row[1:2, :each]
    gu_ref[...] = jnp.zeros_like(gu_ref)
    go_ref[...] = jnp.zeros_like(go_ref)
    load_back.wait()
    for which in range(2):
        relay(which, mine[1 - which]).wait_send()
        relay(which, mine[2]).wait_recv()
        weight_pass(which, 2, mine[2]).start()
    for which in range(2):
        for k in range(4):
            weight_load(which, k).wait()
        for k in range(2):
            weight_pass(which, k, mine[k]).wait_send()
            weight_pass(which, k, others[k]).wait_recv()
    for which in range(2):
        weight_pass(which, 2, mine[2]).wait_send()
        weight_pass(which, 2, others[2]).wait_recv()

    spans = chunks_of(hidden, 512)

    def one(m, carry):
        own_in(m).wait()
        for k in range(1, peers):
            in_copy(m, k).wait()

        @pl.when(m == 0)
        def _():
            for other in range(1, batches):
                for k in range(1, peers):
                    in_copy(other, k).start()

        mine_now = pl.ds(pl.multiple_of(m * pixels, 128), pixels)
        for r in range(rows):
            here = slice(r * width, (r + 1) * width)
            cols = pl.ds(pl.multiple_of(m * pixels + r * width, 128), width)
            value = land[m, r]
            pin[:, cols] = value
            pint[here, :] = value.T
            value = land_back[m, r]
            back[:, cols] = value
            backt[here, :] = value.T
        go_ref[...] += jnp.sum(backt[...].astype(f32), axis=0, keepdims=True)
        for index, (start, size) in enumerate(spans):
            span = slice(start, start + size)
            et = et_ref[span, :]
            wt = w_ref[span, :]
            hid = nt(pint[...], et) + up_ref[:, span]
            dact = nt(backt[...], wt)
            square = hid * hid
            half = 0.5 + 0.5 * jnp.tanh(hid * (GELU_A + (GELU_A * GELU_B) * square))
            full = hid * half
            act = full.astype(bf)
            slope = half + full * (1.0 - half) * (
                2.0 * GELU_A + (6.0 * GELU_A * GELU_B) * square
            )
            dhid = (slope * dact).astype(bf)
            act_all[mine_now, span] = act
            dhid_all[mine_now, span] = dhid
            res_part = nn(act, wt)
            dn_part = nn(dhid, et)
            if index == 0:
                res_acc[...] = res_part
                dn_acc[...] = dn_part
            else:
                res_acc[...] += res_part
                dn_acc[...] += dn_part
            gu_ref[:, span] += jnp.sum(dhid.astype(f32), axis=0, keepdims=True)

        for r in range(rows):
            here = slice(r * width, (r + 1) * width)
            stage[0, m, r] = (res_acc[here, :] + off_ref[...]).astype(bf).T
            stage[1, m, r] = dn_acc[here, :].astype(bf).T
        for which in range(2):
            for k in range(1, peers):
                out_copy(m, k, which).start()
            own_out(m, which).start()
        return carry

    lax.fori_loop(0, batches, one, 0)

    grads = (et_ref, w_ref)

    def pair_copy(which, q):
        return pltpu.make_async_remote_copy(
            src_ref=grads[which].at[owner_rows(2 * q + 1 - core), :],
            dst_ref=pair_in.at[which, q],
            send_sem=pair_send.at[which, q], recv_sem=pair_recv.at[which, q],
            device_id={"sp": sibling}, device_id_type=mesh_id,
        )

    def spare(which, q):
        return grads[which].at[owner_rows(2 * q + 1 - core), :]

    def fetch(which, source, q, slot):
        return pltpu.make_async_copy(source, spare(which, q), fetch_sem.at[which, slot])

    def first_copy(which, slot):
        owner = (2 * diagonal + core, 2 * near[which] + core)[slot]
        return pltpu.make_async_remote_copy(
            src_ref=grads[which].at[owner_rows(owner), :], dst_ref=first_in.at[which, slot],
            send_sem=first_send.at[which, slot], recv_sem=first_recv.at[which, slot],
            device_id={"sp": 2 * near[which] + core}, device_id_type=mesh_id,
        )

    def second_copy(which):
        owner = 2 * near[1 - which] + core
        return pltpu.make_async_remote_copy(
            src_ref=grads[which].at[owner_rows(owner), :], dst_ref=second_in.at[which],
            send_sem=second_send.at[which], recv_sem=second_recv.at[which],
            device_id={"sp": owner}, device_id_type=mesh_id,
        )

    strip = 16

    def add_rows(which, to, source):
        def add(i, carry):
            at = pl.ds(pl.multiple_of(to * owned + i * strip, 16), strip)
            more = pl.ds(pl.multiple_of(source * owned + i * strip, 16), strip)
            total = grads[which][at, :].astype(f32) + grads[which][more, :].astype(f32)
            grads[which][at, :] = total.astype(bf)
            return carry

        lax.fori_loop(0, owned // strip, add, 0)

    def fold_pair(q):
        for which in range(2):
            pair_copy(which, q).wait()
            fetch(which, pair_in.at[which, q], q, q).start()
        for which in range(2):
            fetch(which, pair_in.at[which, q], q, q).wait()
            add_rows(which, 2 * q + core, 2 * q + 1 - core)

            @pl.when(diagonal == q)
            def _():
                first_copy(which, 0).start()

            @pl.when(near[which] == q)
            def _():
                first_copy(which, 1).start()

    waiting = []
    for start, size in spans:
        span = slice(start, start + size)
        et_ref[span, :] = nn(pin[...], dhid_all[:, span]).astype(bf).T
        w_ref[span, :] = nn(back[...], act_all[:, span]).astype(bf).T
        ready = [q for q in range(chips) if start < 2 * (q + 1) * owned <= start + size]
        for q in ready:
            for which in range(2):
                pair_copy(which, q).start()
        for q in waiting:
            fold_pair(q)
        waiting = ready
    for q in waiting:
        fold_pair(q)
    for which in range(2):
        first_copy(which, 0).wait()
        fetch(which, first_in.at[which, 0], 0, chips).start()
        fetch(which, first_in.at[which, 0], 0, chips).wait()
        add_rows(which, 2 * near[1 - which] + core, 1 - core)
        second_copy(which).start()
    for which in range(2):
        first_copy(which, 1).wait()
        fetch(which, first_in.at[which, 1], 1, chips + 1).start()
    for which in range(2):
        fetch(which, first_in.at[which, 1], 1, chips + 1).wait()
        second_copy(which).wait()
        fetch(which, second_in.at[which], 2, chips + 2).start()
    for which in range(2):
        fetch(which, second_in.at[which], 2, chips + 2).wait()

        def gather(i, carry, which=which):
            total = None
            for owner in (spot, 3 - core, 5 - core):
                at = pl.ds(pl.multiple_of(owner * owned + i * strip, 16), strip)
                value = grads[which][at, :].astype(f32)
                total = value if total is None else total + value
            at = pl.ds(pl.multiple_of(which * owned + i * strip, 16), strip)
            share_ref[at, :] = total
            low_ref[at, :] = total.astype(bf)
            return carry

        lax.fori_loop(0, owned // strip, gather, 0)
    piece = small_ref.shape[1]
    each = off_ref.shape[1] // spots
    line[...] = jnp.zeros_like(line)
    for s in range(spots):
        line[:, :owned] = gu_ref[:, s * owned : (s + 1) * owned]
        line[:, owned : owned + each] = go_ref[:, s * each : (s + 1) * each]
        for n in range(small_ref.shape[0] // spots):
            at = n * spots + s
            small_ref[at : at + 1, :] = line[:, n * piece : (n + 1) * piece]
    for m in range(batches):
        for which in range(2):
            own_out(m, which).wait()
            for k in range(1, peers):
                out_copy(m, k, which).wait()


def mlp_fused(normed, back, expand_t, shrink, bias, lines, padded, ident):
    batches, height, channels, width = normed.shape
    peers = lax.axis_size("lvl")
    rows = height // peers
    spots, owned, every = expand_t.shape
    hidden = spots * owned
    chips = spots // 2
    pixels = rows * width
    bf, f32 = jnp.bfloat16, jnp.float32
    hbm = pl.BlockSpec(memory_space=pl.ANY)
    vmem = pl.BlockSpec(memory_space=pltpu.VMEM)
    dma = pltpu.SemaphoreType.DMA
    V, S = pltpu.VMEM, jax.ShapeDtypeStruct
    landing = (batches, rows, every, width)
    return pl.pallas_call(
        mlp_fused_body,
        in_specs=[hbm, hbm, hbm, hbm, vmem],
        out_specs=[hbm, hbm, vmem, vmem, vmem, hbm, hbm, hbm],
        out_shape=[
            S(normed.shape, bf), S(normed.shape, bf),
            S((2 * owned, every), f32), S((2 * owned, every), bf), S((lines, padded), f32),
            S((2, chips, owned, every), bf), S((2, 2, owned, every), bf),
            S((2, owned, every), bf),
        ],
        scratch_shapes=[
            V((1, hidden), f32), V((1, every), f32), V((1, hidden), f32), V((1, every), f32),
            V((1, lines // spots * padded), f32),
            V(landing, bf), V(landing, bf), V((2,) + landing, bf),
            V((hidden, every), bf), V((hidden, every), bf),
            V((every, batches * pixels), bf), V((pixels, every), bf),
            V((every, batches * pixels), bf), V((pixels, every), bf),
            V((pixels, every), f32), V((pixels, every), f32),
            V((batches * pixels, hidden), bf), V((batches * pixels, hidden), bf),
            dma((batches, peers)), dma((batches, peers)),
            dma((2, batches, peers)), dma((2, batches, peers)),
            dma((2, 4)), dma((batches + 1,)), dma((2, batches)),
            dma((2, chips)), dma((2, chips)), dma((2, 2)), dma((2, 2)), dma((2,)), dma((2,)),
            dma((2, chips + 3)), dma((2, 3)), dma((2, 3)), dma((2,)), dma((2,)),
        ],
        compiler_params=pltpu.CompilerParams(
            vmem_limit_bytes=63 * 1024 * 1024, collective_id=ident, has_side_effects=True
        ),
        cost_estimate=pl.CostEstimate(
            flops=12 * batches * pixels * every * hidden,
            bytes_accessed=8 * every * hidden,
            transcendentals=batches * pixels * hidden,
        ),
    )(normed, back, expand_t, shrink, bias)[:5]


def finish_body(
    conv_hbm, xt_hbm, dn_hbm, share_hbm, low_hbm, small_ref, par_ref, mask_ref, k_ref,
    igrad_hbm, zfull, zrecv_hbm, kg_ref, tot_ref, own_ref,
    conv, xt, dn, frame, obuf, taps, acc49, part, coef, stat, stat_all, kcols, msg, srecv,
    kmsg, krecv, zown, zlow, zrecv, zsmall, zsrecv, ztot,
    load_sem, out_sem, s_send, s_recv, k_send, k_recv, h_send, h_recv,
    z_send, z_recv, g_send, g_recv, q_send, q_recv, f_sem,
):
    f32, bf = jnp.float32, jnp.bfloat16
    batches, height, channels, width = conv.shape
    groups = channels // GROUP
    peers, place = lax.axis_size("lvl"), lax.axis_index("lvl")
    spots, spot = lax.axis_size("sp"), lax.axis_index("sp")
    mesh_id = pl.DeviceIdType.MESH

    pairs = [(dn_hbm, dn), (conv_hbm, conv)]
    loads = [
        [
            pltpu.make_async_copy(src.at[m], dst.at[m], load_sem.at[n, m])
            for n, (src, dst) in enumerate(pairs)
        ]
        for m in range(batches)
    ]
    load_x = pltpu.make_async_copy(xt_hbm, xt, load_sem.at[2, 0])
    for batch_loads in loads:
        for load in batch_loads:
            load.start()
    load_x.start()

    barrier = pltpu.get_barrier_semaphore()
    for k in range(1, peers):
        pl.semaphore_signal(
            barrier, inc=1, device_id={"lvl": lax.rem(place + k, peers)}, device_id_type=mesh_id
        )
    for k in range(1, spots):
        pl.semaphore_signal(
            barrier, inc=1, device_id={"sp": lax.rem(spot + k, spots)}, device_id_type=mesh_id
        )

    quarter = share_hbm.shape[0] // peers

    def quarter_rows(at):
        return pl.ds(pl.multiple_of(at * quarter, 8), quarter)

    def z_copy(k):
        to = lax.rem(place + k, peers)
        return pltpu.make_async_remote_copy(
            src_ref=low_hbm.at[quarter_rows(to), :], dst_ref=zrecv_hbm.at[k],
            send_sem=z_send.at[k], recv_sem=z_recv.at[k],
            device_id={"lvl": to}, device_id_type=mesh_id,
        )

    def g_copy(k):
        return pltpu.make_async_remote_copy(
            src_ref=zlow, dst_ref=zfull.at[quarter_rows(place), :],
            send_sem=g_send.at[k], recv_sem=g_recv.at[k],
            device_id={"lvl": lax.rem(place + k, peers)}, device_id_type=mesh_id,
        )

    def g_wait(k):
        source = lax.rem(place + peers - k, peers)
        pltpu.make_async_remote_copy(
            src_ref=zlow, dst_ref=zfull.at[quarter_rows(source), :],
            send_sem=g_send.at[k], recv_sem=g_recv.at[k],
            device_id={"lvl": lax.rem(place + k, peers)}, device_id_type=mesh_id,
        ).wait()

    def spread_copy(src, dst, send, recv, k):
        return pltpu.make_async_remote_copy(
            src_ref=src, dst_ref=dst.at[k], send_sem=send.at[k], recv_sem=recv.at[k],
            device_id={"sp": lax.rem(spot + k, spots)}, device_id_type=mesh_id,
        )

    def q_copy(k):
        return pltpu.make_async_remote_copy(
            src_ref=zsmall, dst_ref=zsrecv.at[k], send_sem=q_send.at[k], recv_sem=q_recv.at[k],
            device_id={"lvl": lax.rem(place + k, peers)}, device_id_type=mesh_id,
        )

    def to_next():
        return pltpu.make_async_remote_copy(
            src_ref=frame.at[:, pl.ds(height, MARGIN)], dst_ref=frame.at[:, pl.ds(0, MARGIN)],
            send_sem=h_send.at[0], recv_sem=h_recv.at[0],
            device_id={"sp": lax.rem(spot + 1, spots)}, device_id_type=mesh_id,
        )

    def to_prev():
        return pltpu.make_async_remote_copy(
            src_ref=frame.at[:, pl.ds(MARGIN, MARGIN)],
            dst_ref=frame.at[:, pl.ds(MARGIN + height, MARGIN)],
            send_sem=h_send.at[1], recv_sem=h_recv.at[1],
            device_id={"sp": lax.rem(spot + spots - 1, spots)}, device_id_type=mesh_id,
        )

    def load_own():
        return pltpu.make_async_copy(share_hbm.at[quarter_rows(place), :], zown, f_sem.at[0])

    def load_part(k):
        return pltpu.make_async_copy(zrecv_hbm.at[k], zrecv.at[k], f_sem.at[k])

    def keep_own():
        return pltpu.make_async_copy(zlow, zfull.at[quarter_rows(place), :], f_sem.at[peers])

    load_own().start()
    pl.semaphore_wait(barrier, peers - 1 + spots - 1)
    for k in range(1, peers):
        z_copy(k).start()

    def slot_sum(ref, own):
        total = None
        for source in range(spots):
            k = lax.rem(spot - source + spots, spots)
            value = ref[k]
            total = value if total is None else total + value
        return total

    stat[...] = jnp.zeros_like(stat)
    kcols[...] = jnp.zeros_like(kcols)
    lane = lax.broadcasted_iota(jnp.int32, (channels, 128), 1)
    every_row = (channels, width)

    def column(ref, at):
        return jnp.broadcast_to(ref[:channels, at : at + 1], every_row)

    for m in range(batches):
        coef[m, 0] = column(par_ref, m)
    for m in range(batches):
        for load in loads[m]:
            load.wait()

        def sums(g, carry, m=m):
            now = pl.ds(pl.multiple_of(g * GROUP, GROUP), GROUP)
            mean = coef[m, 0, now, :]
            plain, cross = None, None
            for i in range(height):
                grad = dn[m, i, now, :].astype(f32)
                turn = grad * (conv[m, i, now, :] - mean)
                plain = grad if plain is None else plain + grad
                cross = turn if cross is None else cross + turn
            part[0, m, now, :] = plain
            part[1, m, now, :] = cross
            return carry

        lax.fori_loop(0, groups, sums, 0)
    tile = jnp.zeros((channels, 128), f32)
    for m in range(batches):
        plain = jnp.sum(part[0, m], axis=1, keepdims=True)
        cross = jnp.sum(part[1, m], axis=1, keepdims=True) * par_ref[:channels, 8 + m : 9 + m]
        tile = jnp.where(lane == m, plain, tile)
        tile = jnp.where(lane == batches + m, cross, tile)
    stat[:channels, :] = tile
    head = 8
    msg[:head, :] = stat[...].T[:head, :]
    msg[head:, :] = small_ref[...]
    srecv[0] = msg[...]
    for k in range(1, spots):
        spread_copy(msg, srecv, s_send, s_recv, k).start()

    masks = lane_tap_masks(width)
    fill_taps(k_ref, taps, masks, groups)
    for k in range(1, spots):
        spread_copy(msg, srecv, s_send, s_recv, k).wait()
    total = slot_sum(srecv, msg)
    tot_ref[...] = total[:head, :]
    zsmall[...] = total[head:, :]
    for k in range(1, peers):
        q_copy(k).start()
    padded = jnp.concatenate(
        [total[:head, :], jnp.zeros((128 - head, total.shape[1]), f32)], axis=0
    )
    stat_all[...] = padded.T

    gain = column(par_ref, 24)
    for m in range(batches):
        rho = column(par_ref, 8 + m)
        lead = rho * gain
        share = lead * column(par_ref, 16 + m)
        coef[m, 1] = lead
        coef[m, 2] = column(stat_all, m) * share
        coef[m, 3] = column(stat_all, batches + m) * rho * share

    def grad_rows(m, now, wanted):
        mean, lead = coef[m, 0, now, :], coef[m, 1, now, :]
        flat, tilt = coef[m, 2, now, :], coef[m, 3, now, :]
        for i in wanted:
            off = (conv[m, i, now, :] - mean) * tilt + flat
            frame[m, MARGIN + i, now, :] = (
                lead * dn[m, i, now, :].astype(f32) - mask_ref[m, i : i + 1, :] * off
            )

    edges = list(range(MARGIN)) + list(range(height - MARGIN, height))

    def rims(g, carry):
        now = pl.ds(pl.multiple_of(g * GROUP, GROUP), GROUP)
        for m in range(batches):
            grad_rows(m, now, edges)
        return carry

    lax.fori_loop(0, groups, rims, 0)

    @pl.when(spot < spots - 1)
    def _():
        to_next().start()

    @pl.when(spot > 0)
    def _():
        to_prev().start()

    load_x.wait()

    def weight_terms(g, carry):
        now = pl.ds(pl.multiple_of(g * GROUP, GROUP), GROUP)
        for t in range(KW * KW):
            acc49[t, now, :] = jnp.zeros((GROUP, width), f32)

        def one(m, inner):
            grad_rows(m, now, range(MARGIN, height - MARGIN))
            for base in range(0, height, ROWS):
                back = [frame[m, MARGIN + base + i, now, :] for i in range(ROWS)]
                for b in range(KW):
                    rolled = [
                        shifted(xt[m, base + r, now, :], b - MARGIN)
                        for r in range(ROWS + KW - 1)
                    ]
                    for a in range(KW):
                        total = None
                        for i in range(ROWS):
                            term = back[i] * rolled[i + a]
                            total = term if total is None else total + term
                        acc49[a * KW + b, now, :] += total
            return inner

        lax.fori_loop(0, batches, one, 0)
        return carry

    middle = groups
    lax.fori_loop(0, middle, weight_terms, 0)
    load_own().wait()
    for k in range(1, peers):
        z_copy(k).wait()
        load_part(k).start()
    for k in range(1, peers):
        load_part(k).wait()

    def fold(i, carry):
        at = pl.ds(pl.multiple_of(i * GROUP, 8), GROUP)
        total = zown[at, :]
        for k in range(1, peers):
            total = total + zrecv[k, at, :].astype(f32)
        zlow[at, :] = total.astype(bf)
        return carry

    lax.fori_loop(0, quarter // GROUP, fold, 0)
    for k in range(1, peers):
        g_copy(k).start()
    keep_own().start()
    lax.fori_loop(middle, groups, weight_terms, 0)
    wide_lane = lax.broadcasted_iota(jnp.int32, (channels, width), 1)

    def reduce_tap(t, carry):
        b = lax.rem(t, KW) - MARGIN
        kept = jnp.logical_and(wide_lane + b >= 0, wide_lane + b < width)
        summed = jnp.sum(jnp.where(kept, acc49[t], 0.0), axis=1, keepdims=True)
        kcols[:channels, :] = jnp.where(lane == t, summed, kcols[:channels, :])
        return carry

    lax.fori_loop(0, KW * KW, reduce_tap, 0)
    kmsg[...] = kcols[...].T[: kmsg.shape[0], :]
    krecv[0] = kmsg[...]
    for k in range(1, spots):
        spread_copy(kmsg, krecv, k_send, k_recv, k).start()


    @pl.when(spot < spots - 1)
    def _():
        to_next().wait_send()
        to_prev().wait_recv()

    @pl.when(spot > 0)
    def _():
        to_prev().wait_send()
        to_next().wait_recv()

    @pl.when(spot == 0)
    def _():
        frame[:, :MARGIN] = jnp.zeros((batches, MARGIN, channels, width), f32)

    @pl.when(spot == spots - 1)
    def _():
        frame[:, MARGIN + height :] = jnp.zeros((batches, MARGIN, channels, width), f32)

    def save(m):
        return pltpu.make_async_copy(obuf.at[m], igrad_hbm.at[m], out_sem.at[m])

    def inputs(m, carry):
        def one(g, inner):
            now = pl.ds(pl.multiple_of(g * GROUP, GROUP), GROUP)
            for base in range(0, height, ROWS):
                outs = depthwise_rows(
                    lambda r: frame[m, base + r, now, :], taps, now, ROWS, -1
                )
                for i in range(ROWS):
                    obuf[m, base + i, now, :] = outs[i].astype(bf)
            return inner

        lax.fori_loop(0, groups, one, 0)
        save(m).start()
        return carry

    lax.fori_loop(0, batches, inputs, 0)
    for k in range(1, spots):
        spread_copy(kmsg, krecv, k_send, k_recv, k).wait()
    kg_ref[...] = slot_sum(krecv, kmsg)
    for k in range(1, peers):
        q_copy(k).wait()
    zsrecv[0] = zsmall[...]
    total = None
    for source in range(peers):
        value = zsrecv[lax.rem(place - source + peers, peers)]
        total = value if total is None else total + value
    ztot[...] = total
    own_ref[...] = jnp.zeros_like(own_ref)
    piece = small_ref.shape[1]
    for n in range(small_ref.shape[0] // spots):
        own_ref[0:1, n * piece : (n + 1) * piece] = ztot[pl.ds(n * spots + spot, 1), :]
    keep_own().wait()
    for k in range(1, peers):
        g_wait(k)
    for m in range(batches):
        save(m).wait()


def finish(conv, xt, dn, share, low, small, params, mask_cells, kernel, ident):
    batches, height, channels, width = conv.shape
    bf, f32 = jnp.bfloat16, jnp.float32
    peers, spots = lax.axis_size("lvl"), lax.axis_size("sp")
    padded = -(-channels // 128) * 128
    taps = -(-(KW * KW) // 8) * 8
    head = 8
    lines = small.shape[0]
    every = share.shape[1]
    quarter = share.shape[0] // peers
    hbm = pl.BlockSpec(memory_space=pl.ANY)
    vmem = pl.BlockSpec(memory_space=pltpu.VMEM)
    dma = pltpu.SemaphoreType.DMA
    framed = (batches, height + 2 * MARGIN, channels, width)
    S = jax.ShapeDtypeStruct
    return pl.pallas_call(
        finish_body,
        in_specs=[hbm] * 5 + [vmem] * 4,
        out_specs=[hbm, hbm, hbm, vmem, vmem, vmem],
        out_shape=[
            S(conv.shape, bf),
            S(share.shape, bf), S((peers, quarter, every), bf),
            S((taps, padded), f32), S((head, padded), f32), S((8, lines // spots * padded), f32),
        ],
        scratch_shapes=[
            pltpu.VMEM(conv.shape, f32), pltpu.VMEM(framed, f32),
            pltpu.VMEM(conv.shape, bf), pltpu.VMEM(framed, f32), pltpu.VMEM(conv.shape, bf),
            pltpu.VMEM((KW * KW, channels, width), f32),
            pltpu.VMEM((KW * KW, channels, width), f32),
            pltpu.VMEM((2, batches, channels, width), f32),
            pltpu.VMEM((batches, 4, channels, width), f32),
            pltpu.VMEM((padded, 128), f32), pltpu.VMEM((padded, 128), f32),
            pltpu.VMEM((padded, 128), f32),
            pltpu.VMEM((head + lines, padded), f32),
            pltpu.VMEM((spots, head + lines, padded), f32),
            pltpu.VMEM((taps, padded), f32),
            pltpu.VMEM((spots, taps, padded), f32),
            pltpu.VMEM((quarter, every), f32), pltpu.VMEM((quarter, every), bf),
            pltpu.VMEM((peers, quarter, every), bf),
            pltpu.VMEM(small.shape, f32),
            pltpu.VMEM((peers,) + small.shape, f32), pltpu.VMEM(small.shape, f32),
            dma((3, batches)), dma((batches,)), dma((spots,)), dma((spots,)), dma((spots,)), dma((spots,)),
            dma((2,)), dma((2,)), dma((peers,)), dma((peers,)), dma((peers,)), dma((peers,)),
            dma((peers,)), dma((peers,)), dma((peers + 1,)),
        ],
        compiler_params=pltpu.CompilerParams(
            vmem_limit_bytes=60 * 1024 * 1024, collective_id=ident, has_side_effects=True
        ),
        cost_estimate=pl.CostEstimate(
            flops=4 * KW * KW * batches * channels * height * width,
            bytes_accessed=34 * batches * channels * height * width,
            transcendentals=0,
        ),
    )(conv, xt, dn, share, low, small, params, mask_cells, kernel)


RATES = {"kernel": 0.15, "scales": 0.2, "expand": 0.035, "uplift": 0.1, "shrink": 0.018, "offset": 0.1}


def close_body(
    crop, step, x_ref, cot_ref, res_ref, dx_ref, mask_ref, ge_ref, gs_ref,
    e_ref, e1_ref, e2_ref, s_ref, s1_ref, s2_ref,
    kg_ref, tot_ref, own_ref,
    k_ref, k1_ref, k2_ref, c_ref, c1_ref, c2_ref, u_ref, u1_ref, u2_ref, o_ref, o1_ref, o2_ref,
    out_ref, igrad_ref, eg_out, em_out, en_out, sg_out, sm_out, sn_out,
    kg_out, km_out, kn_out, cg_out, cm_out, cn_out, ug_out, um_out, un_out, og_out, om_out, on_out,
    scr, scx,
):
    f32 = jnp.float32
    batches, block, height, width = x_ref.shape
    time = jnp.full((8, 128), step[0] + 1, jnp.int32).astype(f32)
    one = 1.0 / (1.0 - jnp.exp(time * math.log(beta_one)))[0:1, 0:1]
    two = 1.0 / (1.0 - jnp.exp(time * math.log(beta_two)))[0:1, 0:1]

    def step_of(weight, first, second, grad, rate):
        first_new = beta_one * first + (1.0 - beta_one) * grad
        second_new = beta_two * second + (1.0 - beta_two) * grad * grad
        update = first_new * one / (jnp.sqrt(second_new * two) + epsilon) + weight_decay * weight
        return second_new, weight - rate * update

    @pl.when(pl.program_id(0) == 0)
    def _():
        taps, channels = k_ref.shape
        kg = kg_ref[:taps, :channels]
        kg_out[...] = kg
        km_out[...], kn_out[...] = step_of(
            k_ref[...], k1_ref[...], k2_ref[...], kg, RATES["kernel"]
        )
        tot = tot_ref[...]
        plain = jnp.sum(tot[:batches], axis=0, keepdims=True)[:, :channels]
        cross = jnp.sum(tot[batches : 2 * batches], axis=0, keepdims=True)[:, :channels]
        for row, grad in ((0, cross), (1, plain)):
            at = slice(row, row + 1)
            cg_out[at, :] = grad
            cm_out[at, :], cn_out[at, :] = step_of(
                c_ref[at, :], c1_ref[at, :], c2_ref[at, :], grad, RATES["scales"]
            )
        owned, each = u_ref.shape[1], o_ref.shape[1]
        ug = own_ref[0:1, :owned]
        ug_out[...] = ug
        um_out[...], un_out[...] = step_of(
            u_ref[...], u1_ref[...], u2_ref[...], ug, RATES["uplift"]
        )
        og = own_ref[0:1, owned : owned + each]
        og_out[...] = og
        om_out[...], on_out[...] = step_of(
            o_ref[...], o1_ref[...], o2_ref[...], og, RATES["offset"]
        )

    strip = 16

    def rows(i, carry):
        at = pl.ds(pl.multiple_of(i * strip, strip), strip)
        for g_ref, w, w1, w2, g_out, m_out, n_out, rate in (
            (ge_ref, e_ref, e1_ref, e2_ref, eg_out, em_out, en_out, RATES["expand"]),
            (gs_ref, s_ref, s1_ref, s2_ref, sg_out, sm_out, sn_out, RATES["shrink"]),
        ):
            grad = g_ref[at, :].astype(f32)
            g_out[at, :] = grad
            m_out[at, :], n_out[at, :] = step_of(w[at, :], w1[at, :], w2[at, :], grad, rate)
        return carry

    lax.fori_loop(0, ge_ref.shape[0] // strip, rows, 0)
    row = lax.broadcasted_iota(jnp.int32, (height, width), 0)

    def cells(g, carry):
        c0 = pl.multiple_of(g * GROUP, GROUP)
        now = pl.ds(c0, GROUP)
        for m in range(batches):
            keep = (row < crop[m]).astype(f32)
            mask = mask_ref[m]
            for i in range(height):
                at = slice(i * GROUP, (i + 1) * GROUP)
                scr[m, at, :] = res_ref[m, i, now, :].astype(f32)
                scx[m, at, :] = dx_ref[m, i, now, :].astype(f32)
            for c in range(GROUP):
                part = pl.ds(c, height, stride=GROUP)
                out_ref[m, c0 + c] = mask * (x_ref[m, c0 + c].astype(f32) + scr[m, part, :])
                dres = cot_ref[m, c0 + c].astype(f32) * mask
                igrad_ref[m, c0 + c] = keep * (dres + scx[m, part, :])
        return carry

    lax.fori_loop(0, block // GROUP, cells, 0)


def close(crop, step, x, cot, res, dx, mask_cells, shares, expand, shrink, kg, tot, own, kernel, scales, uplift, offset):
    batches, channels, height, width = x.shape
    f32 = jnp.float32
    owned, every = expand[0].shape
    block = CLOSE_BLOCK
    steps = channels // block
    part = owned // steps
    natural = pl.BlockSpec((batches, block, height, width), lambda i: (0, i, 0, 0))
    turned = pl.BlockSpec((batches, height, block, width), lambda i: (0, 0, i, 0))
    smem = pl.BlockSpec(memory_space=pltpu.SMEM)
    lines = pl.BlockSpec((part, every), lambda i: (i, 0))
    later = pl.BlockSpec((part, every), lambda i: (i + steps, 0))

    def whole(v):
        zeros = (0,) * v.ndim
        return pl.BlockSpec(v.shape, lambda i: zeros)

    S = jax.ShapeDtypeStruct
    small = list(kernel) + list(scales) + list(uplift) + list(offset)
    return pl.pallas_call(
        close_body,
        grid=(steps,),
        in_specs=[smem, smem, natural, natural, turned, turned, whole(mask_cells), lines, later]
        + [lines] * 6 + [whole(v) for v in (kg, tot, own)] + [whole(v) for v in small],
        out_specs=[natural, natural] + [lines] * 6 + [whole(v) for v in small],
        out_shape=[S(x.shape, f32)] * 2 + [S((owned, every), f32)] * 6
        + [S(v.shape, f32) for v in small],
        scratch_shapes=[
            pltpu.VMEM((batches, GROUP * height, width), f32),
            pltpu.VMEM((batches, GROUP * height, width), f32),
        ],
        compiler_params=pltpu.CompilerParams(vmem_limit_bytes=63 * 1024 * 1024),
    )(
        crop, step, x, cot, res, dx, mask_cells, shares, shares,
        *expand, *shrink, kg, tot, own, *small,
    )


def sums_body(xt_ref, res_ref, dn_ref, conv_ref, mask_ref, par_ref, out_ref, stat_ref, scr):
    batches, height = res_ref.shape[:2]
    width = res_ref.shape[3]

    def one(m, stats):
        lane = lax.broadcasted_iota(jnp.int32, (GROUP, 128), 1)
        mean = jnp.sum(jnp.where(lane == m, par_ref[...], 0.0), axis=1, keepdims=True)
        rho = jnp.sum(jnp.where(lane == batches + m, par_ref[...], 0.0), axis=1, keepdims=True)
        mean = jnp.broadcast_to(mean, (GROUP, width))
        rho = jnp.broadcast_to(rho, (GROUP, width))
        plain = jnp.zeros((GROUP, width), jnp.float32)
        cross = jnp.zeros((GROUP, width), jnp.float32)
        for i in range(height):
            grad = dn_ref[m, i].astype(jnp.float32)
            plain = plain + grad
            cross = cross + grad * ((conv_ref[m, i] - mean) * rho)
            value = xt_ref[m, MARGIN + i] + res_ref[m, i].astype(jnp.float32)
            scr[pl.ds(i, GROUP, stride=height), :] = value * mask_ref[m, i : i + 1, :]
        for c in range(GROUP):
            out_ref[m, c] = scr[c * height : (c + 1) * height, :]
        stats = jnp.where(lane == m, jnp.sum(plain, axis=1, keepdims=True), stats)
        return jnp.where(lane == batches + m, jnp.sum(cross, axis=1, keepdims=True), stats)

    stat_ref[...] = lax.fori_loop(0, batches, one, jnp.zeros((GROUP, 128), jnp.float32))


def output_and_sums(xt, res, dn, conv, mask_cells, params):
    batches, height, channels, width = res.shape
    turned = lambda rows: pl.BlockSpec((batches, rows, GROUP, width), lambda g: (0, 0, g, 0))
    return pl.pallas_call(
        sums_body,
        grid=(pl.cdiv(channels, GROUP),),
        in_specs=[
            turned(height + 2 * MARGIN),
            turned(height), turned(height), turned(height),
            pl.BlockSpec((batches, height, width), lambda g: (0, 0, 0)),
            pl.BlockSpec((GROUP, 128), lambda g: (g, 0)),
        ],
        out_specs=[
            pl.BlockSpec((batches, GROUP, height, width), lambda g: (0, g, 0, 0)),
            pl.BlockSpec((GROUP, 128), lambda g: (g, 0)),
        ],
        out_shape=[
            jax.ShapeDtypeStruct((batches, channels, height, width), jnp.float32),
            jax.ShapeDtypeStruct((channels, 128), jnp.float32),
        ],
        scratch_shapes=[pltpu.VMEM((GROUP * height, width), jnp.float32)],
        cost_estimate=pl.CostEstimate(
            flops=10 * batches * channels * height * width,
            bytes_accessed=20 * batches * channels * height * width,
            transcendentals=0,
        ),
    )(xt, res, dn, conv, mask_cells, params)


def conv_back_body(
    crop, xt_ref, grad_ref, up_ref, dn_ref, cot_ref, k_ref, mask_ref,
    out_ref, kg_ref, scr, wscr, frame, sums,
):
    batches, height = grad_ref.shape[:2]
    width = grad_ref.shape[3]
    masks = lane_tap_masks(width)
    for a in range(KW):
        for b in range(KW):
            t = a * KW + b
            spread = jnp.broadcast_to(k_ref[:, t : t + 1], (GROUP, width))
            wscr[t] = jnp.where(masks[KW - 1 - b], spread, 0.0)
            sums[t] = jnp.zeros((GROUP, width), jnp.float32)

    def one(m, carry):
        for r in range(MARGIN):
            frame[r] = up_ref[m, r]
            frame[MARGIN + height + r] = dn_ref[m, r]
        for i in range(height):
            frame[MARGIN + i] = grad_ref[m, i]
        for base in range(0, height, ROWS):
            for b in range(KW):
                rolled = [
                    shifted(xt_ref[m, base + r], b - MARGIN) for r in range(ROWS + KW - 1)
                ]
                for a in range(KW):
                    part = None
                    for i in range(ROWS):
                        term = frame[MARGIN + base + i] * rolled[i + a]
                        part = term if part is None else part + term
                    sums[a * KW + b] += part
            acc = [None] * ROWS
            for b in range(KW):
                rolled = [
                    shifted(frame[base + r], MARGIN - b) for r in range(ROWS + KW - 1)
                ]
                for a in range(KW):
                    tap = wscr[a * KW + b]
                    for i in range(ROWS):
                        term = tap * rolled[i + KW - 1 - a]
                        acc[i] = term if acc[i] is None else acc[i] + term
            for i in range(ROWS):
                scr[pl.ds(base + i, GROUP, stride=height), :] = acc[i]
        row = lax.broadcasted_iota(jnp.int32, (height, width), 0)
        for c in range(GROUP):
            dres = cot_ref[m, c].astype(jnp.float32) * mask_ref[m]
            total = dres + scr[c * height : (c + 1) * height, :]
            out_ref[m, c] = jnp.where(row < crop[m, 0], total, 0.0)
        return carry

    lax.fori_loop(0, batches, one, 0)
    columns = []
    for t in range(KW * KW):
        kept = jnp.where(masks[t % KW], sums[t], 0.0)
        columns.append((t, jnp.sum(kept, axis=1, keepdims=True)))
    kg_ref[...] = put_columns(columns)


def conv_backward(crop, xt, grad_conv, up, down, cot, kernel, mask_cells):
    batches, height, channels, width = grad_conv.shape
    natural = pl.BlockSpec((batches, GROUP, height, width), lambda g, c: (0, g, 0, 0))
    turned = lambda rows: pl.BlockSpec((batches, rows, GROUP, width), lambda g, c: (0, 0, g, 0))
    return pl.pallas_call(
        conv_back_body,
        grid_spec=pltpu.PrefetchScalarGridSpec(
            num_scalar_prefetch=1,
            grid=(pl.cdiv(channels, GROUP),),
            in_specs=[
                turned(height + 2 * MARGIN),
                turned(height),
                turned(MARGIN), turned(MARGIN),
                natural,
                pl.BlockSpec((GROUP, KW * KW), lambda g, c: (g, 0)),
                pl.BlockSpec((batches, height, width), lambda g, c: (0, 0, 0)),
            ],
            out_specs=[natural, pl.BlockSpec((GROUP, 128), lambda g, c: (g, 0))],
            scratch_shapes=[
                pltpu.VMEM((GROUP * height, width), jnp.float32),
                pltpu.VMEM((KW * KW, GROUP, width), jnp.float32),
                pltpu.VMEM((height + 2 * MARGIN, GROUP, width), jnp.float32),
                pltpu.VMEM((KW * KW, GROUP, width), jnp.float32),
            ],
        ),
        out_shape=[
            jax.ShapeDtypeStruct((batches, channels, height, width), jnp.float32),
            jax.ShapeDtypeStruct((channels, 128), jnp.float32),
        ],
        cost_estimate=pl.CostEstimate(
            flops=4 * KW * KW * batches * channels * height * width,
            bytes_accessed=14 * batches * channels * height * width,
            transcendentals=0,
        ),
    )(crop, xt, grad_conv, up, down, cot, kernel, mask_cells)


def neighbours(head, tail, axis):
    count = lax.axis_size(axis)
    up = lax.ppermute(tail, axis, [(i, i + 1) for i in range(count - 1)])
    down = lax.ppermute(head, axis, [(i + 1, i) for i in range(count - 1)])
    return up, down


def aligned(channels, height, owned, levels):
    return (
        channels % 8 == 0 and height % levels == 0 and height == ROWS
        and owned % 16 == 0 and (2 * owned) % (8 * levels) == 0
        and channels % CLOSE_BLOCK == 0 and owned % (16 * (channels // CLOSE_BLOCK)) == 0
    )


def on_device(
    input_field, cotangent, ocean_mask, crop_rows, step_count,
    kernel, kernel_first, kernel_second,
    scales, scales_first, scales_second,
    expand, expand_first, expand_second,
    uplift, uplift_first, uplift_second,
    shrink, shrink_first, shrink_second,
    offset, offset_first, offset_second,
):
    f32, bf = jnp.float32, jnp.bfloat16
    batches, channels, height, width = input_field.shape
    sp = lax.axis_size("sp")
    lvl = lax.axis_size("lvl")
    place = lax.axis_index("sp")
    owned = uplift.shape[0]
    hidden, every = sp * owned, sp * offset.shape[0]
    if aligned(channels, height, owned, lvl) and sp == 8:
        crop = crop_rows.reshape(batches)
        (
            conv, xt, normed, pixel_back, expand_all, shrink_all, params, mask_cells, bias, turned_k,
        ) = forward(
            crop, input_field, cotangent, ocean_mask, kernel.T, scales,
            expand.T, shrink, uplift[None], offset[None], 0,
        )
        padded = params.shape[0]
        lines = -(-(owned + offset.shape[0]) // padded) * sp
        result, grad_normed, share, low, small = mlp_fused(
            normed, pixel_back, expand_all, shrink_all, bias, lines, padded, 1
        )
        field_grad, shares, _, kernel_rows, both, own = finish(
            conv, xt, grad_normed, share, low, small, params, mask_cells, turned_k, 2
        )
        (
            block_output, input_grad, eg, em, en, sg, sm, sn,
            kg, km, kn, cg, cm, cn, ug, um, un, og, om, on,
        ) = close(
            crop, step_count.reshape(1), input_field, cotangent, result, field_grad, mask_cells,
            shares, (expand.T, expand_first.T, expand_second.T),
            (shrink, shrink_first, shrink_second), kernel_rows, both, own,
            (kernel.T, kernel_first.T, kernel_second.T), (scales, scales_first, scales_second),
            (uplift[None], uplift_first[None], uplift_second[None]),
            (offset[None], offset_first[None], offset_second[None]),
        )
        return (
            block_output, input_grad, kg.T, km.T, kn.T, cg, cm, cn, eg.T, em.T, en.T,
            ug[0], um[0], un[0], sg, sm, sn, og[0], om[0], on[0], step_count + 1,
        )
    else:
        expand_all = lax.all_gather(expand.T.astype(bf), "sp", axis=0, tiled=True)
        shrink_all = lax.all_gather(shrink.astype(bf), "sp", axis=0, tiled=True)
        uplift_all = lax.all_gather(uplift.astype(bf), "sp", axis=0, tiled=True)
        offset_all = lax.all_gather(offset.astype(bf), "sp", axis=0, tiled=True)

        valid = (jnp.arange(height, dtype=jnp.int32)[None, :] < crop_rows).astype(f32)
        mask_cells = ocean_mask.astype(f32) * valid[:, :, None]
        valid_low = valid.astype(bf)[:, None, :, None]
        head = input_field[:, :, :MARGIN] * valid_low[:, :, :MARGIN]
        tail = input_field[:, :, height - MARGIN :] * valid_low[:, :, height - MARGIN :]
        up, down = neighbours(head.transpose(0, 2, 1, 3), tail.transpose(0, 2, 1, 3), "sp")
        conv, xt, dres, stats = conv_forward(
            crop_rows, input_field, cotangent, up, down, kernel, mask_cells
        )
        every = lax.all_gather(stats[:, : 4 * batches], "sp", axis=0)
        sums = every[:, :, :batches]
        squares = every[:, :, batches : 2 * batches]
        cells = every[:, :, 2 * batches : 3 * batches]
        count = jnp.maximum(jnp.sum(cells, axis=0), 1.0)
        mean = jnp.sum(sums, axis=0) / count
        gap = sums / jnp.maximum(cells, 1.0) - mean[None]
        variance = jnp.sum(squares + cells * gap * gap, axis=0) / count
        rho = lax.rsqrt(variance + 1e-05)

        def spread(stat):
            return stat.T[:, None, :, None]

        gain = scales[0][None, None, :, None]
        shift = scales[1][None, None, :, None]
        normed = ((conv - spread(mean)) * spread(rho) * gain + shift).astype(bf)

        def to_pixels(v):
            return lax.all_to_all(v, "lvl", split_axis=1, concat_axis=2, tiled=True)

        def to_channels(v):
            return lax.all_to_all(v, "lvl", split_axis=2, concat_axis=1, tiled=True)

        pixel_back = to_pixels(dres)
        biases = (uplift_all.astype(f32)[None], offset_all.astype(f32)[None])
        result, grad_normed, grad_expand, grad_shrink, grad_uplift, grad_offset = mlp(
            to_pixels(normed), pixel_back, expand_all, shrink_all, *biases
        )
        result = to_channels(result)
        grad_normed = to_channels(grad_normed)
        params = jnp.concatenate([mean, rho], axis=1)
        params = jnp.pad(params, ((0, 0), (0, 128 - params.shape[1])))
        block_output, local = output_and_sums(xt, result, grad_normed, conv, mask_cells, params)
        both = lax.psum(local[:, : 2 * batches], "sp")
        plain, cross = both[:, :batches], both[:, batches:]
        scales_grad = jnp.stack([jnp.sum(cross, axis=1), jnp.sum(plain, axis=1)], axis=0)
        whitened = (conv - spread(mean)) * spread(rho)
        grad_conv = spread(rho) * (
            gain * grad_normed.astype(f32)
            - mask_cells[:, :, None, :] * gain * (spread(plain) + whitened * spread(cross)) / spread(count)
        )
        back_up, back_down = neighbours(
            grad_conv[:, :MARGIN], grad_conv[:, height - MARGIN :], "sp"
        )
        input_grad, kernel_cols = conv_backward(
            crop_rows, xt, grad_conv, back_up, back_down, cotangent, kernel, mask_cells
        )
        kernel_grad = lax.psum(kernel_cols[:, : KW * KW], "sp")

        def own_share(partial):
            rows = partial.shape[0] // sp
            parts = lax.all_to_all(
                partial.reshape(sp, rows, partial.shape[1]), "sp", split_axis=0, concat_axis=0
            )
            share = jnp.sum(parts.astype(f32), axis=0).astype(bf)
            return jnp.sum(lax.all_gather(share, "lvl", axis=0).astype(f32), axis=0)

        share_expand = own_share(grad_expand)
        share_shrink = own_share(grad_shrink)
        small = lax.psum(
            jnp.concatenate([grad_uplift[0], grad_offset[0]]), ("sp", "lvl")
        )
    share_uplift = lax.dynamic_slice_in_dim(small, place * owned, owned)
    share_offset = lax.dynamic_slice_in_dim(
        small, hidden + place * offset.shape[0], offset.shape[0]
    )
    step_float = (step_count + 1).astype(f32)
    kernel_moment, kernel_next = adamw(
        kernel, kernel_first, kernel_second, kernel_grad, 0.15, step_float
    )
    scales_moment, scales_next = adamw(
        scales, scales_first, scales_second, scales_grad, 0.2, step_float
    )
    expand_grad = share_expand.T
    expand_moment, expand_next = adamw(
        expand, expand_first, expand_second, expand_grad, 0.035, step_float
    )
    uplift_moment, uplift_next = adamw(
        uplift, uplift_first, uplift_second, share_uplift, 0.1, step_float
    )
    shrink_moment, shrink_next = adamw(
        shrink, shrink_first, shrink_second, share_shrink, 0.018, step_float
    )
    offset_moment, offset_next = adamw(
        offset, offset_first, offset_second, share_offset, 0.1, step_float
    )
    return (
        block_output, input_grad,
        kernel_grad, kernel_moment, kernel_next,
        scales_grad, scales_moment, scales_next,
        expand_grad, expand_moment, expand_next,
        share_uplift, uplift_moment, uplift_next,
        share_shrink, shrink_moment, shrink_next,
        share_offset, offset_moment, offset_next,
        step_count + 1,
    )


def solution(mesh):
    tile = P(None, "lvl", "sp", None)
    by_channel = P("lvl", None)
    by_scale = P(None, "lvl")
    by_hidden = P(None, "sp")
    by_row = P("sp", None)
    line = P("sp")
    in_specs = (
        tile, tile, P(None, "sp", None), P(None, "sp"), P(),
        by_channel, by_channel, by_channel,
        by_scale, by_scale, by_scale,
        by_hidden, by_hidden, by_hidden,
        line, line, line,
        by_row, by_row, by_row,
        line, line, line,
    )
    out_specs = (
        tile, tile,
        by_channel, by_channel, by_channel,
        by_scale, by_scale, by_scale,
        by_hidden, by_hidden, by_hidden,
        line, line, line,
        by_row, by_row, by_row,
        line, line, line,
        P(),
    )
    return jax.shard_map(
        on_device, mesh=mesh, in_specs=in_specs, out_specs=out_specs, check_vma=False
    )
```

```python
import functools
import math

import jax
import jax.numpy as jnp
from jax import lax
from jax.experimental import pallas as pl
from jax.experimental.pallas import tpu as pltpu
from jax.sharding import PartitionSpec as P

KW = 7
MARGIN = KW // 2
GROUP = 8
CLOSE_BLOCK = 40
ROWS = 16

beta_one = 0.9
beta_two = 0.999
epsilon = 1e-08
weight_decay = 0.01
GELU_A = math.sqrt(2.0 / math.pi)
GELU_B = 0.044715


def adamw(weight, first, second, grad, rate, step_float):
    first_new = beta_one * first + (1.0 - beta_one) * grad
    second_new = beta_two * second + (1.0 - beta_two) * grad * grad
    fix_first = 1.0 - jnp.power(beta_one, step_float)
    fix_second = 1.0 - jnp.power(beta_two, step_float)
    update = (
        first_new / fix_first / (jnp.sqrt(second_new / fix_second) + epsilon)
        + weight_decay * weight
    )
    return (second_new, weight - rate * update)


def lane_tap_masks(width):
    lane = lax.broadcasted_iota(jnp.int32, (GROUP, width), 1)
    return [
        jnp.logical_and(lane + (b - MARGIN) >= 0, lane + (b - MARGIN) < width)
        for b in range(KW)
    ]


def shifted(value, amount):
    width = value.shape[-1]
    turn = (-amount) % width
    return value if turn == 0 else pltpu.roll(value, turn, 1)


def chip_neighbours(chip):
    across = chip + 1 - 2 * lax.rem(chip, 2)
    along = lax.rem(chip + 2, 4)
    return across, along, lax.rem(across + 2, 4)


def fill_taps(k_ref, taps, masks, groups):
    width = taps.shape[2]

    def fill(g, carry):
        now = pl.ds(pl.multiple_of(g * GROUP, GROUP), GROUP)
        for a in range(KW):
            for b in range(KW):
                t = a * KW + b
                tap = jnp.broadcast_to(k_ref[now, t : t + 1], (GROUP, width))
                taps[t, now, :] = jnp.where(masks[b], tap, 0.0)
        return carry

    lax.fori_loop(0, groups, fill, 0)


def depthwise_rows(source, taps, now, rows, sign):
    width = taps.shape[2]
    outs = [None] * rows
    for first in range(0, rows, 8):
        values = [source(first + r) for r in range(8 + KW - 1)]
        for b in range(KW):
            part = [None] * 8
            for a in range(KW):
                tap = taps[a * KW + b, now, :]
                at = a if sign > 0 else KW - 1 - a
                for i in range(8):
                    term = tap * values[i + at]
                    part[i] = term if part[i] is None else part[i] + term
            for i in range(8):
                moved = shifted(part[i], sign * (b - MARGIN))
                at = first + i
                outs[at] = moved if outs[at] is None else outs[at] + moved
    return outs


def put_columns(columns):
    lane = lax.broadcasted_iota(jnp.int32, (GROUP, 128), 1)
    out = jnp.zeros((GROUP, 128), jnp.float32)
    for at, column in columns:
        out = jnp.where(lane == at, column, out)
    return out


def conv_body(
    crop, x_ref, cot_ref, up_ref, dn_ref, k_ref, mask_ref,
    conv_ref, xt_ref, dres_ref, stat_ref, scr, scc, wscr,
):
    batches, _, height, width = x_ref.shape
    masks = lane_tap_masks(width)
    for a in range(KW):
        for b in range(KW):
            t = a * KW + b
            spread = jnp.broadcast_to(k_ref[:, t : t + 1], (GROUP, width))
            wscr[t] = jnp.where(masks[b], spread, 0.0)

    def one(m, stats):
        for c in range(GROUP):
            scr[c * height : (c + 1) * height, :] = x_ref[m, c].astype(jnp.float32)
            scc[c * height : (c + 1) * height, :] = cot_ref[m, c].astype(jnp.float32)
        limit = crop[m, 0]
        for i in range(height):
            row = scr[pl.ds(i, GROUP, stride=height), :]
            xt_ref[m, MARGIN + i] = jnp.where(i < limit, row, 0.0)
            back = scc[pl.ds(i, GROUP, stride=height), :]
            dres_ref[m, i] = (back * mask_ref[m, i : i + 1, :]).astype(jnp.bfloat16)
        for r in range(MARGIN):
            xt_ref[m, r] = up_ref[m, r].astype(jnp.float32)
            xt_ref[m, MARGIN + height + r] = dn_ref[m, r].astype(jnp.float32)
        total = jnp.zeros((GROUP, width), jnp.float32)
        for base in range(0, height, ROWS):
            acc = [None] * ROWS
            for b in range(KW):
                rolled = [
                    shifted(xt_ref[m, base + r], b - MARGIN) for r in range(ROWS + KW - 1)
                ]
                for a in range(KW):
                    tap = wscr[a * KW + b]
                    for i in range(ROWS):
                        term = tap * rolled[i + a]
                        acc[i] = term if acc[i] is None else acc[i] + term
            for i in range(ROWS):
                conv_ref[m, base + i] = acc[i]
                total = total + acc[i] * mask_ref[m, base + i : base + i + 1, :]
        cells = jnp.sum(mask_ref[m])
        summed = jnp.sum(total, axis=1, keepdims=True)
        mean = summed / jnp.maximum(cells, 1.0)
        spread = jnp.zeros((GROUP, width), jnp.float32)
        for i in range(height):
            off = conv_ref[m, i] - mean
            spread = spread + off * off * mask_ref[m, i : i + 1, :]
        squares = jnp.sum(spread, axis=1, keepdims=True)
        lane = lax.broadcasted_iota(jnp.int32, (GROUP, 128), 1)
        stats = jnp.where(lane == m, summed, stats)
        stats = jnp.where(lane == batches + m, squares, stats)
        return jnp.where(lane == 2 * batches + m, cells, stats)

    stat_ref[...] = lax.fori_loop(0, batches, one, jnp.zeros((GROUP, 128), jnp.float32))


def conv_forward(crop, x, cot, up, down, kernel, mask_cells):
    batches, channels, height, width = x.shape
    groups = pl.cdiv(channels, GROUP)
    natural = pl.BlockSpec((batches, GROUP, height, width), lambda g, c: (0, g, 0, 0))
    turned = lambda rows: pl.BlockSpec((batches, rows, GROUP, width), lambda g, c: (0, 0, g, 0))
    return pl.pallas_call(
        conv_body,
        grid_spec=pltpu.PrefetchScalarGridSpec(
            num_scalar_prefetch=1,
            grid=(groups,),
            in_specs=[
                natural,
                natural,
                turned(MARGIN),
                turned(MARGIN),
                pl.BlockSpec((GROUP, KW * KW), lambda g, c: (g, 0)),
                pl.BlockSpec((batches, height, width), lambda g, c: (0, 0, 0)),
            ],
            out_specs=[
                turned(height),
                turned(height + 2 * MARGIN),
                turned(height),
                pl.BlockSpec((GROUP, 128), lambda g, c: (g, 0)),
            ],
            scratch_shapes=[
                pltpu.VMEM((GROUP * height, width), jnp.float32),
                pltpu.VMEM((GROUP * height, width), jnp.float32),
                pltpu.VMEM((KW * KW, GROUP, width), jnp.float32),
            ],
        ),
        out_shape=[
            jax.ShapeDtypeStruct((batches, height, channels, width), jnp.float32),
            jax.ShapeDtypeStruct((batches, height + 2 * MARGIN, channels, width), jnp.float32),
            jax.ShapeDtypeStruct((batches, height, channels, width), jnp.bfloat16),
            jax.ShapeDtypeStruct((channels, 128), jnp.float32),
        ],
        cost_estimate=pl.CostEstimate(
            flops=2 * KW * KW * batches * channels * height * width,
            bytes_accessed=30 * batches * channels * height * width,
            transcendentals=0,
        ),
    )(crop, x, cot, up, down, kernel, mask_cells)


def forward_body(
    crop, x_hbm, cot_hbm, ocean_ref, kt_ref, scale_ref, et_hbm, w_hbm, up_own, off_own,
    conv_hbm, xt_hbm, norm_hbm, back_hbm, et_all, w_all, par_ref, mask_ref, bias_ref, turned_k,
    xv, cotv, xt, conv, dres, norm, edge, rim, cast, scr, scc, taps, part, stat, msg, srecv, scal, bias, kpad, et_own, w_own,
    load_sem, save_sem, own_sem, pair_send, pair_recv, chip_send, chip_recv,
    b_send, b_recv, s_send, s_recv, h_send, h_recv, d_send, d_recv, d_own,
):
    f32, bf = jnp.float32, jnp.bfloat16
    batches, height, channels, width = conv.shape
    groups = channels // GROUP
    peers, place = lax.axis_size("lvl"), lax.axis_index("lvl")
    spots, spot = lax.axis_size("sp"), lax.axis_index("sp")
    chips = spots // 2
    chip, core = spot // 2, lax.rem(spot, 2)
    sibling = spot + 1 - 2 * core
    rows = height // peers
    mesh_id = pl.DeviceIdType.MESH
    near = chip_neighbours(chip)[:2]

    loads = [
        pltpu.make_async_copy(cot_hbm, cotv, load_sem.at[0]),
        pltpu.make_async_copy(x_hbm, xv, load_sem.at[1]),
    ]
    loads[0].start()
    loads[1].start()

    def own_load(which):
        return pltpu.make_async_copy(
            (et_hbm, w_hbm)[which], (et_own, w_own)[which], load_sem.at[2 + which]
        )

    for which in range(2):
        own_load(which).start()
    barrier = pltpu.get_barrier_semaphore()
    for k in range(1, peers):
        pl.semaphore_signal(
            barrier, inc=1, device_id={"lvl": lax.rem(place + k, peers)}, device_id_type=mesh_id
        )
    for k in range(1, spots):
        pl.semaphore_signal(
            barrier, inc=1, device_id={"sp": lax.rem(spot + k, spots)}, device_id_type=mesh_id
        )

    gathered = (et_all, w_all)

    def own_copy(which):
        return pltpu.make_async_copy(cast.at[which], gathered[which].at[spot], own_sem.at[which])

    def pair_copy(which):
        return pltpu.make_async_remote_copy(
            src_ref=cast.at[which], dst_ref=gathered[which].at[spot],
            send_sem=pair_send.at[which], recv_sem=pair_recv.at[which],
            device_id={"sp": sibling}, device_id_type=mesh_id,
        )

    def chip_copy(which, k):
        to = 2 * near[k] + core
        return pltpu.make_async_remote_copy(
            src_ref=cast.at[which], dst_ref=gathered[which].at[spot],
            send_sem=chip_send.at[which, k], recv_sem=chip_recv.at[which, k],
            device_id={"sp": to}, device_id_type=mesh_id,
        )

    def bias_copy(k):
        return pltpu.make_async_remote_copy(
            src_ref=bias, dst_ref=bias_ref.at[spot],
            send_sem=b_send.at[k], recv_sem=b_recv.at[k],
            device_id={"sp": lax.rem(spot + k, spots)}, device_id_type=mesh_id,
        )

    def stat_copy(k):
        return pltpu.make_async_remote_copy(
            src_ref=msg, dst_ref=srecv.at[k], send_sem=s_send.at[k], recv_sem=s_recv.at[k],
            device_id={"sp": lax.rem(spot + k, spots)}, device_id_type=mesh_id,
        )

    def to_next():
        return pltpu.make_async_remote_copy(
            src_ref=edge.at[1], dst_ref=rim.at[0], send_sem=h_send.at[0], recv_sem=h_recv.at[0],
            device_id={"sp": lax.rem(spot + 1, spots)}, device_id_type=mesh_id,
        )

    def to_prev():
        return pltpu.make_async_remote_copy(
            src_ref=edge.at[0], dst_ref=rim.at[1], send_sem=h_send.at[1], recv_sem=h_recv.at[1],
            device_id={"sp": lax.rem(spot + spots - 1, spots)}, device_id_type=mesh_id,
        )

    span = pl.ds(pl.multiple_of(place * channels, 8), channels)

    def dres_copy(k):
        to = lax.rem(place + k, peers)
        return pltpu.make_async_remote_copy(
            src_ref=dres.at[:, pl.ds(to * rows, rows)], dst_ref=back_hbm.at[:, :, span, :],
            send_sem=d_send.at[k], recv_sem=d_recv.at[k],
            device_id={"lvl": to}, device_id_type=mesh_id,
        )

    def dres_own():
        return pltpu.make_async_copy(
            dres.at[:, pl.ds(place * rows, rows)], back_hbm.at[:, :, span, :], d_own.at[0]
        )

    row = lax.broadcasted_iota(jnp.int32, (height, width), 0)
    for m in range(batches):
        keep = (row < crop[m]).astype(f32)
        mask_ref[m] = ocean_ref[m].astype(f32) * keep

    def turn_cot(g, carry):
        c0 = pl.multiple_of(g * GROUP, GROUP)
        now = pl.ds(c0, GROUP)
        for m in range(batches):
            for c in range(GROUP):
                scc[m, c * height : (c + 1) * height, :] = cotv[m, c0 + c].astype(f32) * mask_ref[m]
            for i in range(height):
                dres[m, i, now, :] = scc[m, pl.ds(i, GROUP, stride=height), :].astype(bf)
        return carry

    def turn_x(g, carry):
        c0 = pl.multiple_of(g * GROUP, GROUP)
        now = pl.ds(c0, GROUP)
        for m in range(batches):
            keep = (row < crop[m]).astype(f32)
            for c in range(GROUP):
                scr[m, c * height : (c + 1) * height, :] = xv[m, c0 + c].astype(f32) * keep
            for i in range(height):
                value = scr[m, pl.ds(i, GROUP, stride=height), :]
                xt[m, MARGIN + i, now, :] = value
                if i < MARGIN:
                    edge[0, m, i, now, :] = value.astype(bf)
                if i >= height - MARGIN:
                    edge[1, m, i - (height - MARGIN), now, :] = value.astype(bf)
        return carry

    loads[0].wait()
    lax.fori_loop(0, groups, turn_cot, 0)
    pl.semaphore_wait(barrier, peers - 1 + spots - 1)
    for k in range(1, peers):
        dres_copy(k).start()
    dres_own().start()
    loads[1].wait()
    lax.fori_loop(0, groups, turn_x, 0)

    @pl.when(spot < spots - 1)
    def _():
        to_next().start()

    @pl.when(spot > 0)
    def _():
        to_prev().start()

    for which in range(2):
        own_load(which).wait()
    cast[0] = et_own[...].astype(bf)
    cast[1] = w_own[...].astype(bf)
    bias[...] = jnp.zeros_like(bias)
    bias[0:1, : up_own.shape[1]] = up_own[...].astype(bf).astype(f32)
    bias[1:2, : off_own.shape[1]] = off_own[...].astype(bf).astype(f32)
    stat[...] = jnp.zeros_like(stat)
    kpad[...] = jnp.zeros_like(kpad)
    kpad[: KW * KW, :channels] = kt_ref[...]
    turned_k[...] = kpad[...].T
    scal[...] = jnp.zeros_like(scal)
    scal[0:2, :channels] = scale_ref[...]
    bias_ref[spot] = bias[...]
    for k in range(2):
        chip_copy(k, k).start()
    for k in range(2):
        chip_copy(1 - k, k).start()
    for which in range(2):
        pair_copy(which).start()
        own_copy(which).start()
    for k in range(1, spots):
        bias_copy(k).start()
    masks = lane_tap_masks(width)
    fill_taps(turned_k, taps, masks[::-1], groups)

    @pl.when(spot < spots - 1)
    def _():
        to_next().wait_send()
        to_prev().wait_recv()
        xt[:, MARGIN + height :] = rim[1].astype(f32)

    @pl.when(spot > 0)
    def _():
        to_prev().wait_send()
        to_next().wait_recv()
        xt[:, :MARGIN] = rim[0].astype(f32)

    @pl.when(spot == 0)
    def _():
        xt[:, :MARGIN] = jnp.zeros((batches, MARGIN, channels, width), f32)

    @pl.when(spot == spots - 1)
    def _():
        xt[:, MARGIN + height :] = jnp.zeros((batches, MARGIN, channels, width), f32)

    save_x = pltpu.make_async_copy(xt, xt_hbm, save_sem.at[0])
    save_x.start()

    def convolve(g, carry):
        now = pl.ds(pl.multiple_of(g * GROUP, GROUP), GROUP)

        def one(m, inner):
            for base in range(0, height, ROWS):
                outs = depthwise_rows(
                    lambda r: xt[m, base + r, now, :], taps, now, ROWS, 1
                )
                total = None
                for i in range(ROWS):
                    conv[m, base + i, now, :] = outs[i]
                    value = outs[i] * mask_ref[m, base + i : base + i + 1, :]
                    total = value if total is None else total + value
                if base == 0:
                    part[m, now, :] = total
                else:
                    part[m, now, :] += total
            return inner

        lax.fori_loop(0, batches, one, 0)
        return carry

    lax.fori_loop(0, groups, convolve, 0)
    cells = [jnp.sum(mask_ref[m]) for m in range(batches)]
    lane = lax.broadcasted_iota(jnp.int32, (channels, 128), 1)
    tile = jnp.zeros((channels, 128), f32)
    for m in range(batches):
        summed = jnp.sum(part[m], axis=1, keepdims=True)
        tile = jnp.where(lane == m, summed, tile)
        tile = jnp.where(lane == 16 + m, cells[m], tile)
        part[m] = jnp.broadcast_to(summed / jnp.maximum(cells[m], 1.0), (channels, width))

    def scatter(g, carry):
        now = pl.ds(pl.multiple_of(g * GROUP, GROUP), GROUP)
        for m in range(batches):
            mean = part[m, now, :]
            around = None
            for i in range(height):
                off = conv[m, i, now, :] - mean
                value = off * off * mask_ref[m, i : i + 1, :]
                around = value if around is None else around + value
            part[m, now, :] = around
        return carry

    lax.fori_loop(0, groups, scatter, 0)
    for m in range(batches):
        tile = jnp.where(lane == 8 + m, jnp.sum(part[m], axis=1, keepdims=True), tile)
    stat[:channels, :] = tile
    save_conv = pltpu.make_async_copy(conv, conv_hbm, save_sem.at[1])
    save_conv.start()
    msg[...] = stat[...].T[:24, :]
    srecv[0] = msg[...]
    for k in range(1, spots):
        stat_copy(k).start()
    for k in range(1, spots):
        stat_copy(k).wait()
    order = [lax.rem(spot - source + spots, spots) for source in range(spots)]
    summed, count = None, None
    for k in order:
        value, cell = srecv[k, 0:8, :], srecv[k, 16:24, :]
        summed = value if summed is None else summed + value
        count = cell if count is None else count + cell
    count = jnp.maximum(count, 1.0)
    mean = summed / count
    squares = None
    for k in order:
        cell = srecv[k, 16:24, :]
        gap = srecv[k, 0:8, :] / jnp.maximum(cell, 1.0) - mean
        value = srecv[k, 8:16, :] + cell * gap * gap
        squares = value if squares is None else squares + value
    rho = lax.rsqrt(squares / count + 1e-05)
    filler = jnp.zeros((128 - 32, mean.shape[1]), f32)
    par_ref[...] = jnp.concatenate([mean, rho, 1.0 / count, scal[...], filler], axis=0).T

    def normalize(g, carry):
        now = pl.ds(pl.multiple_of(g * GROUP, GROUP), GROUP)
        par = par_ref[now, :]
        gain = jnp.broadcast_to(par[:, 24:25], (GROUP, width))
        shift = jnp.broadcast_to(par[:, 25:26], (GROUP, width))
        for m in range(batches):
            mean = jnp.broadcast_to(par[:, m : m + 1], (GROUP, width))
            rho = jnp.broadcast_to(par[:, 8 + m : 9 + m], (GROUP, width))
            scale = rho * gain
            for i in range(height):
                value = (conv[m, i, now, :] - mean) * scale + shift
                norm[m, i, now, :] = value.astype(bf)
        return carry

    lax.fori_loop(0, groups, normalize, 0)
    save_norm = pltpu.make_async_copy(norm, norm_hbm, save_sem.at[2])
    save_norm.start()
    for k in range(1, spots):
        pltpu.make_async_remote_copy(
            src_ref=bias, dst_ref=bias_ref.at[lax.rem(spot + spots - k, spots)],
            send_sem=b_send.at[k], recv_sem=b_recv.at[k],
            device_id={"sp": lax.rem(spot + k, spots)}, device_id_type=mesh_id,
        ).wait()
    for which in range(2):
        own_copy(which).wait()
        pltpu.make_async_remote_copy(
            src_ref=cast.at[which], dst_ref=gathered[which].at[sibling],
            send_sem=pair_send.at[which], recv_sem=pair_recv.at[which],
            device_id={"sp": sibling}, device_id_type=mesh_id,
        ).wait()
        for k in range(2):
            other = 2 * near[k] + core
            pltpu.make_async_remote_copy(
                src_ref=cast.at[which], dst_ref=gathered[which].at[other],
                send_sem=chip_send.at[which, k], recv_sem=chip_recv.at[which, k],
                device_id={"sp": other}, device_id_type=mesh_id,
            ).wait()
    dres_own().wait()
    for k in range(1, peers):
        source = pl.ds(pl.multiple_of(lax.rem(place + peers - k, peers) * channels, 8), channels)
        pltpu.make_async_remote_copy(
            src_ref=dres.at[:, pl.ds(lax.rem(place + k, peers) * rows, rows)],
            dst_ref=back_hbm.at[:, :, source, :],
            send_sem=d_send.at[k], recv_sem=d_recv.at[k],
            device_id={"lvl": lax.rem(place + k, peers)}, device_id_type=mesh_id,
        ).wait()
    save_x.wait()
    save_conv.wait()
    save_norm.wait()


def forward(crop, x, cot, ocean, kernel, scales, expand_t, shrink, uplift, offset, ident):
    batches, channels, height, width = x.shape
    f32, bf = jnp.float32, jnp.bfloat16
    peers, spots = lax.axis_size("lvl"), lax.axis_size("sp")
    chips = spots // 2
    rows = height // peers
    owned, every = expand_t.shape
    padded = -(-channels // 128) * 128
    lanes = -(-max(owned, offset.shape[1]) // 128) * 128
    hbm = pl.BlockSpec(memory_space=pl.ANY)
    vmem = pl.BlockSpec(memory_space=pltpu.VMEM)
    dma = pltpu.SemaphoreType.DMA
    turned = (batches, height, channels, width)
    framed = (batches, height + 2 * MARGIN, channels, width)
    rim = (2, batches, MARGIN, channels, width)
    V, S = pltpu.VMEM, jax.ShapeDtypeStruct
    return pl.pallas_call(
        forward_body,
        in_specs=[pl.BlockSpec(memory_space=pltpu.SMEM), hbm, hbm, vmem, vmem, vmem, hbm, hbm, vmem, vmem],
        out_specs=[hbm] * 6 + [vmem] * 4,
        out_shape=[
            S(turned, f32), S(framed, f32), S(turned, bf),
            S((batches, rows, every, width), bf),
            S((spots, owned, every), bf), S((spots, owned, every), bf),
            S((padded, 128), f32), S((batches, height, width), f32), S((spots, 8, lanes), f32),
            S((padded, 128), f32),
        ],
        scratch_shapes=[
            V(x.shape, bf), V(x.shape, bf), V(framed, f32), V(turned, f32), V(turned, bf),
            V(turned, bf), V(rim, bf), V(rim, bf), V((2, owned, every), bf),
            V((batches, GROUP * height, width), f32), V((batches, GROUP * height, width), f32),
            V((KW * KW, channels, width), f32), V((batches, channels, width), f32),
            V((padded, 128), f32), V((24, padded), f32), V((spots, 24, padded), f32),
            V((8, padded), f32), V((8, lanes), f32), V((128, padded), f32),
            V((owned, every), f32), V((owned, every), f32),
            dma((4,)), dma((3,)), dma((2,)), dma((2,)), dma((2,)),
            dma((2, 2)), dma((2, 2)),
            dma((spots,)), dma((spots,)), dma((spots,)), dma((spots,)),
            dma((2,)), dma((2,)), dma((peers,)), dma((peers,)), dma((1,)),
        ],
        compiler_params=pltpu.CompilerParams(
            vmem_limit_bytes=60 * 1024 * 1024, collective_id=ident, has_side_effects=True
        ),
        cost_estimate=pl.CostEstimate(
            flops=2 * KW * KW * batches * channels * height * width,
            bytes_accessed=30 * batches * channels * height * width,
            transcendentals=0,
        ),
    )(crop, x, cot, ocean, kernel, scales, expand_t, shrink, uplift, offset)


def chunks_of(total, size):
    return [(start, min(size, total - start)) for start in range(0, total, size)]


def nt(a, b):
    return lax.dot_general(a, b, (((1,), (1,)), ((), ())), preferred_element_type=jnp.float32)


def nn(a, b):
    return jnp.dot(a, b, preferred_element_type=jnp.float32)


def mlp_body(
    pin_ref, back_ref, et_ref, w_ref, up_ref, off_ref,
    res_ref, dn_ref, ge_out, gw_out, gu_out, go_out,
    pin, pint, back, backt, res_acc, dn_acc, ge, gw, gu, go,
):
    m = pl.program_id(0)
    last = pl.num_programs(0) - 1
    rows, channels, width = pin_ref.shape[1:]
    hidden = et_ref.shape[0]
    for r in range(rows):
        cols = slice(r * width, (r + 1) * width)
        value = pin_ref[0, r]
        pin[:, cols] = value
        pint[cols, :] = value.T
        value = back_ref[0, r]
        back[:, cols] = value
        backt[cols, :] = value.T

    @pl.when(m == 0)
    def _():
        ge[...] = jnp.zeros_like(ge)
        gw[...] = jnp.zeros_like(gw)
        gu[...] = jnp.zeros_like(gu)
        go[...] = jnp.zeros_like(go)

    go[...] += jnp.sum(backt[...].astype(jnp.float32), axis=0, keepdims=True)
    for index, (start, size) in enumerate(chunks_of(hidden, 512)):
        span = slice(start, start + size)
        et = et_ref[span, :]
        wt = w_ref[span, :]
        hid = nt(pint[...], et) + up_ref[:, span]
        dact = nt(backt[...], wt)
        square = hid * hid
        inner = GELU_A * hid * (1.0 + GELU_B * square)
        t = jnp.tanh(inner)
        half = 0.5 * (1.0 + t)
        act = (hid * half).astype(jnp.bfloat16)
        slope = half + 0.5 * hid * (1.0 - t * t) * (GELU_A * (1.0 + 3.0 * GELU_B * square))
        dhid = (slope * dact).astype(jnp.bfloat16)
        res_part = nn(act, wt)
        dn_part = nn(dhid, et)
        if index == 0:
            res_acc[...] = res_part
            dn_acc[...] = dn_part
        else:
            res_acc[...] += res_part
            dn_acc[...] += dn_part
        ge[:, span] += nn(pin[...], dhid)
        gw[:, span] += nn(back[...], act)
        gu[:, span] += jnp.sum(dhid.astype(jnp.float32), axis=0, keepdims=True)

        @pl.when(m == last)
        def _():
            ge_out[span, :] = ge[:, span].astype(jnp.bfloat16).T
            gw_out[span, :] = gw[:, span].astype(jnp.bfloat16).T

    for r in range(rows):
        cols = slice(r * width, (r + 1) * width)
        res_ref[0, r] = (res_acc[cols, :] + off_ref[...]).astype(jnp.bfloat16).T
        dn_ref[0, r] = dn_acc[cols, :].astype(jnp.bfloat16).T

    @pl.when(m == last)
    def _():
        gu_out[...] = gu[...]
        go_out[...] = go[...]


def mlp(pin, back, expand_t, shrink, uplift, offset):
    batches, rows, channels, width = pin.shape
    hidden = expand_t.shape[0]
    pixels = rows * width
    block = pl.BlockSpec((1, rows, channels, width), lambda m: (m, 0, 0, 0))
    whole = lambda shape: pl.BlockSpec(shape, lambda m: (0, 0), pipeline_mode=pl.Buffered(1))
    bf, f32 = jnp.bfloat16, jnp.float32
    return pl.pallas_call(
        mlp_body,
        grid=(batches,),
        in_specs=[
            block, block,
            whole((hidden, channels)), whole((hidden, channels)),
            whole((1, hidden)), whole((1, channels)),
        ],
        out_specs=[
            block, block,
            whole((hidden, channels)), whole((hidden, channels)),
            whole((1, hidden)), whole((1, channels)),
        ],
        out_shape=[
            jax.ShapeDtypeStruct(pin.shape, bf),
            jax.ShapeDtypeStruct(pin.shape, bf),
            jax.ShapeDtypeStruct((hidden, channels), bf),
            jax.ShapeDtypeStruct((hidden, channels), bf),
            jax.ShapeDtypeStruct((1, hidden), f32),
            jax.ShapeDtypeStruct((1, channels), f32),
        ],
        scratch_shapes=[
            pltpu.VMEM((channels, pixels), bf),
            pltpu.VMEM((pixels, channels), bf),
            pltpu.VMEM((channels, pixels), bf),
            pltpu.VMEM((pixels, channels), bf),
            pltpu.VMEM((pixels, channels), f32),
            pltpu.VMEM((pixels, channels), f32),
            pltpu.VMEM((channels, hidden), f32),
            pltpu.VMEM((channels, hidden), f32),
            pltpu.VMEM((1, hidden), f32),
            pltpu.VMEM((1, channels), f32),
        ],
        compiler_params=pltpu.CompilerParams(vmem_limit_bytes=62 * 1024 * 1024),
        cost_estimate=pl.CostEstimate(
            flops=12 * batches * pixels * channels * hidden,
            bytes_accessed=2 * 4 * channels * hidden,
            transcendentals=batches * pixels * hidden,
        ),
    )(pin, back, expand_t, shrink, uplift, offset)


def mlp_fused_body(
    normed, back_hbm, et_hbm, w_hbm, bias_ref,
    res_out, dn_out, share_ref, low_ref, small_ref, pair_in, first_in, second_in,
    up_ref, off_ref, gu_ref, go_ref, line, land, land_back, stage, et_ref, w_ref,
    pin, pint, back, backt, res_acc, dn_acc, act_all, dhid_all,
    in_send, in_recv, out_send, out_recv, load_sem, own_sem, keep_sem,
    pair_send, pair_recv, first_send, first_recv, second_send, second_recv, fetch_sem,
    pass_send, pass_recv, relay_send, relay_recv,
):
    f32, bf = jnp.float32, jnp.bfloat16
    batches, height, channels, width = normed.shape
    peers = lax.axis_size("lvl")
    me = lax.axis_index("lvl")
    rows = height // peers
    pixels = rows * width
    hidden = et_ref.shape[0]
    spots = lax.axis_size("sp")
    spot = lax.axis_index("sp")
    chips = spots // 2
    chip, core = spot // 2, lax.rem(spot, 2)
    owned = hidden // spots
    across, along, diagonal = chip_neighbours(chip)
    near = (across, along)
    sibling = spot + 1 - 2 * core
    mine = (2 * across + core, 2 * along + core, 2 * diagonal + core)
    others = (2 * across + 1 - core, 2 * along + 1 - core, 2 * diagonal + 1 - core)
    mesh_id = pl.DeviceIdType.MESH
    weights = ((et_hbm, et_ref), (w_hbm, w_ref))

    def owner_rows(owner):
        return pl.ds(pl.multiple_of(owner * owned, 16), owned)

    def weight_load(which, k):
        owner = (mine[0], mine[1], spot, sibling)[k]
        return pltpu.make_async_copy(
            weights[which][0].at[owner], weights[which][1].at[owner_rows(owner), :],
            load_sem.at[which, k],
        )

    def weight_pass(which, k, owner):
        rows_now = owner_rows(owner)
        source = weights[which][1].at[rows_now, :] if k == 2 else weights[which][0].at[owner]
        return pltpu.make_async_remote_copy(
            src_ref=source, dst_ref=weights[which][1].at[rows_now, :],
            send_sem=pass_send.at[which, k], recv_sem=pass_recv.at[which, k],
            device_id={"sp": sibling}, device_id_type=mesh_id,
        )

    def relay(which, owner):
        return pltpu.make_async_remote_copy(
            src_ref=weights[which][0].at[owner], dst_ref=weights[which][1].at[owner_rows(owner), :],
            send_sem=relay_send.at[which], recv_sem=relay_recv.at[which],
            device_id={"sp": mine[which]}, device_id_type=mesh_id,
        )

    load_back = pltpu.make_async_copy(back_hbm, land_back, own_sem.at[batches])
    load_back.start()
    for which in range(2):
        for k in range(4):
            weight_load(which, k).start()

    barrier = pltpu.get_barrier_semaphore()
    for k in range(1, peers):
        pl.semaphore_signal(
            barrier, inc=1, device_id={"lvl": lax.rem(me + k, peers)}, device_id_type=mesh_id
        )
    pl.semaphore_signal(barrier, inc=1, device_id={"sp": sibling}, device_id_type=mesh_id)
    for k in range(3):
        pl.semaphore_signal(barrier, inc=1, device_id={"sp": mine[k]}, device_id_type=mesh_id)
    pl.semaphore_wait(barrier, peers - 1 + 4)

    def span_of(at):
        return pl.ds(pl.multiple_of(at * channels, 8), channels)

    def in_copy(m, k):
        to = lax.rem(me + k, peers)
        return pltpu.make_async_remote_copy(
            src_ref=normed.at[m, pl.ds(to * rows, rows)],
            dst_ref=land.at[m, :, span_of(me), :],
            send_sem=in_send.at[m, k], recv_sem=in_recv.at[m, k],
            device_id={"lvl": to}, device_id_type=mesh_id,
        )

    def own_in(m):
        return pltpu.make_async_copy(
            normed.at[m, pl.ds(me * rows, rows)], land.at[m, :, span_of(me), :], own_sem.at[m]
        )

    outs = (res_out, dn_out)

    def out_copy(m, k, which):
        to = lax.rem(me + k, peers)
        return pltpu.make_async_remote_copy(
            src_ref=stage.at[which, m, :, span_of(to), :],
            dst_ref=outs[which].at[m, pl.ds(me * rows, rows)],
            send_sem=out_send.at[which, m, k], recv_sem=out_recv.at[which, m, k],
            device_id={"lvl": to}, device_id_type=mesh_id,
        )

    def own_out(m, which):
        return pltpu.make_async_copy(
            stage.at[which, m, :, span_of(me), :],
            outs[which].at[m, pl.ds(me * rows, rows)],
            keep_sem.at[which, m],
        )

    for m in range(batches):
        own_in(m).start()
    for k in range(1, peers):
        in_copy(0, k).start()
    for which in range(2):
        relay(which, mine[1 - which]).start()
        for k in range(2):
            weight_pass(which, k, mine[k]).start()
    for s in range(spots):
        row = bias_ref[s]
        up_ref[:, s * owned : (s + 1) * owned] = row[0:1, :owned]
        each = off_ref.shape[1] // spots
        off_ref[:, s * each : (s + 1) * each] = row[1:2, :each]
    gu_ref[...] = jnp.zeros_like(gu_ref)
    go_ref[...] = jnp.zeros_like(go_ref)
    load_back.wait()
    for which in range(2):
        relay(which, mine[1 - which]).wait_send()
        relay(which, mine[2]).wait_recv()
        weight_pass(which, 2, mine[2]).start()
    for which in range(2):
        for k in range(4):
            weight_load(which, k).wait()
        for k in range(2):
            weight_pass(which, k, mine[k]).wait_send()
            weight_pass(which, k, others[k]).wait_recv()
    for which in range(2):
        weight_pass(which, 2, mine[2]).wait_send()
        weight_pass(which, 2, others[2]).wait_recv()

    spans = chunks_of(hidden, 512)

    def one(m, carry):
        own_in(m).wait()
        for k in range(1, peers):
            in_copy(m, k).wait()

        @pl.when(m == 0)
        def _():
            for other in range(1, batches):
                for k in range(1, peers):
                    in_copy(other, k).start()

        mine_now = pl.ds(pl.multiple_of(m * pixels, 128), pixels)
        for r in range(rows):
            here = slice(r * width, (r + 1) * width)
            cols = pl.ds(pl.multiple_of(m * pixels + r * width, 128), width)
            value = land[m, r]
            pin[:, cols] = value
            pint[here, :] = value.T
            value = land_back[m, r]
            back[:, cols] = value
            backt[here, :] = value.T
        go_ref[...] += jnp.sum(backt[...].astype(f32), axis=0, keepdims=True)
        for index, (start, size) in enumerate(spans):
            span = slice(start, start + size)
            et = et_ref[span, :]
            wt = w_ref[span, :]
            hid = nt(pint[...], et) + up_ref[:, span]
            dact = nt(backt[...], wt)
            square = hid * hid
            half = 0.5 + 0.5 * jnp.tanh(hid * (GELU_A + (GELU_A * GELU_B) * square))
            full = hid * half
            act = full.astype(bf)
            slope = half + full * (1.0 - half) * (
                2.0 * GELU_A + (6.0 * GELU_A * GELU_B) * square
            )
            dhid = (slope * dact).astype(bf)
            act_all[mine_now, span] = act
            dhid_all[mine_now, span] = dhid
            res_part = nn(act, wt)
            dn_part = nn(dhid, et)
            if index == 0:
                res_acc[...] = res_part
                dn_acc[...] = dn_part
            else:
                res_acc[...] += res_part
                dn_acc[...] += dn_part
            gu_ref[:, span] += jnp.sum(dhid.astype(f32), axis=0, keepdims=True)

        for r in range(rows):
            here = slice(r * width, (r + 1) * width)
            stage[0, m, r] = (res_acc[here, :] + off_ref[...]).astype(bf).T
            stage[1, m, r] = dn_acc[here, :].astype(bf).T
        for which in range(2):
            for k in range(1, peers):
                out_copy(m, k, which).start()
            own_out(m, which).start()
        return carry

    lax.fori_loop(0, batches, one, 0)

    grads = (et_ref, w_ref)

    def pair_copy(which, q):
        return pltpu.make_async_remote_copy(
            src_ref=grads[which].at[owner_rows(2 * q + 1 - core), :],
            dst_ref=pair_in.at[which, q],
            send_sem=pair_send.at[which, q], recv_sem=pair_recv.at[which, q],
            device_id={"sp": sibling}, device_id_type=mesh_id,
        )

    def spare(which, q):
        return grads[which].at[owner_rows(2 * q + 1 - core), :]

    def fetch(which, source, q, slot):
        return pltpu.make_async_copy(source, spare(which, q), fetch_sem.at[which, slot])

    def first_copy(which, slot):
        owner = (2 * diagonal + core, 2 * near[which] + core)[slot]
        return pltpu.make_async_remote_copy(
            src_ref=grads[which].at[owner_rows(owner), :], dst_ref=first_in.at[which, slot],
            send_sem=first_send.at[which, slot], recv_sem=first_recv.at[which, slot],
            device_id={"sp": 2 * near[which] + core}, device_id_type=mesh_id,
        )

    def second_copy(which):
        owner = 2 * near[1 - which] + core
        return pltpu.make_async_remote_copy(
            src_ref=grads[which].at[owner_rows(owner), :], dst_ref=second_in.at[which],
            send_sem=second_send.at[which], recv_sem=second_recv.at[which],
            device_id={"sp": owner}, device_id_type=mesh_id,
        )

    strip = 16

    def add_rows(which, to, source):
        def add(i, carry):
            at = pl.ds(pl.multiple_of(to * owned + i * strip, 16), strip)
            more = pl.ds(pl.multiple_of(source * owned + i * strip, 16), strip)
            total = grads[which][at, :].astype(f32) + grads[which][more, :].astype(f32)
            grads[which][at, :] = total.astype(bf)
            return carry

        lax.fori_loop(0, owned // strip, add, 0)

    def fold_pair(q):
        for which in range(2):
            pair_copy(which, q).wait()
            fetch(which, pair_in.at[which, q], q, q).start()
        for which in range(2):
            fetch(which, pair_in.at[which, q], q, q).wait()
            add_rows(which, 2 * q + core, 2 * q + 1 - core)

            @pl.when(diagonal == q)
            def _():
                first_copy(which, 0).start()

            @pl.when(near[which] == q)
            def _():
                first_copy(which, 1).start()

    waiting = []
    for start, size in spans:
        span = slice(start, start + size)
        et_ref[span, :] = nn(pin[...], dhid_all[:, span]).astype(bf).T
        w_ref[span, :] = nn(back[...], act_all[:, span]).astype(bf).T
        ready = [q for q in range(chips) if start < 2 * (q + 1) * owned <= start + size]
        for q in ready:
            for which in range(2):
                pair_copy(which, q).start()
        for q in waiting:
            fold_pair(q)
        waiting = ready
    for q in waiting:
        fold_pair(q)
    for which in range(2):
        first_copy(which, 0).wait()
        fetch(which, first_in.at[which, 0], 0, chips).start()
        fetch(which, first_in.at[which, 0], 0, chips).wait()
        add_rows(which, 2 * near[1 - which] + core, 1 - core)
        second_copy(which).start()
    for which in range(2):
        first_copy(which, 1).wait()
        fetch(which, first_in.at[which, 1], 1, chips + 1).start()
    for which in range(2):
        fetch(which, first_in.at[which, 1], 1, chips + 1).wait()
        second_copy(which).wait()
        fetch(which, second_in.at[which], 2, chips + 2).start()
    for which in range(2):
        fetch(which, second_in.at[which], 2, chips + 2).wait()

        def gather(i, carry, which=which):
            total = None
            for owner in (spot, 3 - core, 5 - core):
                at = pl.ds(pl.multiple_of(owner * owned + i * strip, 16), strip)
                value = grads[which][at, :].astype(f32)
                total = value if total is None else total + value
            at = pl.ds(pl.multiple_of(which * owned + i * strip, 16), strip)
            share_ref[at, :] = total
            low_ref[at, :] = total.astype(bf)
            return carry

        lax.fori_loop(0, owned // strip, gather, 0)
    piece = small_ref.shape[1]
    each = off_ref.shape[1] // spots
    line[...] = jnp.zeros_like(line)
    for s in range(spots):
        line[:, :owned] = gu_ref[:, s * owned : (s + 1) * owned]
        line[:, owned : owned + each] = go_ref[:, s * each : (s + 1) * each]
        for n in range(small_ref.shape[0] // spots):
            at = n * spots + s
            small_ref[at : at + 1, :] = line[:, n * piece : (n + 1) * piece]
    for m in range(batches):
        for which in range(2):
            own_out(m, which).wait()
            for k in range(1, peers):
                out_copy(m, k, which).wait()


def mlp_fused(normed, back, expand_t, shrink, bias, lines, padded, ident):
    batches, height, channels, width = normed.shape
    peers = lax.axis_size("lvl")
    rows = height // peers
    spots, owned, every = expand_t.shape
    hidden = spots * owned
    chips = spots // 2
    pixels = rows * width
    bf, f32 = jnp.bfloat16, jnp.float32
    hbm = pl.BlockSpec(memory_space=pl.ANY)
    vmem = pl.BlockSpec(memory_space=pltpu.VMEM)
    dma = pltpu.SemaphoreType.DMA
    V, S = pltpu.VMEM, jax.ShapeDtypeStruct
    landing = (batches, rows, every, width)
    return pl.pallas_call(
        mlp_fused_body,
        in_specs=[hbm, hbm, hbm, hbm, vmem],
        out_specs=[hbm, hbm, vmem, vmem, vmem, hbm, hbm, hbm],
        out_shape=[
            S(normed.shape, bf), S(normed.shape, bf),
            S((2 * owned, every), f32), S((2 * owned, every), bf), S((lines, padded), f32),
            S((2, chips, owned, every), bf), S((2, 2, owned, every), bf),
            S((2, owned, every), bf),
        ],
        scratch_shapes=[
            V((1, hidden), f32), V((1, every), f32), V((1, hidden), f32), V((1, every), f32),
            V((1, lines // spots * padded), f32),
            V(landing, bf), V(landing, bf), V((2,) + landing, bf),
            V((hidden, every), bf), V((hidden, every), bf),
            V((every, batches * pixels), bf), V((pixels, every), bf),
            V((every, batches * pixels), bf), V((pixels, every), bf),
            V((pixels, every), f32), V((pixels, every), f32),
            V((batches * pixels, hidden), bf), V((batches * pixels, hidden), bf),
            dma((batches, peers)), dma((batches, peers)),
            dma((2, batches, peers)), dma((2, batches, peers)),
            dma((2, 4)), dma((batches + 1,)), dma((2, batches)),
            dma((2, chips)), dma((2, chips)), dma((2, 2)), dma((2, 2)), dma((2,)), dma((2,)),
            dma((2, chips + 3)), dma((2, 3)), dma((2, 3)), dma((2,)), dma((2,)),
        ],
        compiler_params=pltpu.CompilerParams(
            vmem_limit_bytes=63 * 1024 * 1024, collective_id=ident, has_side_effects=True
        ),
        cost_estimate=pl.CostEstimate(
            flops=12 * batches * pixels * every * hidden,
            bytes_accessed=8 * every * hidden,
            transcendentals=batches * pixels * hidden,
        ),
    )(normed, back, expand_t, shrink, bias)[:5]


def finish_body(
    conv_hbm, xt_hbm, dn_hbm, share_hbm, low_hbm, small_ref, par_ref, mask_ref, k_ref,
    igrad_hbm, zfull, zrecv_hbm, kg_ref, tot_ref, own_ref,
    conv, xt, dn, frame, obuf, taps, acc49, part, coef, stat, stat_all, kcols, msg, srecv,
    kmsg, krecv, zown, zlow, zrecv, zsmall, zsrecv, ztot,
    load_sem, out_sem, s_send, s_recv, k_send, k_recv, h_send, h_recv,
    z_send, z_recv, g_send, g_recv, q_send, q_recv, f_sem,
):
    f32, bf = jnp.float32, jnp.bfloat16
    batches, height, channels, width = conv.shape
    groups = channels // GROUP
    peers, place = lax.axis_size("lvl"), lax.axis_index("lvl")
    spots, spot = lax.axis_size("sp"), lax.axis_index("sp")
    mesh_id = pl.DeviceIdType.MESH

    pairs = [(dn_hbm, dn), (conv_hbm, conv)]
    loads = [
        [
            pltpu.make_async_copy(src.at[m], dst.at[m], load_sem.at[n, m])
            for n, (src, dst) in enumerate(pairs)
        ]
        for m in range(batches)
    ]
    load_x = pltpu.make_async_copy(xt_hbm, xt, load_sem.at[2, 0])
    for batch_loads in loads:
        for load in batch_loads:
            load.start()
    load_x.start()

    barrier = pltpu.get_barrier_semaphore()
    for k in range(1, peers):
        pl.semaphore_signal(
            barrier, inc=1, device_id={"lvl": lax.rem(place + k, peers)}, device_id_type=mesh_id
        )
    for k in range(1, spots):
        pl.semaphore_signal(
            barrier, inc=1, device_id={"sp": lax.rem(spot + k, spots)}, device_id_type=mesh_id
        )

    quarter = share_hbm.shape[0] // peers

    def quarter_rows(at):
        return pl.ds(pl.multiple_of(at * quarter, 8), quarter)

    def z_copy(k):
        to = lax.rem(place + k, peers)
        return pltpu.make_async_remote_copy(
            src_ref=low_hbm.at[quarter_rows(to), :], dst_ref=zrecv_hbm.at[k],
            send_sem=z_send.at[k], recv_sem=z_recv.at[k],
            device_id={"lvl": to}, device_id_type=mesh_id,
        )

    def g_copy(k):
        return pltpu.make_async_remote_copy(
            src_ref=zlow, dst_ref=zfull.at[quarter_rows(place), :],
            send_sem=g_send.at[k], recv_sem=g_recv.at[k],
            device_id={"lvl": lax.rem(place + k, peers)}, device_id_type=mesh_id,
        )

    def g_wait(k):
        source = lax.rem(place + peers - k, peers)
        pltpu.make_async_remote_copy(
            src_ref=zlow, dst_ref=zfull.at[quarter_rows(source), :],
            send_sem=g_send.at[k], recv_sem=g_recv.at[k],
            device_id={"lvl": lax.rem(place + k, peers)}, device_id_type=mesh_id,
        ).wait()

    def spread_copy(src, dst, send, recv, k):
        return pltpu.make_async_remote_copy(
            src_ref=src, dst_ref=dst.at[k], send_sem=send.at[k], recv_sem=recv.at[k],
            device_id={"sp": lax.rem(spot + k, spots)}, device_id_type=mesh_id,
        )

    def q_copy(k):
        return pltpu.make_async_remote_copy(
            src_ref=zsmall, dst_ref=zsrecv.at[k], send_sem=q_send.at[k], recv_sem=q_recv.at[k],
            device_id={"lvl": lax.rem(place + k, peers)}, device_id_type=mesh_id,
        )

    def to_next():
        return pltpu.make_async_remote_copy(
            src_ref=frame.at[:, pl.ds(height, MARGIN)], dst_ref=frame.at[:, pl.ds(0, MARGIN)],
            send_sem=h_send.at[0], recv_sem=h_recv.at[0],
            device_id={"sp": lax.rem(spot + 1, spots)}, device_id_type=mesh_id,
        )

    def to_prev():
        return pltpu.make_async_remote_copy(
            src_ref=frame.at[:, pl.ds(MARGIN, MARGIN)],
            dst_ref=frame.at[:, pl.ds(MARGIN + height, MARGIN)],
            send_sem=h_send.at[1], recv_sem=h_recv.at[1],
            device_id={"sp": lax.rem(spot + spots - 1, spots)}, device_id_type=mesh_id,
        )

    def load_own():
        return pltpu.make_async_copy(share_hbm.at[quarter_rows(place), :], zown, f_sem.at[0])

    def load_part(k):
        return pltpu.make_async_copy(zrecv_hbm.at[k], zrecv.at[k], f_sem.at[k])

    def keep_own():
        return pltpu.make_async_copy(zlow, zfull.at[quarter_rows(place), :], f_sem.at[peers])

    load_own().start()
    pl.semaphore_wait(barrier, peers - 1 + spots - 1)
    for k in range(1, peers):
        z_copy(k).start()

    def slot_sum(ref, own):
        total = None
        for source in range(spots):
            k = lax.rem(spot - source + spots, spots)
            value = ref[k]
            total = value if total is None else total + value
        return total

    stat[...] = jnp.zeros_like(stat)
    kcols[...] = jnp.zeros_like(kcols)
    lane = lax.broadcasted_iota(jnp.int32, (channels, 128), 1)
    every_row = (channels, width)

    def column(ref, at):
        return jnp.broadcast_to(ref[:channels, at : at + 1], every_row)

    for m in range(batches):
        coef[m, 0] = column(par_ref, m)
    for m in range(batches):
        for load in loads[m]:
            load.wait()

        def sums(g, carry, m=m):
            now = pl.ds(pl.multiple_of(g * GROUP, GROUP), GROUP)
            mean = coef[m, 0, now, :]
            plain, cross = None, None
            for i in range(height):
                grad = dn[m, i, now, :].astype(f32)
                turn = grad * (conv[m, i, now, :] - mean)
                plain = grad if plain is None else plain + grad
                cross = turn if cross is None else cross + turn
            part[0, m, now, :] = plain
            part[1, m, now, :] = cross
            return carry

        lax.fori_loop(0, groups, sums, 0)
    tile = jnp.zeros((channels, 128), f32)
    for m in range(batches):
        plain = jnp.sum(part[0, m], axis=1, keepdims=True)
        cross = jnp.sum(part[1, m], axis=1, keepdims=True) * par_ref[:channels, 8 + m : 9 + m]
        tile = jnp.where(lane == m, plain, tile)
        tile = jnp.where(lane == batches + m, cross, tile)
    stat[:channels, :] = tile
    head = 8
    msg[:head, :] = stat[...].T[:head, :]
    msg[head:, :] = small_ref[...]
    srecv[0] = msg[...]
    for k in range(1, spots):
        spread_copy(msg, srecv, s_send, s_recv, k).start()

    masks = lane_tap_masks(width)
    fill_taps(k_ref, taps, masks, groups)
    for k in range(1, spots):
        spread_copy(msg, srecv, s_send, s_recv, k).wait()
    total = slot_sum(srecv, msg)
    tot_ref[...] = total[:head, :]
    zsmall[...] = total[head:, :]
    for k in range(1, peers):
        q_copy(k).start()
    padded = jnp.concatenate(
        [total[:head, :], jnp.zeros((128 - head, total.shape[1]), f32)], axis=0
    )
    stat_all[...] = padded.T

    gain = column(par_ref, 24)
    for m in range(batches):
        rho = column(par_ref, 8 + m)
        lead = rho * gain
        share = lead * column(par_ref, 16 + m)
        coef[m, 1] = lead
        coef[m, 2] = column(stat_all, m) * share
        coef[m, 3] = column(stat_all, batches + m) * rho * share

    def grad_rows(m, now, wanted):
        mean, lead = coef[m, 0, now, :], coef[m, 1, now, :]
        flat, tilt = coef[m, 2, now, :], coef[m, 3, now, :]
        for i in wanted:
            off = (conv[m, i, now, :] - mean) * tilt + flat
            frame[m, MARGIN + i, now, :] = (
                lead * dn[m, i, now, :].astype(f32) - mask_ref[m, i : i + 1, :] * off
            )

    edges = list(range(MARGIN)) + list(range(height - MARGIN, height))

    def rims(g, carry):
        now = pl.ds(pl.multiple_of(g * GROUP, GROUP), GROUP)
        for m in range(batches):
            grad_rows(m, now, edges)
        return carry

    lax.fori_loop(0, groups, rims, 0)

    @pl.when(spot < spots - 1)
    def _():
        to_next().start()

    @pl.when(spot > 0)
    def _():
        to_prev().start()

    load_x.wait()

    def weight_terms(g, carry):
        now = pl.ds(pl.multiple_of(g * GROUP, GROUP), GROUP)
        for t in range(KW * KW):
            acc49[t, now, :] = jnp.zeros((GROUP, width), f32)

        def one(m, inner):
            grad_rows(m, now, range(MARGIN, height - MARGIN))
            for base in range(0, height, ROWS):
                back = [frame[m, MARGIN + base + i, now, :] for i in range(ROWS)]
                for b in range(KW):
                    rolled = [
                        shifted(xt[m, base + r, now, :], b - MARGIN)
                        for r in range(ROWS + KW - 1)
                    ]
                    for a in range(KW):
                        total = None
                        for i in range(ROWS):
                            term = back[i] * rolled[i + a]
                            total = term if total is None else total + term
                        acc49[a * KW + b, now, :] += total
            return inner

        lax.fori_loop(0, batches, one, 0)
        return carry

    middle = groups
    lax.fori_loop(0, middle, weight_terms, 0)
    load_own().wait()
    for k in range(1, peers):
        z_copy(k).wait()
        load_part(k).start()
    for k in range(1, peers):
        load_part(k).wait()

    def fold(i, carry):
        at = pl.ds(pl.multiple_of(i * GROUP, 8), GROUP)
        total = zown[at, :]
        for k in range(1, peers):
            total = total + zrecv[k, at, :].astype(f32)
        zlow[at, :] = total.astype(bf)
        return carry

    lax.fori_loop(0, quarter // GROUP, fold, 0)
    for k in range(1, peers):
        g_copy(k).start()
    keep_own().start()
    lax.fori_loop(middle, groups, weight_terms, 0)
    wide_lane = lax.broadcasted_iota(jnp.int32, (channels, width), 1)

    def reduce_tap(t, carry):
        b = lax.rem(t, KW) - MARGIN
        kept = jnp.logical_and(wide_lane + b >= 0, wide_lane + b < width)
        summed = jnp.sum(jnp.where(kept, acc49[t], 0.0), axis=1, keepdims=True)
        kcols[:channels, :] = jnp.where(lane == t, summed, kcols[:channels, :])
        return carry

    lax.fori_loop(0, KW * KW, reduce_tap, 0)
    kmsg[...] = kcols[...].T[: kmsg.shape[0], :]
    krecv[0] = kmsg[...]
    for k in range(1, spots):
        spread_copy(kmsg, krecv, k_send, k_recv, k).start()


    @pl.when(spot < spots - 1)
    def _():
        to_next().wait_send()
        to_prev().wait_recv()

    @pl.when(spot > 0)
    def _():
        to_prev().wait_send()
        to_next().wait_recv()

    @pl.when(spot == 0)
    def _():
        frame[:, :MARGIN] = jnp.zeros((batches, MARGIN, channels, width), f32)

    @pl.when(spot == spots - 1)
    def _():
        frame[:, MARGIN + height :] = jnp.zeros((batches, MARGIN, channels, width), f32)

    def save(m):
        return pltpu.make_async_copy(obuf.at[m], igrad_hbm.at[m], out_sem.at[m])

    def inputs(m, carry):
        def one(g, inner):
            now = pl.ds(pl.multiple_of(g * GROUP, GROUP), GROUP)
            for base in range(0, height, ROWS):
                outs = depthwise_rows(
                    lambda r: frame[m, base + r, now, :], taps, now, ROWS, -1
                )
                for i in range(ROWS):
                    obuf[m, base + i, now, :] = outs[i].astype(bf)
            return inner

        lax.fori_loop(0, groups, one, 0)
        save(m).start()
        return carry

    lax.fori_loop(0, batches, inputs, 0)
    for k in range(1, spots):
        spread_copy(kmsg, krecv, k_send, k_recv, k).wait()
    kg_ref[...] = slot_sum(krecv, kmsg)
    for k in range(1, peers):
        q_copy(k).wait()
    zsrecv[0] = zsmall[...]
    total = None
    for source in range(peers):
        value = zsrecv[lax.rem(place - source + peers, peers)]
        total = value if total is None else total + value
    ztot[...] = total
    own_ref[...] = jnp.zeros_like(own_ref)
    piece = small_ref.shape[1]
    for n in range(small_ref.shape[0] // spots):
        own_ref[0:1, n * piece : (n + 1) * piece] = ztot[pl.ds(n * spots + spot, 1), :]
    keep_own().wait()
    for k in range(1, peers):
        g_wait(k)
    for m in range(batches):
        save(m).wait()


def finish(conv, xt, dn, share, low, small, params, mask_cells, kernel, ident):
    batches, height, channels, width = conv.shape
    bf, f32 = jnp.bfloat16, jnp.float32
    peers, spots = lax.axis_size("lvl"), lax.axis_size("sp")
    padded = -(-channels // 128) * 128
    taps = -(-(KW * KW) // 8) * 8
    head = 8
    lines = small.shape[0]
    every = share.shape[1]
    quarter = share.shape[0] // peers
    hbm = pl.BlockSpec(memory_space=pl.ANY)
    vmem = pl.BlockSpec(memory_space=pltpu.VMEM)
    dma = pltpu.SemaphoreType.DMA
    framed = (batches, height + 2 * MARGIN, channels, width)
    S = jax.ShapeDtypeStruct
    return pl.pallas_call(
        finish_body,
        in_specs=[hbm] * 5 + [vmem] * 4,
        out_specs=[hbm, hbm, hbm, vmem, vmem, vmem],
        out_shape=[
            S(conv.shape, bf),
            S(share.shape, bf), S((peers, quarter, every), bf),
            S((taps, padded), f32), S((head, padded), f32), S((8, lines // spots * padded), f32),
        ],
        scratch_shapes=[
            pltpu.VMEM(conv.shape, f32), pltpu.VMEM(framed, f32),
            pltpu.VMEM(conv.shape, bf), pltpu.VMEM(framed, f32), pltpu.VMEM(conv.shape, bf),
            pltpu.VMEM((KW * KW, channels, width), f32),
            pltpu.VMEM((KW * KW, channels, width), f32),
            pltpu.VMEM((2, batches, channels, width), f32),
            pltpu.VMEM((batches, 4, channels, width), f32),
            pltpu.VMEM((padded, 128), f32), pltpu.VMEM((padded, 128), f32),
            pltpu.VMEM((padded, 128), f32),
            pltpu.VMEM((head + lines, padded), f32),
            pltpu.VMEM((spots, head + lines, padded), f32),
            pltpu.VMEM((taps, padded), f32),
            pltpu.VMEM((spots, taps, padded), f32),
            pltpu.VMEM((quarter, every), f32), pltpu.VMEM((quarter, every), bf),
            pltpu.VMEM((peers, quarter, every), bf),
            pltpu.VMEM(small.shape, f32),
            pltpu.VMEM((peers,) + small.shape, f32), pltpu.VMEM(small.shape, f32),
            dma((3, batches)), dma((batches,)), dma((spots,)), dma((spots,)), dma((spots,)), dma((spots,)),
            dma((2,)), dma((2,)), dma((peers,)), dma((peers,)), dma((peers,)), dma((peers,)),
            dma((peers,)), dma((peers,)), dma((peers + 1,)),
        ],
        compiler_params=pltpu.CompilerParams(
            vmem_limit_bytes=60 * 1024 * 1024, collective_id=ident, has_side_effects=True
        ),
        cost_estimate=pl.CostEstimate(
            flops=4 * KW * KW * batches * channels * height * width,
            bytes_accessed=34 * batches * channels * height * width,
            transcendentals=0,
        ),
    )(conv, xt, dn, share, low, small, params, mask_cells, kernel)


RATES = {"kernel": 0.15, "scales": 0.2, "expand": 0.035, "uplift": 0.1, "shrink": 0.018, "offset": 0.1}


def close_body(
    crop, step, x_ref, cot_ref, res_ref, dx_ref, mask_ref, ge_ref, gs_ref,
    e_ref, e1_ref, e2_ref, s_ref, s1_ref, s2_ref,
    kg_ref, tot_ref, own_ref,
    k_ref, k1_ref, k2_ref, c_ref, c1_ref, c2_ref, u_ref, u1_ref, u2_ref, o_ref, o1_ref, o2_ref,
    out_ref, igrad_ref, eg_out, em_out, en_out, sg_out, sm_out, sn_out,
    kg_out, km_out, kn_out, cg_out, cm_out, cn_out, ug_out, um_out, un_out, og_out, om_out, on_out,
    scr, scx,
):
    f32 = jnp.float32
    batches, block, height, width = x_ref.shape
    time = jnp.full((8, 128), step[0] + 1, jnp.int32).astype(f32)
    one = 1.0 / (1.0 - jnp.exp(time * math.log(beta_one)))[0:1, 0:1]
    two = 1.0 / (1.0 - jnp.exp(time * math.log(beta_two)))[0:1, 0:1]

    def step_of(weight, first, second, grad, rate):
        first_new = beta_one * first + (1.0 - beta_one) * grad
        second_new = beta_two * second + (1.0 - beta_two) * grad * grad
        update = first_new * one / (jnp.sqrt(second_new * two) + epsilon) + weight_decay * weight
        return second_new, weight - rate * update

    @pl.when(pl.program_id(0) == 0)
    def _():
        taps, channels = k_ref.shape
        kg = kg_ref[:taps, :channels]
        kg_out[...] = kg
        km_out[...], kn_out[...] = step_of(
            k_ref[...], k1_ref[...], k2_ref[...], kg, RATES["kernel"]
        )
        tot = tot_ref[...]
        plain = jnp.sum(tot[:batches], axis=0, keepdims=True)[:, :channels]
        cross = jnp.sum(tot[batches : 2 * batches], axis=0, keepdims=True)[:, :channels]
        for row, grad in ((0, cross), (1, plain)):
            at = slice(row, row + 1)
            cg_out[at, :] = grad
            cm_out[at, :], cn_out[at, :] = step_of(
                c_ref[at, :], c1_ref[at, :], c2_ref[at, :], grad, RATES["scales"]
            )
        owned, each = u_ref.shape[1], o_ref.shape[1]
        ug = own_ref[0:1, :owned]
        ug_out[...] = ug
        um_out[...], un_out[...] = step_of(
            u_ref[...], u1_ref[...], u2_ref[...], ug, RATES["uplift"]
        )
        og = own_ref[0:1, owned : owned + each]
        og_out[...] = og
        om_out[...], on_out[...] = step_of(
            o_ref[...], o1_ref[...], o2_ref[...], og, RATES["offset"]
        )

    strip = ge_ref.shape[0]

    def rows(i, carry):
        at = pl.ds(pl.multiple_of(i * strip, strip), strip)
        for g_ref, w, w1, w2, g_out, m_out, n_out, rate in (
            (ge_ref, e_ref, e1_ref, e2_ref, eg_out, em_out, en_out, RATES["expand"]),
            (gs_ref, s_ref, s1_ref, s2_ref, sg_out, sm_out, sn_out, RATES["shrink"]),
        ):
            grad = g_ref[at, :].astype(f32)
            g_out[at, :] = grad
            m_out[at, :], n_out[at, :] = step_of(w[at, :], w1[at, :], w2[at, :], grad, rate)
        return carry

    lax.fori_loop(0, ge_ref.shape[0] // strip, rows, 0)
    row = lax.broadcasted_iota(jnp.int32, (height, width), 0)

    def cells(g, carry):
        c0 = pl.multiple_of(g * GROUP, GROUP)
        now = pl.ds(c0, GROUP)
        for m in range(batches):
            keep = (row < crop[m]).astype(f32)
            mask = mask_ref[m]
            for i in range(height):
                at = slice(i * GROUP, (i + 1) * GROUP)
                scr[m, at, :] = res_ref[m, i, now, :].astype(f32)
                scx[m, at, :] = dx_ref[m, i, now, :].astype(f32)
            for c in range(GROUP):
                part = pl.ds(c, height, stride=GROUP)
                out_ref[m, c0 + c] = mask * (x_ref[m, c0 + c].astype(f32) + scr[m, part, :])
                dres = cot_ref[m, c0 + c].astype(f32) * mask
                igrad_ref[m, c0 + c] = keep * (dres + scx[m, part, :])
        return carry

    lax.fori_loop(0, block // GROUP, cells, 0)


def close(crop, step, x, cot, res, dx, mask_cells, shares, expand, shrink, kg, tot, own, kernel, scales, uplift, offset):
    batches, channels, height, width = x.shape
    f32 = jnp.float32
    owned, every = expand[0].shape
    block = CLOSE_BLOCK
    steps = channels // block
    part = owned // steps
    natural = pl.BlockSpec((batches, block, height, width), lambda i: (0, i, 0, 0))
    turned = pl.BlockSpec((batches, height, block, width), lambda i: (0, 0, i, 0))
    smem = pl.BlockSpec(memory_space=pltpu.SMEM)
    lines = pl.BlockSpec((part, every), lambda i: (i, 0))
    later = pl.BlockSpec((part, every), lambda i: (i + steps, 0))

    def whole(v):
        zeros = (0,) * v.ndim
        return pl.BlockSpec(v.shape, lambda i: zeros)

    S = jax.ShapeDtypeStruct
    small = list(kernel) + list(scales) + list(uplift) + list(offset)
    return pl.pallas_call(
        close_body,
        grid=(steps,),
        in_specs=[smem, smem, natural, natural, turned, turned, whole(mask_cells), lines, later]
        + [lines] * 6 + [whole(v) for v in (kg, tot, own)] + [whole(v) for v in small],
        out_specs=[natural, natural] + [lines] * 6 + [whole(v) for v in small],
        out_shape=[S(x.shape, f32)] * 2 + [S((owned, every), f32)] * 6
        + [S(v.shape, f32) for v in small],
        scratch_shapes=[
            pltpu.VMEM((batches, GROUP * height, width), f32),
            pltpu.VMEM((batches, GROUP * height, width), f32),
        ],
        compiler_params=pltpu.CompilerParams(vmem_limit_bytes=63 * 1024 * 1024),
    )(
        crop, step, x, cot, res, dx, mask_cells, shares, shares,
        *expand, *shrink, kg, tot, own, *small,
    )


def sums_body(xt_ref, res_ref, dn_ref, conv_ref, mask_ref, par_ref, out_ref, stat_ref, scr):
    batches, height = res_ref.shape[:2]
    width = res_ref.shape[3]

    def one(m, stats):
        lane = lax.broadcasted_iota(jnp.int32, (GROUP, 128), 1)
        mean = jnp.sum(jnp.where(lane == m, par_ref[...], 0.0), axis=1, keepdims=True)
        rho = jnp.sum(jnp.where(lane == batches + m, par_ref[...], 0.0), axis=1, keepdims=True)
        mean = jnp.broadcast_to(mean, (GROUP, width))
        rho = jnp.broadcast_to(rho, (GROUP, width))
        plain = jnp.zeros((GROUP, width), jnp.float32)
        cross = jnp.zeros((GROUP, width), jnp.float32)
        for i in range(height):
            grad = dn_ref[m, i].astype(jnp.float32)
            plain = plain + grad
            cross = cross + grad * ((conv_ref[m, i] - mean) * rho)
            value = xt_ref[m, MARGIN + i] + res_ref[m, i].astype(jnp.float32)
            scr[pl.ds(i, GROUP, stride=height), :] = value * mask_ref[m, i : i + 1, :]
        for c in range(GROUP):
            out_ref[m, c] = scr[c * height : (c + 1) * height, :]
        stats = jnp.where(lane == m, jnp.sum(plain, axis=1, keepdims=True), stats)
        return jnp.where(lane == batches + m, jnp.sum(cross, axis=1, keepdims=True), stats)

    stat_ref[...] = lax.fori_loop(0, batches, one, jnp.zeros((GROUP, 128), jnp.float32))


def output_and_sums(xt, res, dn, conv, mask_cells, params):
    batches, height, channels, width = res.shape
    turned = lambda rows: pl.BlockSpec((batches, rows, GROUP, width), lambda g: (0, 0, g, 0))
    return pl.pallas_call(
        sums_body,
        grid=(pl.cdiv(channels, GROUP),),
        in_specs=[
            turned(height + 2 * MARGIN),
            turned(height), turned(height), turned(height),
            pl.BlockSpec((batches, height, width), lambda g: (0, 0, 0)),
            pl.BlockSpec((GROUP, 128), lambda g: (g, 0)),
        ],
        out_specs=[
            pl.BlockSpec((batches, GROUP, height, width), lambda g: (0, g, 0, 0)),
            pl.BlockSpec((GROUP, 128), lambda g: (g, 0)),
        ],
        out_shape=[
            jax.ShapeDtypeStruct((batches, channels, height, width), jnp.float32),
            jax.ShapeDtypeStruct((channels, 128), jnp.float32),
        ],
        scratch_shapes=[pltpu.VMEM((GROUP * height, width), jnp.float32)],
        cost_estimate=pl.CostEstimate(
            flops=10 * batches * channels * height * width,
            bytes_accessed=20 * batches * channels * height * width,
            transcendentals=0,
        ),
    )(xt, res, dn, conv, mask_cells, params)


def conv_back_body(
    crop, xt_ref, grad_ref, up_ref, dn_ref, cot_ref, k_ref, mask_ref,
    out_ref, kg_ref, scr, wscr, frame, sums,
):
    batches, height = grad_ref.shape[:2]
    width = grad_ref.shape[3]
    masks = lane_tap_masks(width)
    for a in range(KW):
        for b in range(KW):
            t = a * KW + b
            spread = jnp.broadcast_to(k_ref[:, t : t + 1], (GROUP, width))
            wscr[t] = jnp.where(masks[KW - 1 - b], spread, 0.0)
            sums[t] = jnp.zeros((GROUP, width), jnp.float32)

    def one(m, carry):
        for r in range(MARGIN):
            frame[r] = up_ref[m, r]
            frame[MARGIN + height + r] = dn_ref[m, r]
        for i in range(height):
            frame[MARGIN + i] = grad_ref[m, i]
        for base in range(0, height, ROWS):
            for b in range(KW):
                rolled = [
                    shifted(xt_ref[m, base + r], b - MARGIN) for r in range(ROWS + KW - 1)
                ]
                for a in range(KW):
                    part = None
                    for i in range(ROWS):
                        term = frame[MARGIN + base + i] * rolled[i + a]
                        part = term if part is None else part + term
                    sums[a * KW + b] += part
            acc = [None] * ROWS
            for b in range(KW):
                rolled = [
                    shifted(frame[base + r], MARGIN - b) for r in range(ROWS + KW - 1)
                ]
                for a in range(KW):
                    tap = wscr[a * KW + b]
                    for i in range(ROWS):
                        term = tap * rolled[i + KW - 1 - a]
                        acc[i] = term if acc[i] is None else acc[i] + term
            for i in range(ROWS):
                scr[pl.ds(base + i, GROUP, stride=height), :] = acc[i]
        row = lax.broadcasted_iota(jnp.int32, (height, width), 0)
        for c in range(GROUP):
            dres = cot_ref[m, c].astype(jnp.float32) * mask_ref[m]
            total = dres + scr[c * height : (c + 1) * height, :]
            out_ref[m, c] = jnp.where(row < crop[m, 0], total, 0.0)
        return carry

    lax.fori_loop(0, batches, one, 0)
    columns = []
    for t in range(KW * KW):
        kept = jnp.where(masks[t % KW], sums[t], 0.0)
        columns.append((t, jnp.sum(kept, axis=1, keepdims=True)))
    kg_ref[...] = put_columns(columns)


def conv_backward(crop, xt, grad_conv, up, down, cot, kernel, mask_cells):
    batches, height, channels, width = grad_conv.shape
    natural = pl.BlockSpec((batches, GROUP, height, width), lambda g, c: (0, g, 0, 0))
    turned = lambda rows: pl.BlockSpec((batches, rows, GROUP, width), lambda g, c: (0, 0, g, 0))
    return pl.pallas_call(
        conv_back_body,
        grid_spec=pltpu.PrefetchScalarGridSpec(
            num_scalar_prefetch=1,
            grid=(pl.cdiv(channels, GROUP),),
            in_specs=[
                turned(height + 2 * MARGIN),
                turned(height),
                turned(MARGIN), turned(MARGIN),
                natural,
                pl.BlockSpec((GROUP, KW * KW), lambda g, c: (g, 0)),
                pl.BlockSpec((batches, height, width), lambda g, c: (0, 0, 0)),
            ],
            out_specs=[natural, pl.BlockSpec((GROUP, 128), lambda g, c: (g, 0))],
            scratch_shapes=[
                pltpu.VMEM((GROUP * height, width), jnp.float32),
                pltpu.VMEM((KW * KW, GROUP, width), jnp.float32),
                pltpu.VMEM((height + 2 * MARGIN, GROUP, width), jnp.float32),
                pltpu.VMEM((KW * KW, GROUP, width), jnp.float32),
            ],
        ),
        out_shape=[
            jax.ShapeDtypeStruct((batches, channels, height, width), jnp.float32),
            jax.ShapeDtypeStruct((channels, 128), jnp.float32),
        ],
        cost_estimate=pl.CostEstimate(
            flops=4 * KW * KW * batches * channels * height * width,
            bytes_accessed=14 * batches * channels * height * width,
            transcendentals=0,
        ),
    )(crop, xt, grad_conv, up, down, cot, kernel, mask_cells)


def neighbours(head, tail, axis):
    count = lax.axis_size(axis)
    up = lax.ppermute(tail, axis, [(i, i + 1) for i in range(count - 1)])
    down = lax.ppermute(head, axis, [(i + 1, i) for i in range(count - 1)])
    return up, down


def aligned(channels, height, owned, levels):
    return (
        channels % 8 == 0 and height % levels == 0 and height == ROWS
        and owned % 16 == 0 and (2 * owned) % (8 * levels) == 0
        and channels % CLOSE_BLOCK == 0 and owned % (16 * (channels // CLOSE_BLOCK)) == 0
    )


def on_device(
    input_field, cotangent, ocean_mask, crop_rows, step_count,
    kernel, kernel_first, kernel_second,
    scales, scales_first, scales_second,
    expand, expand_first, expand_second,
    uplift, uplift_first, uplift_second,
    shrink, shrink_first, shrink_second,
    offset, offset_first, offset_second,
):
    f32, bf = jnp.float32, jnp.bfloat16
    batches, channels, height, width = input_field.shape
    sp = lax.axis_size("sp")
    lvl = lax.axis_size("lvl")
    place = lax.axis_index("sp")
    owned = uplift.shape[0]
    hidden, every = sp * owned, sp * offset.shape[0]
    if aligned(channels, height, owned, lvl) and sp == 8:
        crop = crop_rows.reshape(batches)
        (
            conv, xt, normed, pixel_back, expand_all, shrink_all, params, mask_cells, bias, turned_k,
        ) = forward(
            crop, input_field, cotangent, ocean_mask, kernel.T, scales,
            expand.T, shrink, uplift[None], offset[None], 0,
        )
        padded = params.shape[0]
        lines = -(-(owned + offset.shape[0]) // padded) * sp
        result, grad_normed, share, low, small = mlp_fused(
            normed, pixel_back, expand_all, shrink_all, bias, lines, padded, 1
        )
        field_grad, shares, _, kernel_rows, both, own = finish(
            conv, xt, grad_normed, share, low, small, params, mask_cells, turned_k, 2
        )
        (
            block_output, input_grad, eg, em, en, sg, sm, sn,
            kg, km, kn, cg, cm, cn, ug, um, un, og, om, on,
        ) = close(
            crop, step_count.reshape(1), input_field, cotangent, result, field_grad, mask_cells,
            shares, (expand.T, expand_first.T, expand_second.T),
            (shrink, shrink_first, shrink_second), kernel_rows, both, own,
            (kernel.T, kernel_first.T, kernel_second.T), (scales, scales_first, scales_second),
            (uplift[None], uplift_first[None], uplift_second[None]),
            (offset[None], offset_first[None], offset_second[None]),
        )
        return (
            block_output, input_grad, kg.T, km.T, kn.T, cg, cm, cn, eg.T, em.T, en.T,
            ug[0], um[0], un[0], sg, sm, sn, og[0], om[0], on[0], step_count + 1,
        )
    else:
        expand_all = lax.all_gather(expand.T.astype(bf), "sp", axis=0, tiled=True)
        shrink_all = lax.all_gather(shrink.astype(bf), "sp", axis=0, tiled=True)
        uplift_all = lax.all_gather(uplift.astype(bf), "sp", axis=0, tiled=True)
        offset_all = lax.all_gather(offset.astype(bf), "sp", axis=0, tiled=True)

        valid = (jnp.arange(height, dtype=jnp.int32)[None, :] < crop_rows).astype(f32)
        mask_cells = ocean_mask.astype(f32) * valid[:, :, None]
        valid_low = valid.astype(bf)[:, None, :, None]
        head = input_field[:, :, :MARGIN] * valid_low[:, :, :MARGIN]
        tail = input_field[:, :, height - MARGIN :] * valid_low[:, :, height - MARGIN :]
        up, down = neighbours(head.transpose(0, 2, 1, 3), tail.transpose(0, 2, 1, 3), "sp")
        conv, xt, dres, stats = conv_forward(
            crop_rows, input_field, cotangent, up, down, kernel, mask_cells
        )
        every = lax.all_gather(stats[:, : 4 * batches], "sp", axis=0)
        sums = every[:, :, :batches]
        squares = every[:, :, batches : 2 * batches]
        cells = every[:, :, 2 * batches : 3 * batches]
        count = jnp.maximum(jnp.sum(cells, axis=0), 1.0)
        mean = jnp.sum(sums, axis=0) / count
        gap = sums / jnp.maximum(cells, 1.0) - mean[None]
        variance = jnp.sum(squares + cells * gap * gap, axis=0) / count
        rho = lax.rsqrt(variance + 1e-05)

        def spread(stat):
            return stat.T[:, None, :, None]

        gain = scales[0][None, None, :, None]
        shift = scales[1][None, None, :, None]
        normed = ((conv - spread(mean)) * spread(rho) * gain + shift).astype(bf)

        def to_pixels(v):
            return lax.all_to_all(v, "lvl", split_axis=1, concat_axis=2, tiled=True)

        def to_channels(v):
            return lax.all_to_all(v, "lvl", split_axis=2, concat_axis=1, tiled=True)

        pixel_back = to_pixels(dres)
        biases = (uplift_all.astype(f32)[None], offset_all.astype(f32)[None])
        result, grad_normed, grad_expand, grad_shrink, grad_uplift, grad_offset = mlp(
            to_pixels(normed), pixel_back, expand_all, shrink_all, *biases
        )
        result = to_channels(result)
        grad_normed = to_channels(grad_normed)
        params = jnp.concatenate([mean, rho], axis=1)
        params = jnp.pad(params, ((0, 0), (0, 128 - params.shape[1])))
        block_output, local = output_and_sums(xt, result, grad_normed, conv, mask_cells, params)
        both = lax.psum(local[:, : 2 * batches], "sp")
        plain, cross = both[:, :batches], both[:, batches:]
        scales_grad = jnp.stack([jnp.sum(cross, axis=1), jnp.sum(plain, axis=1)], axis=0)
        whitened = (conv - spread(mean)) * spread(rho)
        grad_conv = spread(rho) * (
            gain * grad_normed.astype(f32)
            - mask_cells[:, :, None, :] * gain * (spread(plain) + whitened * spread(cross)) / spread(count)
        )
        back_up, back_down = neighbours(
            grad_conv[:, :MARGIN], grad_conv[:, height - MARGIN :], "sp"
        )
        input_grad, kernel_cols = conv_backward(
            crop_rows, xt, grad_conv, back_up, back_down, cotangent, kernel, mask_cells
        )
        kernel_grad = lax.psum(kernel_cols[:, : KW * KW], "sp")

        def own_share(partial):
            rows = partial.shape[0] // sp
            parts = lax.all_to_all(
                partial.reshape(sp, rows, partial.shape[1]), "sp", split_axis=0, concat_axis=0
            )
            share = jnp.sum(parts.astype(f32), axis=0).astype(bf)
            return jnp.sum(lax.all_gather(share, "lvl", axis=0).astype(f32), axis=0)

        share_expand = own_share(grad_expand)
        share_shrink = own_share(grad_shrink)
        small = lax.psum(
            jnp.concatenate([grad_uplift[0], grad_offset[0]]), ("sp", "lvl")
        )
    share_uplift = lax.dynamic_slice_in_dim(small, place * owned, owned)
    share_offset = lax.dynamic_slice_in_dim(
        small, hidden + place * offset.shape[0], offset.shape[0]
    )
    step_float = (step_count + 1).astype(f32)
    kernel_moment, kernel_next = adamw(
        kernel, kernel_first, kernel_second, kernel_grad, 0.15, step_float
    )
    scales_moment, scales_next = adamw(
        scales, scales_first, scales_second, scales_grad, 0.2, step_float
    )
    expand_grad = share_expand.T
    expand_moment, expand_next = adamw(
        expand, expand_first, expand_second, expand_grad, 0.035, step_float
    )
    uplift_moment, uplift_next = adamw(
        uplift, uplift_first, uplift_second, share_uplift, 0.1, step_float
    )
    shrink_moment, shrink_next = adamw(
        shrink, shrink_first, shrink_second, share_shrink, 0.018, step_float
    )
    offset_moment, offset_next = adamw(
        offset, offset_first, offset_second, share_offset, 0.1, step_float
    )
    return (
        block_output, input_grad,
        kernel_grad, kernel_moment, kernel_next,
        scales_grad, scales_moment, scales_next,
        expand_grad, expand_moment, expand_next,
        share_uplift, uplift_moment, uplift_next,
        share_shrink, shrink_moment, shrink_next,
        share_offset, offset_moment, offset_next,
        step_count + 1,
    )


def solution(mesh):
    tile = P(None, "lvl", "sp", None)
    by_channel = P("lvl", None)
    by_scale = P(None, "lvl")
    by_hidden = P(None, "sp")
    by_row = P("sp", None)
    line = P("sp")
    in_specs = (
        tile, tile, P(None, "sp", None), P(None, "sp"), P(),
        by_channel, by_channel, by_channel,
        by_scale, by_scale, by_scale,
        by_hidden, by_hidden, by_hidden,
        line, line, line,
        by_row, by_row, by_row,
        line, line, line,
    )
    out_specs = (
        tile, tile,
        by_channel, by_channel, by_channel,
        by_scale, by_scale, by_scale,
        by_hidden, by_hidden, by_hidden,
        line, line, line,
        by_row, by_row, by_row,
        line, line, line,
        P(),
    )
    return jax.shard_map(
        on_device, mesh=mesh, in_specs=in_specs, out_specs=out_specs, check_vma=False
    )
```
